512 devices in a mesh: bulk: 64 (over x, z, core), span: 8 (over y).
Axes of the slice: x: 4, y: 8, z: 8, core: 2. Of those that a mesh axis runs over, the one named last changes fastest.
Arguments:
- snapshots: float32 [1048576, 128], P(('span', 'bulk'))
- jac_blocks: bfloat16 [8192, 4, 128, 128], P(('span', 'bulk'))
- jac_cols: int32 [8192, 4], P(('span', 'bulk')), may hold values from 0 to 8191, as said below
Outputs:
- modes: float32 [1048576, 128], P(('span', 'bulk'))
- factor: float32 [128, 128], replicated
- jac_modes: bfloat16 [1048576, 128], P(('span', 'bulk'))
- reduced: float32 [128, 128], replicated
The draws below stay inside these ranges and needn't reach their ends.
Inputs may be any that keep to these rules, and one draw needn't show every extreme that they name: jac_cols[r, 0] = r. Every column block lies in the die region of r (aligned runs of 1024 block rows) and within 16 block rows of the shard of 16 block rows that holds r.
All inputs are finite; a program needn't handle non-finite values.
Results may differ from the reference program's by a relative error of at most 0.0029.
The reference program's roundings to bfloat16 on the way (of `modes_b`) count: a program that leaves them out, or rounds other values in their place, can miss the bound.
Values may be sent and summed in bfloat16 or wider, within the bound.
A program may use at most 64 MiB of HBM per device.

```python
import math
import jax
import jax.numpy as jnp
from jax import lax

K = 128
BLOCK = 128
NB = 4
RB_DEV = 16
REGION = 1024
ROWBLOCKS = 8192
ROWS = 1048576


def draw_snapshots(key, part):
    key_base = jax.random.fold_in(key, 0)
    key_order = jax.random.fold_in(key, 3)
    key_cols = jax.random.fold_in(key, 4)
    key_sign = jax.random.fold_in(key, 5)
    index = jnp.arange(K, dtype=jnp.float32)
    singular = 3.0 * jnp.exp(-math.log(2500.0) * index / (K - 1))
    order = jax.random.permutation(key_order, K)
    singular = jnp.take(singular, order)
    table = jnp.cos(math.pi * (index[:, None] + 0.5) * index[None, :] / K) * math.sqrt(2.0 / K)
    table = table * jnp.where(index == 0.0, math.sqrt(0.5), 1.0)[None, :]
    mixing = singular[:, None] * table.T
    columns = jax.random.permutation(key_cols, K)
    signs = (2 * jax.random.randint(key_sign, (K,), 0, 2, dtype=jnp.int32) - 1).astype(jnp.float32)
    mixing = jnp.take(mixing, columns, axis=1) * signs[None, :]
    base = jax.random.normal(key_base, (ROWS, K), jnp.float32)
    return jnp.dot(base, mixing, precision=lax.Precision.HIGHEST, preferred_element_type=jnp.float32)


def draw_jac_cols(key, part):
    block_ids = jnp.arange(ROWBLOCKS, dtype=jnp.int32)
    region_low = block_ids // REGION * REGION
    region_high = region_low + REGION - 1
    shard_start = block_ids // RB_DEV * RB_DEV
    offsets = jax.random.randint(key, (ROWBLOCKS, NB - 1), -RB_DEV, 2 * RB_DEV, dtype=jnp.int32)
    others = jnp.clip(shard_start[:, None] + offsets, region_low[:, None], region_high[:, None])
    return jnp.concatenate([block_ids[:, None], others], axis=1).astype(jnp.int32)


def draw_jac_blocks(key, part):
    key_val, key_diag = jax.random.split(key, 2)
    shape = (ROWBLOCKS, NB, BLOCK, BLOCK)
    values = jax.random.normal(key_val, shape, jnp.float32)
    values = values * (1.5 / math.sqrt(BLOCK * NB))
    rising = 1.0 + 2.0 * jnp.arange(ROWBLOCKS, dtype=jnp.float32) / ROWBLOCKS
    spread = jnp.exp(jax.random.uniform(key_diag, (ROWBLOCKS, BLOCK), jnp.float32, 0.0, math.log(3.0)))
    diag_vals = rising[:, None] * spread
    identity = jnp.eye(BLOCK, dtype=jnp.float32)
    first_slot = (jnp.arange(NB) == 0).astype(jnp.float32)
    extra = diag_vals[:, None, :, None] * identity[None, None, :, :] * first_slot[None, :, None, None]
    return (values + extra).astype(jnp.bfloat16)


def setup_inputs(seed: int = 0) -> dict:
    arg_keys = jax.random.split(jax.random.key(seed), 4)
    return {
        "snapshots": draw_snapshots(jax.random.fold_in(arg_keys[3], 71), 0),
        "jac_blocks": draw_jac_blocks(jax.random.fold_in(arg_keys[3], 71), 0),
        "jac_cols": draw_jac_cols(jax.random.fold_in(arg_keys[3], 71), 0),
    }


def cholesky_step(data):
    high = lax.Precision.HIGHEST
    gram = lax.dot_general(data.astype(jnp.float32), data.astype(jnp.float32), (((0,), (0,)), ((), ())), precision=high, preferred_element_type=jnp.float32) / ROWS
    lower = jnp.linalg.cholesky(gram)
    inverse = lax.linalg.triangular_solve(lower, jnp.eye(K, dtype=jnp.float32), left_side=True, lower=True)
    result = jnp.dot(data.astype(jnp.float32), inverse.T.astype(jnp.float32), precision=high, preferred_element_type=jnp.float32)
    return (result, lower)

def reference(snapshots, jac_blocks, jac_cols):
    high = lax.Precision.HIGHEST
    first, lower1 = cholesky_step(snapshots)
    modes, lower2 = cholesky_step(first)
    factor = jnp.dot(lower2.T.astype(jnp.float32), lower1.T.astype(jnp.float32), precision=high, preferred_element_type=jnp.float32)
    modes_b = modes.astype(jnp.bfloat16)
    mode_blocks = modes_b.reshape(ROWBLOCKS, BLOCK, K)
    groups = ROWBLOCKS // RB_DEV
    blocks_grouped = jac_blocks.reshape(groups, RB_DEV, NB, BLOCK, BLOCK)
    cols_grouped = jac_cols.reshape(groups, RB_DEV, NB)

    def one_group(pair):
        blocks, cols = pair
        picked = jnp.take(mode_blocks, cols.astype(jnp.int32), axis=0)
        product = jnp.einsum('rnij,rnjk->rik', blocks.astype(jnp.float32), picked.astype(jnp.float32), precision=high)
        return product.astype(jnp.bfloat16).reshape(RB_DEV * BLOCK, K)
    jac_modes = lax.map(one_group, (blocks_grouped, cols_grouped)).reshape(ROWS, K)
    reduced = lax.dot_general(modes.astype(jnp.float32), jac_modes.astype(jnp.float32), (((0,), (0,)), ((), ())), precision=high, preferred_element_type=jnp.float32) / ROWS
    return (modes, factor, jac_modes, reduced)
```

```python
import functools

import jax
import jax.numpy as jnp
from jax import lax
from jax.experimental import pallas as pl
from jax.experimental.pallas import tpu as pltpu
from jax.sharding import PartitionSpec as P

MESH = pl.DeviceIdType.MESH


def with_halo(array, sides, width):
    for axis, dim in sides:
        size, length = (lax.axis_size(axis), array.shape[dim])
        up = [(i, (i + 1) % size) for i in range(size - 1)]
        down = [(j, i) for i, j in up]
        last = lax.slice_in_dim(array, length - width, length, axis=dim)
        initial = lax.slice_in_dim(array, 0, width, axis=dim)
        before = lax.ppermute(last, axis, up)
        after = lax.ppermute(initial, axis, down)
        array = jnp.concatenate([before, array, after], axis=dim)
    return array


def _groups(nx, nz, ny):
    b = lax.axis_index("bulk")
    s = lax.axis_index("span")
    core = b % 2
    z = (b // 2) % nz
    x = b // (2 * nz)
    return [
        (2, core, lambda p: (b - core + p, s)),
        (nx, x, lambda p: ((p * nz + z) * 2 + core, s)),
        (nz, z, lambda p: ((x * nz + p) * 2 + core, s)),
        (ny, s, lambda p: (b, p)),
    ]


def _allreduce_kernel(dims, x_ref, o_ref, slots, send_sem, recv_sem):
    groups = _groups(*dims)
    barrier = pltpu.get_barrier_semaphore()
    peers = 0
    for n, pos, dev in groups:
        for d in range(1, n):
            pl.semaphore_signal(barrier, inc=1, device_id=dev((pos + d) % n), device_id_type=MESH)
            peers += 1
    pl.semaphore_wait(barrier, peers)

    offset = 0
    src = x_ref
    for n, pos, dev in groups:
        own = offset + pos
        if src is not x_ref:
            slots[own] = src
        else:
            slots[own] = x_ref[...]
        send_from = x_ref if src is x_ref else slots.at[own]
        copies = []
        for d in range(1, n):
            peer = (pos + d) % n
            copy = pltpu.make_async_remote_copy(
                src_ref=send_from,
                dst_ref=slots.at[own],
                send_sem=send_sem.at[offset + peer],
                recv_sem=recv_sem.at[own],
                device_id=dev(peer),
                device_id_type=MESH,
            )
            copy.start()
            copies.append(copy)
        for d in range(1, n):
            j = offset + (pos + d) % n
            pltpu.make_async_remote_copy(
                src_ref=slots.at[j],
                dst_ref=slots.at[j],
                send_sem=send_sem.at[j],
                recv_sem=recv_sem.at[j],
                device_id=dev(0),
                device_id_type=MESH,
            ).wait_recv()
        for copy in copies:
            copy.wait_send()
        acc = slots[offset]
        for k in range(1, n):
            acc = acc + slots[offset + k]
        src = acc
        offset += n
    o_ref[...] = src


def make_allreduce(dims, cid):
    total = sum((2,) + tuple(dims))

    def allreduce(partial_value):
        return pl.pallas_call(
            functools.partial(_allreduce_kernel, dims),
            out_shape=jax.ShapeDtypeStruct(partial_value.shape, jnp.float32),
            in_specs=[pl.BlockSpec(memory_space=pltpu.VMEM)],
            out_specs=pl.BlockSpec(memory_space=pltpu.VMEM),
            scratch_shapes=[
                pltpu.VMEM((total,) + partial_value.shape, jnp.float32),
                pltpu.SemaphoreType.DMA((total,)),
                pltpu.SemaphoreType.DMA((total,)),
            ],
            compiler_params=pltpu.CompilerParams(collective_id=cid, has_side_effects=True),
        )(partial_value)

    return allreduce


def cholesky_step(data, row_count, allreduce):
    high = lax.Precision.HIGHEST
    width = data.shape[1]
    partial_value = lax.dot_general(
        data, data, (((0,), (0,)), ((), ())), precision=high, preferred_element_type=jnp.float32
    )
    gram = allreduce(partial_value) / row_count
    lower = jnp.linalg.cholesky(gram)
    inverse = lax.linalg.triangular_solve(
        lower, jnp.eye(width, dtype=jnp.float32), left_side=True, lower=True
    )
    result = jnp.dot(data, inverse.T, precision=high, preferred_element_type=jnp.float32)
    return (result, lower)


def shards(dims, snapshots, jac_blocks, jac_cols):
    high = lax.Precision.HIGHEST
    local_rows, width = snapshots.shape
    block_rows = jac_cols.shape[0]
    blk = jac_blocks.shape[2]
    row_count = local_rows * lax.axis_size(("bulk", "span"))
    first, lower1 = cholesky_step(snapshots, row_count, make_allreduce(dims, 0))
    modes, lower2 = cholesky_step(first, row_count, make_allreduce(dims, 1))
    factor = jnp.dot(lower2.T, lower1.T, precision=high, preferred_element_type=jnp.float32)
    modes_b = modes.astype(jnp.bfloat16)
    shard_start = (
        lax.axis_index("span") * lax.axis_size("bulk") + lax.axis_index("bulk")
    ) * block_rows
    relative = jac_cols - shard_start
    extended = with_halo(modes_b, (("bulk", 0),), local_rows)
    ext_blocks = extended.reshape(3 * block_rows, blk, width)
    picked = jnp.take(ext_blocks, relative + block_rows, axis=0)
    product = jnp.einsum("rnij,rnjk->rik", jac_blocks, picked, preferred_element_type=jnp.float32)
    jac_modes = product.astype(jnp.bfloat16).reshape(local_rows, width)
    partial_value = lax.dot_general(
        modes,
        jac_modes.astype(jnp.float32),
        (((0,), (0,)), ((), ())),
        precision=high,
        preferred_element_type=jnp.float32,
    )
    reduced = make_allreduce(dims, 2)(partial_value) / row_count
    return (modes, factor, jac_modes, reduced)


def _torus_dims(mesh):
    coords = [d.coords for d in mesh.devices.flat]
    return tuple(len({c[i] for c in coords}) for i in (0, 2, 1))


def solution(mesh):
    nx, nz, ny = _torus_dims(mesh)
    assert mesh.shape["bulk"] == 2 * nx * nz and mesh.shape["span"] == ny
    return jax.shard_map(
        functools.partial(shards, (nx, nz, ny)),
        mesh=mesh,
        in_specs=(
            P(("span", "bulk"), None),
            P(("span", "bulk"), None, None, None),
            P(("span", "bulk"), None),
        ),
        out_specs=(P(("span", "bulk"), None), P(), P(("span", "bulk"), None), P()),
        check_vma=False,
    )
```

```python
import functools

import jax
import jax.numpy as jnp
from jax import lax
from jax.experimental import pallas as pl
from jax.experimental.pallas import tpu as pltpu
from jax.sharding import PartitionSpec as P

MESH = pl.DeviceIdType.MESH


def with_halo(array, sides, width):
    for axis, dim in sides:
        size, length = (lax.axis_size(axis), array.shape[dim])
        up = [(i, (i + 1) % size) for i in range(size - 1)]
        down = [(j, i) for i, j in up]
        last = lax.slice_in_dim(array, length - width, length, axis=dim)
        initial = lax.slice_in_dim(array, 0, width, axis=dim)
        before = lax.ppermute(last, axis, up)
        after = lax.ppermute(initial, axis, down)
        array = jnp.concatenate([before, array, after], axis=dim)
    return array


def _coords(nx, nz):
    b = lax.axis_index("bulk")
    s = lax.axis_index("span")
    core = b % 2
    z = (b // 2) % nz
    x = b // (2 * nz)
    return b, s, core, x, z


def _remote(src, dst, send_sem, recv_sem, device):
    return pltpu.make_async_remote_copy(
        src_ref=src, dst_ref=dst, send_sem=send_sem, recv_sem=recv_sem,
        device_id=device, device_id_type=MESH,
    )


def _allreduce_kernel(dims, x_ref, o_ref, s_core, s_x, s_z, s_y, res, send_sem, recv_sem):
    nx, nz, ny = dims
    b, s, core, x, z = _coords(nx, nz)
    rows = x_ref.shape[0]
    half = rows // 2
    chunk = half // nx
    partner = (b + 1 - 2 * core, s)
    x_dev = lambda p: ((p * nz + z) * 2 + core, s)
    z_dev = lambda p: ((x * nz + p) * 2 + core, s)
    y_dev = lambda p: (b, p)
    o_core, o_x, o_z, o_y = 0, 2, 2 + nx, 2 + nx + nz
    o_gx = o_y + ny
    o_gc = o_gx + nx

    barrier = pltpu.get_barrier_semaphore()
    peers = [partner]
    for n, pos, dev in ((nx, x, x_dev), (nz, z, z_dev), (ny, s, y_dev)):
        peers += [dev((pos + d) % n) for d in range(1, n)]
    for peer in peers:
        pl.semaphore_signal(barrier, inc=1, device_id=peer, device_id_type=MESH)
    pl.semaphore_wait(barrier, len(peers))

    mine = pl.multiple_of(core * half, half)
    theirs = pl.multiple_of((1 - core) * half, half)
    c_copy = _remote(x_ref.at[pl.ds(theirs, half)], s_core.at[core],
                     send_sem.at[o_core], recv_sem.at[o_core + core], partner)
    c_copy.start()
    s_core[core] = x_ref[pl.ds(mine, half), :]
    _remote(s_core.at[1 - core], s_core.at[1 - core], send_sem.at[o_core],
            recv_sem.at[o_core + 1 - core], partner).wait_recv()
    c_copy.wait_send()
    s_core[core] = s_core[0] + s_core[1]

    copies = []
    for d in range(1, nx):
        p = (x + d) % nx
        cp = _remote(s_core.at[core, pl.ds(pl.multiple_of(p * chunk, chunk), chunk)], s_x.at[x],
                     send_sem.at[o_x + p], recv_sem.at[o_x + x], x_dev(p))
        cp.start()
        copies.append(cp)
    s_x[x] = s_core[core, pl.ds(pl.multiple_of(x * chunk, chunk), chunk), :]
    for d in range(1, nx):
        j = (x + d) % nx
        _remote(s_x.at[j], s_x.at[j], send_sem.at[o_x + j], recv_sem.at[o_x + j], x_dev(j)).wait_recv()
    for cp in copies:
        cp.wait_send()
    acc = s_x[0]
    for k in range(1, nx):
        acc = acc + s_x[k]

    for n, pos, dev, slots, off in ((nz, z, z_dev, s_z, o_z), (ny, s, y_dev, s_y, o_y)):
        slots[pos] = acc
        copies = []
        for d in range(1, n):
            p = (pos + d) % n
            cp = _remote(slots.at[pos], slots.at[pos], send_sem.at[off + p], recv_sem.at[off + pos], dev(p))
            cp.start()
            copies.append(cp)
        for d in range(1, n):
            j = (pos + d) % n
            _remote(slots.at[j], slots.at[j], send_sem.at[off + j], recv_sem.at[off + j], dev(j)).wait_recv()
        for cp in copies:
            cp.wait_send()
        acc = slots[0]
        for k in range(1, n):
            acc = acc + slots[k]

    row = lambda p: pl.multiple_of(core * half + p * chunk, chunk)
    res[pl.ds(row(x), chunk), :] = acc
    copies = []
    for d in range(1, nx):
        p = (x + d) % nx
        cp = _remote(res.at[pl.ds(row(x), chunk)], res.at[pl.ds(row(x), chunk)],
                     send_sem.at[o_gx + p], recv_sem.at[o_gx + x], x_dev(p))
        cp.start()
        copies.append(cp)
    for d in range(1, nx):
        j = (x + d) % nx
        _remote(res.at[pl.ds(row(j), chunk)], res.at[pl.ds(row(j), chunk)],
                send_sem.at[o_gx + j], recv_sem.at[o_gx + j], x_dev(j)).wait_recv()
    for cp in copies:
        cp.wait_send()

    cp = _remote(res.at[pl.ds(mine, half)], res.at[pl.ds(mine, half)],
                 send_sem.at[o_gc], recv_sem.at[o_gc + core], partner)
    cp.start()
    _remote(res.at[pl.ds(theirs, half)], res.at[pl.ds(theirs, half)],
            send_sem.at[o_gc], recv_sem.at[o_gc + 1 - core], partner).wait_recv()
    cp.wait_send()
    o_ref[...] = res[...]


def make_allreduce(dims, cid):
    nx, nz, ny = dims
    total = 2 + nx + nz + ny + nx + 2

    def allreduce(partial_value):
        rows, cols = partial_value.shape
        half = rows // 2
        chunk = half // nx
        return pl.pallas_call(
            functools.partial(_allreduce_kernel, dims),
            out_shape=jax.ShapeDtypeStruct(partial_value.shape, jnp.float32),
            in_specs=[pl.BlockSpec(memory_space=pltpu.VMEM)],
            out_specs=pl.BlockSpec(memory_space=pltpu.VMEM),
            scratch_shapes=[
                pltpu.VMEM((2, half, cols), jnp.float32),
                pltpu.VMEM((nx, chunk, cols), jnp.float32),
                pltpu.VMEM((nz, chunk, cols), jnp.float32),
                pltpu.VMEM((ny, chunk, cols), jnp.float32),
                pltpu.VMEM((rows, cols), jnp.float32),
                pltpu.SemaphoreType.DMA((total,)),
                pltpu.SemaphoreType.DMA((total,)),
            ],
            compiler_params=pltpu.CompilerParams(collective_id=cid, has_side_effects=True),
        )(partial_value)

    return allreduce


def cholesky_step(data, row_count, allreduce):
    high = lax.Precision.HIGHEST
    width = data.shape[1]
    partial_value = lax.dot_general(
        data, data, (((0,), (0,)), ((), ())), precision=high, preferred_element_type=jnp.float32
    )
    gram = allreduce(partial_value) / row_count
    lower = jnp.linalg.cholesky(gram)
    inverse = lax.linalg.triangular_solve(
        lower, jnp.eye(width, dtype=jnp.float32), left_side=True, lower=True
    )
    result = jnp.dot(data, inverse.T, precision=high, preferred_element_type=jnp.float32)
    return (result, lower)


def shards(dims, snapshots, jac_blocks, jac_cols):
    high = lax.Precision.HIGHEST
    local_rows, width = snapshots.shape
    block_rows = jac_cols.shape[0]
    blk = jac_blocks.shape[2]
    row_count = local_rows * lax.axis_size(("bulk", "span"))
    first, lower1 = cholesky_step(snapshots, row_count, make_allreduce(dims, 0))
    modes, lower2 = cholesky_step(first, row_count, make_allreduce(dims, 1))
    factor = jnp.dot(lower2.T, lower1.T, precision=high, preferred_element_type=jnp.float32)
    modes_b = modes.astype(jnp.bfloat16)
    shard_start = (
        lax.axis_index("span") * lax.axis_size("bulk") + lax.axis_index("bulk")
    ) * block_rows
    relative = jac_cols - shard_start
    extended = with_halo(modes_b, (("bulk", 0),), local_rows)
    ext_blocks = extended.reshape(3 * block_rows, blk, width)
    picked = jnp.take(ext_blocks, relative + block_rows, axis=0)
    product = jnp.einsum("rnij,rnjk->rik", jac_blocks, picked, preferred_element_type=jnp.float32)
    jac_modes = product.astype(jnp.bfloat16).reshape(local_rows, width)
    partial_value = lax.dot_general(
        modes,
        jac_modes.astype(jnp.float32),
        (((0,), (0,)), ((), ())),
        precision=high,
        preferred_element_type=jnp.float32,
    )
    reduced = make_allreduce(dims, 2)(partial_value) / row_count
    return (modes, factor, jac_modes, reduced)


def _torus_dims(mesh):
    coords = [d.coords for d in mesh.devices.flat]
    return tuple(len({c[i] for c in coords}) for i in (0, 2, 1))


def solution(mesh):
    nx, nz, ny = _torus_dims(mesh)
    assert mesh.shape["bulk"] == 2 * nx * nz and mesh.shape["span"] == ny
    return jax.shard_map(
        functools.partial(shards, (nx, nz, ny)),
        mesh=mesh,
        in_specs=(
            P(("span", "bulk"), None),
            P(("span", "bulk"), None, None, None),
            P(("span", "bulk"), None),
        ),
        out_specs=(P(("span", "bulk"), None), P(), P(("span", "bulk"), None), P()),
        check_vma=False,
    )
```

```python
import functools

import jax
import jax.numpy as jnp
from jax import lax
from jax.experimental import pallas as pl
from jax.experimental.pallas import tpu as pltpu
from jax.sharding import PartitionSpec as P

MESH = pl.DeviceIdType.MESH


def with_halo(array, sides, width):
    for axis, dim in sides:
        size, length = (lax.axis_size(axis), array.shape[dim])
        up = [(i, (i + 1) % size) for i in range(size - 1)]
        down = [(j, i) for i, j in up]
        last = lax.slice_in_dim(array, length - width, length, axis=dim)
        initial = lax.slice_in_dim(array, 0, width, axis=dim)
        before = lax.ppermute(last, axis, up)
        after = lax.ppermute(initial, axis, down)
        array = jnp.concatenate([before, array, after], axis=dim)
    return array


def _coords(nx, nz):
    b = lax.axis_index("bulk")
    s = lax.axis_index("span")
    core = b % 2
    z = (b // 2) % nz
    x = b // (2 * nz)
    return b, s, core, x, z


def _remote(src, dst, send_sem, recv_sem, device):
    return pltpu.make_async_remote_copy(
        src_ref=src, dst_ref=dst, send_sem=send_sem, recv_sem=recv_sem,
        device_id=device, device_id_type=MESH,
    )


def _allreduce_kernel(dims, x_ref, o_ref, s_core, s_x, s_z, s_y, res, send_sem, recv_sem):
    nx, nz, ny = dims
    b, s, core, x, z = _coords(nx, nz)
    rows = x_ref.shape[0]
    half = rows // 2
    chunk = half // nx
    partner = (b + 1 - 2 * core, s)
    x_dev = lambda p: ((p * nz + z) * 2 + core, s)
    z_dev = lambda p: ((x * nz + p) * 2 + core, s)
    y_dev = lambda p: (b, p)
    o_core, o_x, o_z, o_y = 0, 2, 2 + nx, 2 + nx + nz
    o_gx = o_y + ny
    o_gc = o_gx + nx

    barrier = pltpu.get_barrier_semaphore()
    peers = [partner]
    for n, pos, dev in ((nx, x, x_dev), (nz, z, z_dev), (ny, s, y_dev)):
        peers += [dev((pos + d) % n) for d in range(1, n)]
    for peer in peers:
        pl.semaphore_signal(barrier, inc=1, device_id=peer, device_id_type=MESH)
    pl.semaphore_wait(barrier, len(peers))

    mine = pl.multiple_of(core * half, half)
    theirs = pl.multiple_of((1 - core) * half, half)
    c_copy = _remote(x_ref.at[pl.ds(theirs, half)], s_core.at[core],
                     send_sem.at[o_core], recv_sem.at[o_core + core], partner)
    c_copy.start()
    s_core[core] = x_ref[pl.ds(mine, half), :]
    _remote(s_core.at[1 - core], s_core.at[1 - core], send_sem.at[o_core],
            recv_sem.at[o_core + 1 - core], partner).wait_recv()
    c_copy.wait_send()
    s_core[core] = s_core[0] + s_core[1]

    copies = []
    for d in range(1, nx):
        p = (x + d) % nx
        cp = _remote(s_core.at[core, pl.ds(pl.multiple_of(p * chunk, chunk), chunk)], s_x.at[x],
                     send_sem.at[o_x + p], recv_sem.at[o_x + x], x_dev(p))
        cp.start()
        copies.append(cp)
    s_x[x] = s_core[core, pl.ds(pl.multiple_of(x * chunk, chunk), chunk), :]
    for d in range(1, nx):
        j = (x + d) % nx
        _remote(s_x.at[j], s_x.at[j], send_sem.at[o_x + j], recv_sem.at[o_x + j], x_dev(j)).wait_recv()
    for cp in copies:
        cp.wait_send()
    acc = s_x[0]
    for k in range(1, nx):
        acc = acc + s_x[k]

    for n, pos, dev, slots, off in ((nz, z, z_dev, s_z, o_z), (ny, s, y_dev, s_y, o_y)):
        slots[pos] = acc
        copies = []
        for d in range(1, n):
            p = (pos + d) % n
            cp = _remote(slots.at[pos], slots.at[pos], send_sem.at[off + p], recv_sem.at[off + pos], dev(p))
            cp.start()
            copies.append(cp)
        for d in range(1, n):
            j = (pos + d) % n
            _remote(slots.at[j], slots.at[j], send_sem.at[off + j], recv_sem.at[off + j], dev(j)).wait_recv()
        for cp in copies:
            cp.wait_send()
        acc = slots[0]
        for k in range(1, n):
            acc = acc + slots[k]

    row = lambda p: pl.multiple_of(core * half + p * chunk, chunk)
    res[pl.ds(row(x), chunk), :] = acc
    copies = []
    for d in range(1, nx):
        p = (x + d) % nx
        cp = _remote(res.at[pl.ds(row(x), chunk)], res.at[pl.ds(row(x), chunk)],
                     send_sem.at[o_gx + p], recv_sem.at[o_gx + x], x_dev(p))
        cp.start()
        copies.append(cp)
    for d in range(1, nx):
        j = (x + d) % nx
        _remote(res.at[pl.ds(row(j), chunk)], res.at[pl.ds(row(j), chunk)],
                send_sem.at[o_gx + j], recv_sem.at[o_gx + j], x_dev(j)).wait_recv()
    for cp in copies:
        cp.wait_send()

    cp = _remote(res.at[pl.ds(mine, half)], res.at[pl.ds(mine, half)],
                 send_sem.at[o_gc], recv_sem.at[o_gc + core], partner)
    cp.start()
    _remote(res.at[pl.ds(theirs, half)], res.at[pl.ds(theirs, half)],
            send_sem.at[o_gc], recv_sem.at[o_gc + 1 - core], partner).wait_recv()
    cp.wait_send()
    o_ref[...] = res[...]


def make_allreduce(dims, cid):
    nx, nz, ny = dims
    total = 2 + nx + nz + ny + nx + 2

    def allreduce(partial_value):
        rows, cols = partial_value.shape
        half = rows // 2
        chunk = half // nx
        return pl.pallas_call(
            functools.partial(_allreduce_kernel, dims),
            out_shape=jax.ShapeDtypeStruct(partial_value.shape, jnp.float32),
            in_specs=[pl.BlockSpec(memory_space=pltpu.VMEM)],
            out_specs=pl.BlockSpec(memory_space=pltpu.VMEM),
            scratch_shapes=[
                pltpu.VMEM((2, half, cols), jnp.float32),
                pltpu.VMEM((nx, chunk, cols), jnp.float32),
                pltpu.VMEM((nz, chunk, cols), jnp.float32),
                pltpu.VMEM((ny, chunk, cols), jnp.float32),
                pltpu.VMEM((rows, cols), jnp.float32),
                pltpu.SemaphoreType.DMA((total,)),
                pltpu.SemaphoreType.DMA((total,)),
            ],
            compiler_params=pltpu.CompilerParams(collective_id=cid, has_side_effects=True),
        )(partial_value)

    return allreduce


def _chol_kernel(g_ref, lt_ref, w_ref, a_ref):
    n = g_ref.shape[0]
    a_ref[...] = g_ref[...]
    sub = lax.broadcasted_iota(jnp.int32, (n, n), 0)
    lane = lax.broadcasted_iota(jnp.int32, (n, n), 1)
    w_ref[...] = jnp.where(sub == lane, 1.0, 0.0).astype(jnp.float32)
    lane_row = lax.broadcasted_iota(jnp.int32, (1, n), 1)
    for k in range(n):
        row = a_ref[k:k + 1, :]
        root = jnp.sqrt(row[:, k:k + 1])
        lrow = jnp.where(lane_row >= k, row / root, 0.0)
        lt_ref[k:k + 1, :] = lrow
        wrow = w_ref[k:k + 1, :] / root
        w_ref[k:k + 1, :] = wrow
        if k + 1 < n:
            r1 = (k + 1) // 8 * 8
            blk = a_ref[r1:, :]
            idx = lax.broadcasted_iota(jnp.int32, (n - r1, 1), 0) + r1
            m = jnp.where(idx > k, blk[:, k:k + 1] / root, 0.0)
            a_ref[r1:, :] = blk - m * lrow
            w_ref[r1:, :] = w_ref[r1:, :] - m * wrow

def chol_inv(g):
    n = g.shape[0]
    return pl.pallas_call(
        _chol_kernel,
        out_shape=(jax.ShapeDtypeStruct((n, n), jnp.float32), jax.ShapeDtypeStruct((n, n), jnp.float32)),
        in_specs=[pl.BlockSpec(memory_space=pltpu.VMEM)],
        out_specs=(pl.BlockSpec(memory_space=pltpu.VMEM), pl.BlockSpec(memory_space=pltpu.VMEM)),
        scratch_shapes=[pltpu.VMEM((n, n), jnp.float32)],
    )(g)


def cholesky_step(data, row_count, allreduce):
    high = lax.Precision.HIGHEST
    partial_value = lax.dot_general(
        data, data, (((0,), (0,)), ((), ())), precision=high, preferred_element_type=jnp.float32
    )
    gram = allreduce(partial_value) / row_count
    gram = (gram + gram.T) / 2
    upper, inverse = chol_inv(gram)
    result = lax.dot_general(
        data, inverse, (((1,), (1,)), ((), ())), precision=high, preferred_element_type=jnp.float32
    )
    return (result, upper)


def shards(dims, snapshots, jac_blocks, jac_cols):
    high = lax.Precision.HIGHEST
    local_rows, width = snapshots.shape
    block_rows = jac_cols.shape[0]
    blk = jac_blocks.shape[2]
    row_count = local_rows * lax.axis_size(("bulk", "span"))
    first, upper1 = cholesky_step(snapshots, row_count, make_allreduce(dims, 0))
    modes, upper2 = cholesky_step(first, row_count, make_allreduce(dims, 1))
    factor = jnp.dot(upper2, upper1, precision=high, preferred_element_type=jnp.float32)
    modes_b = modes.astype(jnp.bfloat16)
    shard_start = (
        lax.axis_index("span") * lax.axis_size("bulk") + lax.axis_index("bulk")
    ) * block_rows
    relative = jac_cols - shard_start
    extended = with_halo(modes_b, (("bulk", 0),), local_rows)
    ext_blocks = extended.reshape(3 * block_rows, blk, width)
    picked = jnp.take(ext_blocks, relative + block_rows, axis=0)
    product = jnp.einsum("rnij,rnjk->rik", jac_blocks, picked, preferred_element_type=jnp.float32)
    jac_modes = product.astype(jnp.bfloat16).reshape(local_rows, width)
    partial_value = lax.dot_general(
        modes,
        jac_modes.astype(jnp.float32),
        (((0,), (0,)), ((), ())),
        precision=high,
        preferred_element_type=jnp.float32,
    )
    reduced = make_allreduce(dims, 2)(partial_value) / row_count
    return (modes, factor, jac_modes, reduced)


def _torus_dims(mesh):
    coords = [d.coords for d in mesh.devices.flat]
    return tuple(len({c[i] for c in coords}) for i in (0, 2, 1))


def solution(mesh):
    nx, nz, ny = _torus_dims(mesh)
    assert mesh.shape["bulk"] == 2 * nx * nz and mesh.shape["span"] == ny
    return jax.shard_map(
        functools.partial(shards, (nx, nz, ny)),
        mesh=mesh,
        in_specs=(
            P(("span", "bulk"), None),
            P(("span", "bulk"), None, None, None),
            P(("span", "bulk"), None),
        ),
        out_specs=(P(("span", "bulk"), None), P(), P(("span", "bulk"), None), P()),
        check_vma=False,
    )
```

```python
import functools

import jax
import jax.numpy as jnp
from jax import lax
from jax.experimental import pallas as pl
from jax.experimental.pallas import tpu as pltpu
from jax.sharding import PartitionSpec as P

MESH = pl.DeviceIdType.MESH


def with_halo(array, sides, width):
    for axis, dim in sides:
        size, length = (lax.axis_size(axis), array.shape[dim])
        up = [(i, (i + 1) % size) for i in range(size - 1)]
        down = [(j, i) for i, j in up]
        last = lax.slice_in_dim(array, length - width, length, axis=dim)
        initial = lax.slice_in_dim(array, 0, width, axis=dim)
        before = lax.ppermute(last, axis, up)
        after = lax.ppermute(initial, axis, down)
        array = jnp.concatenate([before, array, after], axis=dim)
    return array


def _coords(nx, nz):
    b = lax.axis_index("bulk")
    s = lax.axis_index("span")
    core = b % 2
    z = (b // 2) % nz
    x = b // (2 * nz)
    return b, s, core, x, z


def _remote(src, dst, send_sem, recv_sem, device):
    return pltpu.make_async_remote_copy(
        src_ref=src, dst_ref=dst, send_sem=send_sem, recv_sem=recv_sem,
        device_id=device, device_id_type=MESH,
    )


def _allreduce_kernel(dims, x_ref, o_ref, s_core, s_x, s_z, s_y, res, send_sem, recv_sem):
    nx, nz, ny = dims
    b, s, core, x, z = _coords(nx, nz)
    rows = x_ref.shape[0]
    half = rows // 2
    chunk = half // nx
    partner = (b + 1 - 2 * core, s)
    x_dev = lambda p: ((p * nz + z) * 2 + core, s)
    z_dev = lambda p: ((x * nz + p) * 2 + core, s)
    y_dev = lambda p: (b, p)
    o_core, o_x, o_z, o_y = 0, 2, 2 + nx, 2 + nx + nz
    o_gx = o_y + ny
    o_gc = o_gx + nx

    barrier = pltpu.get_barrier_semaphore()
    peers = [partner]
    for n, pos, dev in ((nx, x, x_dev), (nz, z, z_dev), (ny, s, y_dev)):
        peers += [dev((pos + d) % n) for d in range(1, n)]
    for peer in peers:
        pl.semaphore_signal(barrier, inc=1, device_id=peer, device_id_type=MESH)
    pl.semaphore_wait(barrier, len(peers))

    mine = pl.multiple_of(core * half, half)
    theirs = pl.multiple_of((1 - core) * half, half)
    c_copy = _remote(x_ref.at[pl.ds(theirs, half)], s_core.at[core],
                     send_sem.at[o_core], recv_sem.at[o_core + core], partner)
    c_copy.start()
    s_core[core] = x_ref[pl.ds(mine, half), :]
    _remote(s_core.at[1 - core], s_core.at[1 - core], send_sem.at[o_core],
            recv_sem.at[o_core + 1 - core], partner).wait_recv()
    c_copy.wait_send()
    s_core[core] = s_core[0] + s_core[1]

    copies = []
    for d in range(1, nx):
        p = (x + d) % nx
        cp = _remote(s_core.at[core, pl.ds(pl.multiple_of(p * chunk, chunk), chunk)], s_x.at[x],
                     send_sem.at[o_x + p], recv_sem.at[o_x + x], x_dev(p))
        cp.start()
        copies.append(cp)
    s_x[x] = s_core[core, pl.ds(pl.multiple_of(x * chunk, chunk), chunk), :]
    for d in range(1, nx):
        j = (x + d) % nx
        _remote(s_x.at[j], s_x.at[j], send_sem.at[o_x + j], recv_sem.at[o_x + j], x_dev(j)).wait_recv()
    for cp in copies:
        cp.wait_send()
    acc = s_x[0]
    for k in range(1, nx):
        acc = acc + s_x[k]

    for n, pos, dev, slots, off in ((nz, z, z_dev, s_z, o_z), (ny, s, y_dev, s_y, o_y)):
        slots[pos] = acc
        copies = []
        for d in range(1, n):
            p = (pos + d) % n
            cp = _remote(slots.at[pos], slots.at[pos], send_sem.at[off + p], recv_sem.at[off + pos], dev(p))
            cp.start()
            copies.append(cp)
        for d in range(1, n):
            j = (pos + d) % n
            _remote(slots.at[j], slots.at[j], send_sem.at[off + j], recv_sem.at[off + j], dev(j)).wait_recv()
        for cp in copies:
            cp.wait_send()
        acc = slots[0]
        for k in range(1, n):
            acc = acc + slots[k]

    row = lambda p: pl.multiple_of(core * half + p * chunk, chunk)
    res[pl.ds(row(x), chunk), :] = acc
    copies = []
    for d in range(1, nx):
        p = (x + d) % nx
        cp = _remote(res.at[pl.ds(row(x), chunk)], res.at[pl.ds(row(x), chunk)],
                     send_sem.at[o_gx + p], recv_sem.at[o_gx + x], x_dev(p))
        cp.start()
        copies.append(cp)
    for d in range(1, nx):
        j = (x + d) % nx
        _remote(res.at[pl.ds(row(j), chunk)], res.at[pl.ds(row(j), chunk)],
                send_sem.at[o_gx + j], recv_sem.at[o_gx + j], x_dev(j)).wait_recv()
    for cp in copies:
        cp.wait_send()

    cp = _remote(res.at[pl.ds(mine, half)], res.at[pl.ds(mine, half)],
                 send_sem.at[o_gc], recv_sem.at[o_gc + core], partner)
    cp.start()
    _remote(res.at[pl.ds(theirs, half)], res.at[pl.ds(theirs, half)],
            send_sem.at[o_gc], recv_sem.at[o_gc + 1 - core], partner).wait_recv()
    cp.wait_send()
    o_ref[...] = res[...]


def make_allreduce(dims, cid):
    nx, nz, ny = dims
    total = 2 + nx + nz + ny + nx + 2

    def allreduce(partial_value):
        rows, cols = partial_value.shape
        half = rows // 2
        chunk = half // nx
        return pl.pallas_call(
            functools.partial(_allreduce_kernel, dims),
            out_shape=jax.ShapeDtypeStruct(partial_value.shape, jnp.float32),
            in_specs=[pl.BlockSpec(memory_space=pltpu.VMEM)],
            out_specs=pl.BlockSpec(memory_space=pltpu.VMEM),
            scratch_shapes=[
                pltpu.VMEM((2, half, cols), jnp.float32),
                pltpu.VMEM((nx, chunk, cols), jnp.float32),
                pltpu.VMEM((nz, chunk, cols), jnp.float32),
                pltpu.VMEM((ny, chunk, cols), jnp.float32),
                pltpu.VMEM((rows, cols), jnp.float32),
                pltpu.SemaphoreType.DMA((total,)),
                pltpu.SemaphoreType.DMA((total,)),
            ],
            compiler_params=pltpu.CompilerParams(collective_id=cid, has_side_effects=True),
        )(partial_value)

    return allreduce


def _chol_kernel(g_ref, lt_ref, w_ref):
    n = g_ref.shape[0]
    a = g_ref[...]
    sub = lax.broadcasted_iota(jnp.int32, (n, n), 0)
    lane = lax.broadcasted_iota(jnp.int32, (n, n), 1)
    w = jnp.where(sub == lane, 1.0, 0.0).astype(jnp.float32)
    lane_row = lax.broadcasted_iota(jnp.int32, (1, n), 1)
    lt_rows = []
    w_rows = []
    for k in range(n):
        r0 = k // 8 * 8
        row = a[k - r0:k - r0 + 1, :]
        recip = 1.0 / jnp.sqrt(row[:, k:k + 1])
        lrow = jnp.where(lane_row >= k, row * recip, 0.0)
        wrow = w[k - r0:k - r0 + 1, :] * recip
        lt_rows.append(lrow)
        w_rows.append(wrow)
        if k % 8 == 7:
            lt_ref[r0:r0 + 8, :] = jnp.concatenate(lt_rows, axis=0)
            w_ref[r0:r0 + 8, :] = jnp.concatenate(w_rows, axis=0)
            lt_rows, w_rows = [], []
        if k + 1 < n:
            r1 = (k + 1) // 8 * 8
            if r1 > r0:
                a = a[r1 - r0:]
                w = w[r1 - r0:]
            idx = lax.broadcasted_iota(jnp.int32, (n - r1, 1), 0) + r1
            m = jnp.where(idx > k, a[:, k:k + 1] * recip, 0.0)
            a = a - m * lrow
            w = w - m * wrow

def chol_inv(g):
    n = g.shape[0]
    return pl.pallas_call(
        _chol_kernel,
        out_shape=(jax.ShapeDtypeStruct((n, n), jnp.float32), jax.ShapeDtypeStruct((n, n), jnp.float32)),
        in_specs=[pl.BlockSpec(memory_space=pltpu.VMEM)],
        out_specs=(pl.BlockSpec(memory_space=pltpu.VMEM), pl.BlockSpec(memory_space=pltpu.VMEM)),
    )(g)


def cholesky_step(data, row_count, allreduce):
    high = lax.Precision.HIGHEST
    partial_value = lax.dot_general(
        data, data, (((0,), (0,)), ((), ())), precision=high, preferred_element_type=jnp.float32
    )
    gram = allreduce(partial_value) / row_count
    gram = (gram + gram.T) / 2
    upper, inverse = chol_inv(gram)
    result = lax.dot_general(
        data, inverse, (((1,), (1,)), ((), ())), precision=high, preferred_element_type=jnp.float32
    )
    return (result, upper)


def shards(dims, snapshots, jac_blocks, jac_cols):
    high = lax.Precision.HIGHEST
    local_rows, width = snapshots.shape
    block_rows = jac_cols.shape[0]
    blk = jac_blocks.shape[2]
    row_count = local_rows * lax.axis_size(("bulk", "span"))
    first, upper1 = cholesky_step(snapshots, row_count, make_allreduce(dims, 0))
    modes, upper2 = cholesky_step(first, row_count, make_allreduce(dims, 1))
    factor = jnp.dot(upper2, upper1, precision=high, preferred_element_type=jnp.float32)
    modes_b = modes.astype(jnp.bfloat16)
    shard_start = (
        lax.axis_index("span") * lax.axis_size("bulk") + lax.axis_index("bulk")
    ) * block_rows
    relative = jac_cols - shard_start
    extended = with_halo(modes_b, (("bulk", 0),), local_rows)
    ext_blocks = extended.reshape(3 * block_rows, blk, width)
    picked = jnp.take(ext_blocks, relative + block_rows, axis=0)
    product = jnp.einsum("rnij,rnjk->rik", jac_blocks, picked, preferred_element_type=jnp.float32)
    jac_modes = product.astype(jnp.bfloat16).reshape(local_rows, width)
    partial_value = lax.dot_general(
        modes,
        jac_modes.astype(jnp.float32),
        (((0,), (0,)), ((), ())),
        precision=high,
        preferred_element_type=jnp.float32,
    )
    reduced = make_allreduce(dims, 2)(partial_value) / row_count
    return (modes, factor, jac_modes, reduced)


def _torus_dims(mesh):
    coords = [d.coords for d in mesh.devices.flat]
    return tuple(len({c[i] for c in coords}) for i in (0, 2, 1))


def solution(mesh):
    nx, nz, ny = _torus_dims(mesh)
    assert mesh.shape["bulk"] == 2 * nx * nz and mesh.shape["span"] == ny
    return jax.shard_map(
        functools.partial(shards, (nx, nz, ny)),
        mesh=mesh,
        in_specs=(
            P(("span", "bulk"), None),
            P(("span", "bulk"), None, None, None),
            P(("span", "bulk"), None),
        ),
        out_specs=(P(("span", "bulk"), None), P(), P(("span", "bulk"), None), P()),
        check_vma=False,
    )
```

```python
import functools

import jax
import jax.numpy as jnp
from jax import lax
from jax.experimental import pallas as pl
from jax.experimental.pallas import tpu as pltpu
from jax.sharding import PartitionSpec as P

MESH = pl.DeviceIdType.MESH


def _coords(nx, nz):
    b = lax.axis_index("bulk")
    s = lax.axis_index("span")
    core = b % 2
    z = (b // 2) % nz
    x = b // (2 * nz)
    return b, s, core, x, z


def _remote(src, dst, send_sem, recv_sem, device):
    return pltpu.make_async_remote_copy(
        src_ref=src, dst_ref=dst, send_sem=send_sem, recv_sem=recv_sem,
        device_id=device, device_id_type=MESH,
    )


def _allreduce_kernel(dims, x_ref, o_ref, s_core, s_x, s_z, s_y, res, send_sem, recv_sem):
    nx, nz, ny = dims
    b, s, core, x, z = _coords(nx, nz)
    rows = x_ref.shape[0]
    half = rows // 2
    chunk = half // nx
    partner = (b + 1 - 2 * core, s)
    x_dev = lambda p: ((p * nz + z) * 2 + core, s)
    z_dev = lambda p: ((x * nz + p) * 2 + core, s)
    y_dev = lambda p: (b, p)
    o_core, o_x, o_z, o_y = 0, 2, 2 + nx, 2 + nx + nz
    o_gx = o_y + ny
    o_gc = o_gx + nx

    barrier = pltpu.get_barrier_semaphore()
    peers = [partner]
    for n, pos, dev in ((nx, x, x_dev), (nz, z, z_dev), (ny, s, y_dev)):
        peers += [dev((pos + d) % n) for d in range(1, n)]
    for peer in peers:
        pl.semaphore_signal(barrier, inc=1, device_id=peer, device_id_type=MESH)
    pl.semaphore_wait(barrier, len(peers))

    mine = pl.multiple_of(core * half, half)
    theirs = pl.multiple_of((1 - core) * half, half)
    c_copy = _remote(x_ref.at[pl.ds(theirs, half)], s_core.at[core],
                     send_sem.at[o_core], recv_sem.at[o_core + core], partner)
    c_copy.start()
    s_core[core] = x_ref[pl.ds(mine, half), :]
    _remote(s_core.at[1 - core], s_core.at[1 - core], send_sem.at[o_core],
            recv_sem.at[o_core + 1 - core], partner).wait_recv()
    c_copy.wait_send()
    s_core[core] = s_core[0] + s_core[1]

    copies = []
    for d in range(1, nx):
        p = (x + d) % nx
        cp = _remote(s_core.at[core, pl.ds(pl.multiple_of(p * chunk, chunk), chunk)], s_x.at[x],
                     send_sem.at[o_x + p], recv_sem.at[o_x + x], x_dev(p))
        cp.start()
        copies.append(cp)
    s_x[x] = s_core[core, pl.ds(pl.multiple_of(x * chunk, chunk), chunk), :]
    for d in range(1, nx):
        j = (x + d) % nx
        _remote(s_x.at[j], s_x.at[j], send_sem.at[o_x + j], recv_sem.at[o_x + j], x_dev(j)).wait_recv()
    for cp in copies:
        cp.wait_send()
    acc = s_x[0]
    for k in range(1, nx):
        acc = acc + s_x[k]

    for n, pos, dev, slots, off in ((nz, z, z_dev, s_z, o_z), (ny, s, y_dev, s_y, o_y)):
        slots[pos] = acc
        copies = []
        for d in range(1, n):
            p = (pos + d) % n
            cp = _remote(slots.at[pos], slots.at[pos], send_sem.at[off + p], recv_sem.at[off + pos], dev(p))
            cp.start()
            copies.append(cp)
        for d in range(1, n):
            j = (pos + d) % n
            _remote(slots.at[j], slots.at[j], send_sem.at[off + j], recv_sem.at[off + j], dev(j)).wait_recv()
        for cp in copies:
            cp.wait_send()
        acc = slots[0]
        for k in range(1, n):
            acc = acc + slots[k]

    row = lambda p: pl.multiple_of(core * half + p * chunk, chunk)
    res[pl.ds(row(x), chunk), :] = acc
    copies = []
    for d in range(1, nx):
        p = (x + d) % nx
        cp = _remote(res.at[pl.ds(row(x), chunk)], res.at[pl.ds(row(x), chunk)],
                     send_sem.at[o_gx + p], recv_sem.at[o_gx + x], x_dev(p))
        cp.start()
        copies.append(cp)
    for d in range(1, nx):
        j = (x + d) % nx
        _remote(res.at[pl.ds(row(j), chunk)], res.at[pl.ds(row(j), chunk)],
                send_sem.at[o_gx + j], recv_sem.at[o_gx + j], x_dev(j)).wait_recv()
    for cp in copies:
        cp.wait_send()

    cp = _remote(res.at[pl.ds(mine, half)], res.at[pl.ds(mine, half)],
                 send_sem.at[o_gc], recv_sem.at[o_gc + core], partner)
    cp.start()
    _remote(res.at[pl.ds(theirs, half)], res.at[pl.ds(theirs, half)],
            send_sem.at[o_gc], recv_sem.at[o_gc + 1 - core], partner).wait_recv()
    cp.wait_send()
    o_ref[...] = res[...]


def make_allreduce(dims, cid):
    nx, nz, ny = dims
    total = 2 + nx + nz + ny + nx + 2

    def allreduce(partial_value):
        rows, cols = partial_value.shape
        half = rows // 2
        chunk = half // nx
        return pl.pallas_call(
            functools.partial(_allreduce_kernel, dims),
            out_shape=jax.ShapeDtypeStruct(partial_value.shape, jnp.float32),
            in_specs=[pl.BlockSpec(memory_space=pltpu.VMEM)],
            out_specs=pl.BlockSpec(memory_space=pltpu.VMEM),
            scratch_shapes=[
                pltpu.VMEM((2, half, cols), jnp.float32),
                pltpu.VMEM((nx, chunk, cols), jnp.float32),
                pltpu.VMEM((nz, chunk, cols), jnp.float32),
                pltpu.VMEM((ny, chunk, cols), jnp.float32),
                pltpu.VMEM((rows, cols), jnp.float32),
                pltpu.SemaphoreType.DMA((total,)),
                pltpu.SemaphoreType.DMA((total,)),
            ],
            compiler_params=pltpu.CompilerParams(collective_id=cid, has_side_effects=True),
        )(partial_value)

    return allreduce


def _chol_kernel(g_ref, lt_ref, w_ref):
    n = g_ref.shape[0]
    a = g_ref[...]
    sub = lax.broadcasted_iota(jnp.int32, (n, n), 0)
    lane = lax.broadcasted_iota(jnp.int32, (n, n), 1)
    w = jnp.where(sub == lane, 1.0, 0.0).astype(jnp.float32)
    lane_row = lax.broadcasted_iota(jnp.int32, (1, n), 1)
    lt_rows = []
    w_rows = []
    for k in range(n):
        r0 = k // 8 * 8
        row = a[k - r0:k - r0 + 1, :]
        recip = 1.0 / jnp.sqrt(row[:, k:k + 1])
        lrow = jnp.where(lane_row >= k, row * recip, 0.0)
        wrow = w[k - r0:k - r0 + 1, :] * recip
        lt_rows.append(lrow)
        w_rows.append(wrow)
        if k % 8 == 7:
            lt_ref[r0:r0 + 8, :] = jnp.concatenate(lt_rows, axis=0)
            w_ref[r0:r0 + 8, :] = jnp.concatenate(w_rows, axis=0)
            lt_rows, w_rows = [], []
        if k + 1 < n:
            r1 = (k + 1) // 8 * 8
            if r1 > r0:
                a = a[r1 - r0:]
                w = w[r1 - r0:]
            idx = lax.broadcasted_iota(jnp.int32, (n - r1, 1), 0) + r1
            m = jnp.where(idx > k, a[:, k:k + 1] * recip, 0.0)
            a = a - m * lrow
            w = w - m * wrow

def chol_inv(g):
    n = g.shape[0]
    return pl.pallas_call(
        _chol_kernel,
        out_shape=(jax.ShapeDtypeStruct((n, n), jnp.float32), jax.ShapeDtypeStruct((n, n), jnp.float32)),
        in_specs=[pl.BlockSpec(memory_space=pltpu.VMEM)],
        out_specs=(pl.BlockSpec(memory_space=pltpu.VMEM), pl.BlockSpec(memory_space=pltpu.VMEM)),
    )(g)


def _jac_kernel(nbulk, cols_ref, modes_ref, jac_ref, out_ref, ext, send_sem, recv_sem):
    b = lax.axis_index("bulk")
    s = lax.axis_index("span")
    rb = modes_ref.shape[0]
    has_left = b > 0
    has_right = b < nbulk - 1
    barrier = pltpu.get_barrier_semaphore()

    @pl.when(has_left)
    def _():
        pl.semaphore_signal(barrier, inc=1, device_id=(b - 1, s), device_id_type=MESH)

    @pl.when(has_right)
    def _():
        pl.semaphore_signal(barrier, inc=1, device_id=(b + 1, s), device_id_type=MESH)

    pl.semaphore_wait(barrier, has_left.astype(jnp.int32) + has_right.astype(jnp.int32))

    to_left = pltpu.make_async_remote_copy(
        src_ref=modes_ref, dst_ref=ext.at[pl.ds(2 * rb, rb)], send_sem=send_sem.at[0],
        recv_sem=recv_sem.at[1], device_id=(b - 1, s), device_id_type=MESH)
    to_right = pltpu.make_async_remote_copy(
        src_ref=modes_ref, dst_ref=ext.at[pl.ds(0, rb)], send_sem=send_sem.at[1],
        recv_sem=recv_sem.at[0], device_id=(b + 1, s), device_id_type=MESH)

    @pl.when(has_left)
    def _():
        to_left.start()

    @pl.when(has_right)
    def _():
        to_right.start()

    ext[pl.ds(rb, rb)] = modes_ref[...]

    @pl.when(jnp.logical_not(has_left))
    def _():
        ext[pl.ds(0, rb)] = jnp.zeros(modes_ref.shape, modes_ref.dtype)

    @pl.when(jnp.logical_not(has_right))
    def _():
        ext[pl.ds(2 * rb, rb)] = jnp.zeros(modes_ref.shape, modes_ref.dtype)

    @pl.when(has_left)
    def _():
        to_right.wait_recv()
        to_left.wait_send()

    @pl.when(has_right)
    def _():
        to_left.wait_recv()
        to_right.wait_send()

    start = (s * nbulk + b) * rb - rb

    def row(r, carry):
        acc = None
        for n in range(jac_ref.shape[1]):
            idx = jnp.clip(cols_ref[r, n] - start, 0, 3 * rb - 1)
            term = jnp.dot(jac_ref[r, n], ext[idx], preferred_element_type=jnp.float32)
            acc = term if acc is None else acc + term
        out_ref[r] = acc.astype(out_ref.dtype)
        return carry

    lax.fori_loop(0, rb, row, 0)


def jac_apply(nbulk, cid, jac_cols, modes_b, jac_blocks):
    rb, nb, blk, width = jac_blocks.shape[0], jac_blocks.shape[1], jac_blocks.shape[2], modes_b.shape[1]
    modes_blocks = modes_b.reshape(rb, blk, width)
    out = pl.pallas_call(
        functools.partial(_jac_kernel, nbulk),
        out_shape=jax.ShapeDtypeStruct((rb, blk, width), jnp.bfloat16),
        in_specs=[pl.BlockSpec(memory_space=pltpu.SMEM),
                  pl.BlockSpec(memory_space=pltpu.VMEM),
                  pl.BlockSpec(memory_space=pltpu.VMEM)],
        out_specs=pl.BlockSpec(memory_space=pltpu.VMEM),
        scratch_shapes=[
            pltpu.VMEM((3 * rb, blk, width), jnp.bfloat16),
            pltpu.SemaphoreType.DMA((2,)),
            pltpu.SemaphoreType.DMA((2,)),
        ],
        compiler_params=pltpu.CompilerParams(collective_id=cid, has_side_effects=True),
    )(jac_cols, modes_blocks, jac_blocks)
    return out.reshape(rb * blk, width)


def cholesky_step(data, row_count, allreduce):
    high = lax.Precision.HIGHEST
    partial_value = lax.dot_general(
        data, data, (((0,), (0,)), ((), ())), precision=high, preferred_element_type=jnp.float32
    )
    gram = allreduce(partial_value) / row_count
    gram = (gram + gram.T) / 2
    upper, inverse = chol_inv(gram)
    result = lax.dot_general(
        data, inverse, (((1,), (1,)), ((), ())), precision=high, preferred_element_type=jnp.float32
    )
    return (result, upper)


def shards(dims, snapshots, jac_blocks, jac_cols):
    high = lax.Precision.HIGHEST
    local_rows, width = snapshots.shape
    block_rows = jac_cols.shape[0]
    blk = jac_blocks.shape[2]
    row_count = local_rows * lax.axis_size(("bulk", "span"))
    first, upper1 = cholesky_step(snapshots, row_count, make_allreduce(dims, 0))
    modes, upper2 = cholesky_step(first, row_count, make_allreduce(dims, 1))
    factor = jnp.dot(upper2, upper1, precision=high, preferred_element_type=jnp.float32)
    modes_b = modes.astype(jnp.bfloat16)
    jac_modes = jac_apply(lax.axis_size("bulk"), 3, jac_cols, modes_b, jac_blocks)
    partial_value = lax.dot_general(
        modes,
        jac_modes.astype(jnp.float32),
        (((0,), (0,)), ((), ())),
        precision=high,
        preferred_element_type=jnp.float32,
    )
    reduced = make_allreduce(dims, 2)(partial_value) / row_count
    return (modes, factor, jac_modes, reduced)


def _torus_dims(mesh):
    coords = [d.coords for d in mesh.devices.flat]
    return tuple(len({c[i] for c in coords}) for i in (0, 2, 1))


def solution(mesh):
    nx, nz, ny = _torus_dims(mesh)
    assert mesh.shape["bulk"] == 2 * nx * nz and mesh.shape["span"] == ny
    return jax.shard_map(
        functools.partial(shards, (nx, nz, ny)),
        mesh=mesh,
        in_specs=(
            P(("span", "bulk"), None),
            P(("span", "bulk"), None, None, None),
            P(("span", "bulk"), None),
        ),
        out_specs=(P(("span", "bulk"), None), P(), P(("span", "bulk"), None), P()),
        check_vma=False,
    )
```

```python
import functools

import jax
import jax.numpy as jnp
from jax import lax
from jax.experimental import pallas as pl
from jax.experimental.pallas import tpu as pltpu
from jax.sharding import PartitionSpec as P

MESH = pl.DeviceIdType.MESH


def _coords(nx, nz):
    b = lax.axis_index("bulk")
    s = lax.axis_index("span")
    core = b % 2
    z = (b // 2) % nz
    x = b // (2 * nz)
    return b, s, core, x, z


def _remote(src, dst, send_sem, recv_sem, device):
    return pltpu.make_async_remote_copy(
        src_ref=src, dst_ref=dst, send_sem=send_sem, recv_sem=recv_sem,
        device_id=device, device_id_type=MESH,
    )


def _allreduce_kernel(dims, x_ref, o_ref, s_core, s_x, s_z, s_y, res, send_sem, recv_sem):
    nx, nz, ny = dims
    b, s, core, x, z = _coords(nx, nz)
    rows = x_ref.shape[0]
    half = rows // 2
    chunk = half // nx
    partner = (b + 1 - 2 * core, s)
    x_dev = lambda p: ((p * nz + z) * 2 + core, s)
    z_dev = lambda p: ((x * nz + p) * 2 + core, s)
    y_dev = lambda p: (b, p)
    o_core, o_x, o_z, o_y = 0, 2, 2 + nx, 2 + nx + nz
    o_gx = o_y + ny
    o_gc = o_gx + nx

    barrier = pltpu.get_barrier_semaphore()
    peers = [partner]
    for n, pos, dev in ((nx, x, x_dev), (nz, z, z_dev), (ny, s, y_dev)):
        peers += [dev((pos + d) % n) for d in range(1, n)]
    for peer in peers:
        pl.semaphore_signal(barrier, inc=1, device_id=peer, device_id_type=MESH)
    pl.semaphore_wait(barrier, len(peers))

    mine = pl.multiple_of(core * half, half)
    theirs = pl.multiple_of((1 - core) * half, half)
    c_copy = _remote(x_ref.at[pl.ds(theirs, half)], s_core.at[core],
                     send_sem.at[o_core], recv_sem.at[o_core + core], partner)
    c_copy.start()
    s_core[core] = x_ref[pl.ds(mine, half), :]
    _remote(s_core.at[1 - core], s_core.at[1 - core], send_sem.at[o_core],
            recv_sem.at[o_core + 1 - core], partner).wait_recv()
    c_copy.wait_send()
    s_core[core] = s_core[0] + s_core[1]

    copies = []
    for d in range(1, nx):
        p = (x + d) % nx
        cp = _remote(s_core.at[core, pl.ds(pl.multiple_of(p * chunk, chunk), chunk)], s_x.at[x],
                     send_sem.at[o_x + p], recv_sem.at[o_x + x], x_dev(p))
        cp.start()
        copies.append(cp)
    s_x[x] = s_core[core, pl.ds(pl.multiple_of(x * chunk, chunk), chunk), :]
    for d in range(1, nx):
        j = (x + d) % nx
        _remote(s_x.at[j], s_x.at[j], send_sem.at[o_x + j], recv_sem.at[o_x + j], x_dev(j)).wait_recv()
    for cp in copies:
        cp.wait_send()
    acc = s_x[0]
    for k in range(1, nx):
        acc = acc + s_x[k]

    for n, pos, dev, slots, off in ((nz, z, z_dev, s_z, o_z), (ny, s, y_dev, s_y, o_y)):
        slots[pos] = acc
        copies = []
        for d in range(1, n):
            p = (pos + d) % n
            cp = _remote(slots.at[pos], slots.at[pos], send_sem.at[off + p], recv_sem.at[off + pos], dev(p))
            cp.start()
            copies.append(cp)
        for d in range(1, n):
            j = (pos + d) % n
            _remote(slots.at[j], slots.at[j], send_sem.at[off + j], recv_sem.at[off + j], dev(j)).wait_recv()
        for cp in copies:
            cp.wait_send()
        acc = slots[0]
        for k in range(1, n):
            acc = acc + slots[k]

    row = lambda p: pl.multiple_of(core * half + p * chunk, chunk)
    res[pl.ds(row(x), chunk), :] = acc
    copies = []
    for d in range(1, nx):
        p = (x + d) % nx
        cp = _remote(res.at[pl.ds(row(x), chunk)], res.at[pl.ds(row(x), chunk)],
                     send_sem.at[o_gx + p], recv_sem.at[o_gx + x], x_dev(p))
        cp.start()
        copies.append(cp)
    for d in range(1, nx):
        j = (x + d) % nx
        _remote(res.at[pl.ds(row(j), chunk)], res.at[pl.ds(row(j), chunk)],
                send_sem.at[o_gx + j], recv_sem.at[o_gx + j], x_dev(j)).wait_recv()
    for cp in copies:
        cp.wait_send()

    cp = _remote(res.at[pl.ds(mine, half)], res.at[pl.ds(mine, half)],
                 send_sem.at[o_gc], recv_sem.at[o_gc + core], partner)
    cp.start()
    _remote(res.at[pl.ds(theirs, half)], res.at[pl.ds(theirs, half)],
            send_sem.at[o_gc], recv_sem.at[o_gc + 1 - core], partner).wait_recv()
    cp.wait_send()
    o_ref[...] = res[...]


def make_allreduce(dims, cid):
    nx, nz, ny = dims
    total = 2 + nx + nz + ny + nx + 2

    def allreduce(partial_value):
        rows, cols = partial_value.shape
        half = rows // 2
        chunk = half // nx
        return pl.pallas_call(
            functools.partial(_allreduce_kernel, dims),
            out_shape=jax.ShapeDtypeStruct(partial_value.shape, jnp.float32),
            in_specs=[pl.BlockSpec(memory_space=pltpu.VMEM)],
            out_specs=pl.BlockSpec(memory_space=pltpu.VMEM),
            scratch_shapes=[
                pltpu.VMEM((2, half, cols), jnp.float32),
                pltpu.VMEM((nx, chunk, cols), jnp.float32),
                pltpu.VMEM((nz, chunk, cols), jnp.float32),
                pltpu.VMEM((ny, chunk, cols), jnp.float32),
                pltpu.VMEM((rows, cols), jnp.float32),
                pltpu.SemaphoreType.DMA((total,)),
                pltpu.SemaphoreType.DMA((total,)),
            ],
            compiler_params=pltpu.CompilerParams(collective_id=cid, has_side_effects=True),
        )(partial_value)

    return allreduce


def _chol_kernel(count, g_ref, lt_ref, w_ref):
    n = g_ref.shape[0]
    g = g_ref[...] / count
    a = (g + g.T) / 2
    sub = lax.broadcasted_iota(jnp.int32, (n, n), 0)
    lane = lax.broadcasted_iota(jnp.int32, (n, n), 1)
    w = jnp.where(sub == lane, 1.0, 0.0).astype(jnp.float32)
    lane_row = lax.broadcasted_iota(jnp.int32, (1, n), 1)
    lt_rows = []
    w_rows = []
    for k in range(n):
        r0 = k // 8 * 8
        row = a[k - r0:k - r0 + 1, :]
        recip = lax.rsqrt(row[:, k:k + 1])
        lrow = jnp.where(lane_row >= k, row * recip, 0.0)
        wrow = w[k - r0:k - r0 + 1, :] * recip
        lt_rows.append(lrow)
        w_rows.append(wrow)
        if k % 8 == 7:
            lt_ref[r0:r0 + 8, :] = jnp.concatenate(lt_rows, axis=0)
            w_ref[r0:r0 + 8, :] = jnp.concatenate(w_rows, axis=0)
            lt_rows, w_rows = [], []
        if k + 1 < n:
            r1 = (k + 1) // 8 * 8
            if r1 > r0:
                a = a[r1 - r0:]
                w = w[r1 - r0:]
            idx = lax.broadcasted_iota(jnp.int32, (n - r1, 1), 0) + r1
            m = jnp.where(idx > k, a[:, k:k + 1] * recip, 0.0)
            a = a - m * lrow
            w = w - m * wrow

def chol_inv(g, count):
    n = g.shape[0]
    return pl.pallas_call(
        functools.partial(_chol_kernel, float(count)),
        out_shape=(jax.ShapeDtypeStruct((n, n), jnp.float32), jax.ShapeDtypeStruct((n, n), jnp.float32)),
        in_specs=[pl.BlockSpec(memory_space=pltpu.VMEM)],
        out_specs=(pl.BlockSpec(memory_space=pltpu.VMEM), pl.BlockSpec(memory_space=pltpu.VMEM)),
    )(g)


def _jac_kernel(nbulk, cols_ref, modes_ref, jac_ref, out_ref, ext, send_sem, recv_sem):
    b = lax.axis_index("bulk")
    s = lax.axis_index("span")
    rb = modes_ref.shape[0]
    has_left = b > 0
    has_right = b < nbulk - 1
    barrier = pltpu.get_barrier_semaphore()

    @pl.when(has_left)
    def _():
        pl.semaphore_signal(barrier, inc=1, device_id=(b - 1, s), device_id_type=MESH)

    @pl.when(has_right)
    def _():
        pl.semaphore_signal(barrier, inc=1, device_id=(b + 1, s), device_id_type=MESH)

    pl.semaphore_wait(barrier, has_left.astype(jnp.int32) + has_right.astype(jnp.int32))

    to_left = pltpu.make_async_remote_copy(
        src_ref=modes_ref, dst_ref=ext.at[pl.ds(2 * rb, rb)], send_sem=send_sem.at[0],
        recv_sem=recv_sem.at[1], device_id=(b - 1, s), device_id_type=MESH)
    to_right = pltpu.make_async_remote_copy(
        src_ref=modes_ref, dst_ref=ext.at[pl.ds(0, rb)], send_sem=send_sem.at[1],
        recv_sem=recv_sem.at[0], device_id=(b + 1, s), device_id_type=MESH)

    @pl.when(has_left)
    def _():
        to_left.start()

    @pl.when(has_right)
    def _():
        to_right.start()

    ext[pl.ds(rb, rb)] = modes_ref[...]

    @pl.when(jnp.logical_not(has_left))
    def _():
        ext[pl.ds(0, rb)] = jnp.zeros(modes_ref.shape, modes_ref.dtype)

    @pl.when(jnp.logical_not(has_right))
    def _():
        ext[pl.ds(2 * rb, rb)] = jnp.zeros(modes_ref.shape, modes_ref.dtype)

    @pl.when(has_left)
    def _():
        to_right.wait_recv()
        to_left.wait_send()

    @pl.when(has_right)
    def _():
        to_left.wait_recv()
        to_right.wait_send()

    start = (s * nbulk + b) * rb - rb

    def row(r, carry):
        acc = None
        for n in range(jac_ref.shape[1]):
            idx = jnp.clip(cols_ref[r, n] - start, 0, 3 * rb - 1)
            term = jnp.dot(jac_ref[r, n], ext[idx], preferred_element_type=jnp.float32)
            acc = term if acc is None else acc + term
        out_ref[r] = acc.astype(out_ref.dtype)
        return carry

    lax.fori_loop(0, rb, row, 0)


def jac_apply(nbulk, cid, jac_cols, modes_b, jac_blocks):
    rb, nb, blk, width = jac_blocks.shape[0], jac_blocks.shape[1], jac_blocks.shape[2], modes_b.shape[1]
    modes_blocks = modes_b.reshape(rb, blk, width)
    out = pl.pallas_call(
        functools.partial(_jac_kernel, nbulk),
        out_shape=jax.ShapeDtypeStruct((rb, blk, width), jnp.bfloat16),
        in_specs=[pl.BlockSpec(memory_space=pltpu.SMEM),
                  pl.BlockSpec(memory_space=pltpu.VMEM),
                  pl.BlockSpec(memory_space=pltpu.VMEM)],
        out_specs=pl.BlockSpec(memory_space=pltpu.VMEM),
        scratch_shapes=[
            pltpu.VMEM((3 * rb, blk, width), jnp.bfloat16),
            pltpu.SemaphoreType.DMA((2,)),
            pltpu.SemaphoreType.DMA((2,)),
        ],
        compiler_params=pltpu.CompilerParams(collective_id=cid, has_side_effects=True),
    )(jac_cols, modes_blocks, jac_blocks)
    return out.reshape(rb * blk, width)


def cholesky_step(data, row_count, allreduce):
    high = lax.Precision.HIGHEST
    partial_value = lax.dot_general(
        data, data, (((0,), (0,)), ((), ())), precision=high, preferred_element_type=jnp.float32
    )
    upper, inverse = chol_inv(allreduce(partial_value), row_count)
    result = lax.dot_general(
        data, inverse, (((1,), (1,)), ((), ())), precision=high, preferred_element_type=jnp.float32
    )
    return (result, upper)


def shards(dims, snapshots, jac_blocks, jac_cols):
    high = lax.Precision.HIGHEST
    local_rows, width = snapshots.shape
    block_rows = jac_cols.shape[0]
    blk = jac_blocks.shape[2]
    row_count = local_rows * lax.axis_size(("bulk", "span"))
    first, upper1 = cholesky_step(snapshots, row_count, make_allreduce(dims, 0))
    modes, upper2 = cholesky_step(first, row_count, make_allreduce(dims, 1))
    factor = jnp.dot(upper2, upper1, precision=high, preferred_element_type=jnp.float32)
    modes_b = modes.astype(jnp.bfloat16)
    jac_modes = jac_apply(lax.axis_size("bulk"), 3, jac_cols, modes_b, jac_blocks)
    partial_value = lax.dot_general(
        modes,
        jac_modes.astype(jnp.float32),
        (((0,), (0,)), ((), ())),
        precision=high,
        preferred_element_type=jnp.float32,
    )
    reduced = make_allreduce(dims, 2)(partial_value) / row_count
    return (modes, factor, jac_modes, reduced)


def _torus_dims(mesh):
    coords = [d.coords for d in mesh.devices.flat]
    return tuple(len({c[i] for c in coords}) for i in (0, 2, 1))


def solution(mesh):
    nx, nz, ny = _torus_dims(mesh)
    assert mesh.shape["bulk"] == 2 * nx * nz and mesh.shape["span"] == ny
    return jax.shard_map(
        functools.partial(shards, (nx, nz, ny)),
        mesh=mesh,
        in_specs=(
            P(("span", "bulk"), None),
            P(("span", "bulk"), None, None, None),
            P(("span", "bulk"), None),
        ),
        out_specs=(P(("span", "bulk"), None), P(), P(("span", "bulk"), None), P()),
        check_vma=False,
    )
```

```python
import functools

import jax
import jax.numpy as jnp
from jax import lax
from jax.experimental import pallas as pl
from jax.experimental.pallas import tpu as pltpu
from jax.sharding import PartitionSpec as P

MESH = pl.DeviceIdType.MESH


def _coords(nx, nz):
    b = lax.axis_index("bulk")
    s = lax.axis_index("span")
    core = b % 2
    z = (b // 2) % nz
    x = b // (2 * nz)
    return b, s, core, x, z


def _remote(src, dst, send_sem, recv_sem, device):
    return pltpu.make_async_remote_copy(
        src_ref=src, dst_ref=dst, send_sem=send_sem, recv_sem=recv_sem,
        device_id=device, device_id_type=MESH,
    )


def _allreduce_kernel(dims, scale, x_ref, o_ref, s_core, s_x, s_z, s_y, res, send_sem, recv_sem):
    nx, nz, ny = dims
    b, s, core, x, z = _coords(nx, nz)
    rows = x_ref.shape[0]
    half = rows // 2
    chunk = half // nx
    partner = (b + 1 - 2 * core, s)
    x_dev = lambda p: ((p * nz + z) * 2 + core, s)
    z_dev = lambda p: ((x * nz + p) * 2 + core, s)
    y_dev = lambda p: (b, p)
    o_core, o_x, o_z, o_y = 0, 2, 2 + nx, 2 + nx + nz
    o_gx = o_y + ny
    o_gc = o_gx + nx

    barrier = pltpu.get_barrier_semaphore()
    peers = [partner]
    for n, pos, dev in ((nx, x, x_dev), (nz, z, z_dev), (ny, s, y_dev)):
        peers += [dev((pos + d) % n) for d in range(1, n)]
    for peer in peers:
        pl.semaphore_signal(barrier, inc=1, device_id=peer, device_id_type=MESH)
    pl.semaphore_wait(barrier, len(peers))

    mine = pl.multiple_of(core * half, half)
    theirs = pl.multiple_of((1 - core) * half, half)
    c_copy = _remote(x_ref.at[pl.ds(theirs, half)], s_core.at[core],
                     send_sem.at[o_core], recv_sem.at[o_core + core], partner)
    c_copy.start()
    s_core[core] = x_ref[pl.ds(mine, half), :]
    _remote(s_core.at[1 - core], s_core.at[1 - core], send_sem.at[o_core],
            recv_sem.at[o_core + 1 - core], partner).wait_recv()
    c_copy.wait_send()
    s_core[core] = s_core[0] + s_core[1]

    copies = []
    for d in range(1, nx):
        p = (x + d) % nx
        cp = _remote(s_core.at[core, pl.ds(pl.multiple_of(p * chunk, chunk), chunk)], s_x.at[x],
                     send_sem.at[o_x + p], recv_sem.at[o_x + x], x_dev(p))
        cp.start()
        copies.append(cp)
    s_x[x] = s_core[core, pl.ds(pl.multiple_of(x * chunk, chunk), chunk), :]
    for d in range(1, nx):
        j = (x + d) % nx
        _remote(s_x.at[j], s_x.at[j], send_sem.at[o_x + j], recv_sem.at[o_x + j], x_dev(j)).wait_recv()
    for cp in copies:
        cp.wait_send()
    acc = s_x[0]
    for k in range(1, nx):
        acc = acc + s_x[k]

    for n, pos, dev, slots, off in ((nz, z, z_dev, s_z, o_z), (ny, s, y_dev, s_y, o_y)):
        slots[pos] = acc
        copies = []
        for d in range(1, n):
            p = (pos + d) % n
            cp = _remote(slots.at[pos], slots.at[pos], send_sem.at[off + p], recv_sem.at[off + pos], dev(p))
            cp.start()
            copies.append(cp)
        for d in range(1, n):
            j = (pos + d) % n
            _remote(slots.at[j], slots.at[j], send_sem.at[off + j], recv_sem.at[off + j], dev(j)).wait_recv()
        for cp in copies:
            cp.wait_send()
        acc = slots[0]
        for k in range(1, n):
            acc = acc + slots[k]

    row = lambda p: pl.multiple_of(core * half + p * chunk, chunk)
    res[pl.ds(row(x), chunk), :] = acc
    copies = []
    for d in range(1, nx):
        p = (x + d) % nx
        cp = _remote(res.at[pl.ds(row(x), chunk)], res.at[pl.ds(row(x), chunk)],
                     send_sem.at[o_gx + p], recv_sem.at[o_gx + x], x_dev(p))
        cp.start()
        copies.append(cp)
    for d in range(1, nx):
        j = (x + d) % nx
        _remote(res.at[pl.ds(row(j), chunk)], res.at[pl.ds(row(j), chunk)],
                send_sem.at[o_gx + j], recv_sem.at[o_gx + j], x_dev(j)).wait_recv()
    for cp in copies:
        cp.wait_send()

    cp = _remote(res.at[pl.ds(mine, half)], res.at[pl.ds(mine, half)],
                 send_sem.at[o_gc], recv_sem.at[o_gc + core], partner)
    cp.start()
    _remote(res.at[pl.ds(theirs, half)], res.at[pl.ds(theirs, half)],
            send_sem.at[o_gc], recv_sem.at[o_gc + 1 - core], partner).wait_recv()
    cp.wait_send()
    o_ref[...] = res[...] if scale == 1.0 else res[...] * scale


def make_allreduce(dims, cid, scale=1.0):
    nx, nz, ny = dims
    total = 2 + nx + nz + ny + nx + 2

    def allreduce(partial_value):
        rows, cols = partial_value.shape
        half = rows // 2
        chunk = half // nx
        return pl.pallas_call(
            functools.partial(_allreduce_kernel, dims, scale),
            out_shape=jax.ShapeDtypeStruct(partial_value.shape, jnp.float32),
            in_specs=[pl.BlockSpec(memory_space=pltpu.VMEM)],
            out_specs=pl.BlockSpec(memory_space=pltpu.VMEM),
            scratch_shapes=[
                pltpu.VMEM((2, half, cols), jnp.float32),
                pltpu.VMEM((nx, chunk, cols), jnp.float32),
                pltpu.VMEM((nz, chunk, cols), jnp.float32),
                pltpu.VMEM((ny, chunk, cols), jnp.float32),
                pltpu.VMEM((rows, cols), jnp.float32),
                pltpu.SemaphoreType.DMA((total,)),
                pltpu.SemaphoreType.DMA((total,)),
            ],
            compiler_params=pltpu.CompilerParams(collective_id=cid, has_side_effects=True),
        )(partial_value)

    return allreduce


def _chol_kernel(count, g_ref, lt_ref, w_ref):
    n = g_ref.shape[0]
    g = g_ref[...] / count
    a = (g + g.T) / 2
    sub = lax.broadcasted_iota(jnp.int32, (n, n), 0)
    lane = lax.broadcasted_iota(jnp.int32, (n, n), 1)
    w = jnp.where(sub == lane, 1.0, 0.0).astype(jnp.float32)
    lane_row = lax.broadcasted_iota(jnp.int32, (1, n), 1)
    lt_rows = []
    w_rows = []
    for k in range(n):
        r0 = k // 8 * 8
        row = a[k - r0:k - r0 + 1, :]
        recip = lax.rsqrt(row[:, k:k + 1])
        lrow = jnp.where(lane_row >= k, row * recip, 0.0)
        wrow = w[k - r0:k - r0 + 1, :] * recip
        lt_rows.append(lrow)
        w_rows.append(wrow)
        if k % 8 == 7:
            lt_ref[r0:r0 + 8, :] = jnp.concatenate(lt_rows, axis=0)
            w_ref[r0:r0 + 8, :] = jnp.concatenate(w_rows, axis=0)
            lt_rows, w_rows = [], []
        if k + 1 < n:
            r1 = (k + 1) // 8 * 8
            if r1 > r0:
                a = a[r1 - r0:]
                w = w[r1 - r0:]
            idx = lax.broadcasted_iota(jnp.int32, (n - r1, 1), 0) + r1
            m = jnp.where(idx > k, a[:, k:k + 1] * recip, 0.0)
            a = a - m * lrow
            w = w - m * wrow

def chol_inv(g, count):
    n = g.shape[0]
    return pl.pallas_call(
        functools.partial(_chol_kernel, float(count)),
        out_shape=(jax.ShapeDtypeStruct((n, n), jnp.float32), jax.ShapeDtypeStruct((n, n), jnp.float32)),
        in_specs=[pl.BlockSpec(memory_space=pltpu.VMEM)],
        out_specs=(pl.BlockSpec(memory_space=pltpu.VMEM), pl.BlockSpec(memory_space=pltpu.VMEM)),
    )(g)


def _jac_kernel(nbulk, cols_hbm, modes_ref, jac_ref, out_ref, ext, cols_ref, cols_sem, send_sem, recv_sem):
    cols_copy = pltpu.make_async_copy(cols_hbm, cols_ref, cols_sem)
    cols_copy.start()
    b = lax.axis_index("bulk")
    s = lax.axis_index("span")
    rb = modes_ref.shape[0]
    has_left = b > 0
    has_right = b < nbulk - 1
    barrier = pltpu.get_barrier_semaphore()

    @pl.when(has_left)
    def _():
        pl.semaphore_signal(barrier, inc=1, device_id=(b - 1, s), device_id_type=MESH)

    @pl.when(has_right)
    def _():
        pl.semaphore_signal(barrier, inc=1, device_id=(b + 1, s), device_id_type=MESH)

    pl.semaphore_wait(barrier, has_left.astype(jnp.int32) + has_right.astype(jnp.int32))

    to_left = pltpu.make_async_remote_copy(
        src_ref=modes_ref, dst_ref=ext.at[pl.ds(2 * rb, rb)], send_sem=send_sem.at[0],
        recv_sem=recv_sem.at[1], device_id=(b - 1, s), device_id_type=MESH)
    to_right = pltpu.make_async_remote_copy(
        src_ref=modes_ref, dst_ref=ext.at[pl.ds(0, rb)], send_sem=send_sem.at[1],
        recv_sem=recv_sem.at[0], device_id=(b + 1, s), device_id_type=MESH)

    @pl.when(has_left)
    def _():
        to_left.start()

    @pl.when(has_right)
    def _():
        to_right.start()

    ext[pl.ds(rb, rb)] = modes_ref[...]

    @pl.when(jnp.logical_not(has_left))
    def _():
        ext[pl.ds(0, rb)] = jnp.zeros(modes_ref.shape, modes_ref.dtype)

    @pl.when(jnp.logical_not(has_right))
    def _():
        ext[pl.ds(2 * rb, rb)] = jnp.zeros(modes_ref.shape, modes_ref.dtype)

    @pl.when(has_left)
    def _():
        to_right.wait_recv()
        to_left.wait_send()

    @pl.when(has_right)
    def _():
        to_left.wait_recv()
        to_right.wait_send()

    cols_copy.wait()
    start = (s * nbulk + b) * rb - rb

    def row(r, carry):
        acc = None
        for n in range(jac_ref.shape[1]):
            idx = jnp.clip(cols_ref[n, r] - start, 0, 3 * rb - 1)
            term = jnp.dot(jac_ref[r, n], ext[idx], preferred_element_type=jnp.float32)
            acc = term if acc is None else acc + term
        out_ref[r] = acc.astype(out_ref.dtype)
        return carry

    lax.fori_loop(0, rb, row, 0)


def jac_apply(nbulk, cid, jac_cols, modes_b, jac_blocks):
    rb, nb, blk, width = jac_blocks.shape[0], jac_blocks.shape[1], jac_blocks.shape[2], modes_b.shape[1]
    modes_blocks = modes_b.reshape(rb, blk, width)
    out = pl.pallas_call(
        functools.partial(_jac_kernel, nbulk),
        out_shape=jax.ShapeDtypeStruct((rb, blk, width), jnp.bfloat16),
        in_specs=[pl.BlockSpec(memory_space=pl.ANY),
                  pl.BlockSpec(memory_space=pltpu.VMEM),
                  pl.BlockSpec(memory_space=pltpu.VMEM)],
        out_specs=pl.BlockSpec(memory_space=pltpu.VMEM),
        scratch_shapes=[
            pltpu.VMEM((3 * rb, blk, width), jnp.bfloat16),
            pltpu.SMEM(jac_cols.shape[::-1], jnp.int32),
            pltpu.SemaphoreType.DMA(()),
            pltpu.SemaphoreType.DMA((2,)),
            pltpu.SemaphoreType.DMA((2,)),
        ],
        compiler_params=pltpu.CompilerParams(collective_id=cid, has_side_effects=True),
    )(jac_cols.T, modes_blocks, jac_blocks)
    return out.reshape(rb * blk, width)


def cholesky_step(data, row_count, allreduce):
    high = lax.Precision.HIGHEST
    partial_value = lax.dot_general(
        data, data, (((0,), (0,)), ((), ())), precision=high, preferred_element_type=jnp.float32
    )
    upper, inverse = chol_inv(allreduce(partial_value), row_count)
    result = lax.dot_general(
        data, inverse, (((1,), (1,)), ((), ())), precision=high, preferred_element_type=jnp.float32
    )
    return (result, upper)


def shards(dims, snapshots, jac_blocks, jac_cols):
    high = lax.Precision.HIGHEST
    local_rows, width = snapshots.shape
    block_rows = jac_cols.shape[0]
    blk = jac_blocks.shape[2]
    row_count = local_rows * lax.axis_size(("bulk", "span"))
    first, upper1 = cholesky_step(snapshots, row_count, make_allreduce(dims, 0))
    modes, upper2 = cholesky_step(first, row_count, make_allreduce(dims, 1))
    factor = jnp.dot(upper2, upper1, precision=high, preferred_element_type=jnp.float32)
    modes_b = modes.astype(jnp.bfloat16)
    jac_modes = jac_apply(lax.axis_size("bulk"), 3, jac_cols, modes_b, jac_blocks)
    partial_value = lax.dot_general(
        modes,
        jac_modes.astype(jnp.float32),
        (((0,), (0,)), ((), ())),
        precision=high,
        preferred_element_type=jnp.float32,
    )
    reduced = make_allreduce(dims, 2, 1.0 / row_count)(partial_value)
    return (modes, factor, jac_modes, reduced)


def _torus_dims(mesh):
    coords = [d.coords for d in mesh.devices.flat]
    return tuple(len({c[i] for c in coords}) for i in (0, 2, 1))


def solution(mesh):
    nx, nz, ny = _torus_dims(mesh)
    assert mesh.shape["bulk"] == 2 * nx * nz and mesh.shape["span"] == ny
    return jax.shard_map(
        functools.partial(shards, (nx, nz, ny)),
        mesh=mesh,
        in_specs=(
            P(("span", "bulk"), None),
            P(("span", "bulk"), None, None, None),
            P(("span", "bulk"), None),
        ),
        out_specs=(P(("span", "bulk"), None), P(), P(("span", "bulk"), None), P()),
        check_vma=False,
    )
```

```python
import functools

import jax
import jax.numpy as jnp
from jax import lax
from jax.experimental import pallas as pl
from jax.experimental.pallas import tpu as pltpu
from jax.sharding import PartitionSpec as P

MESH = pl.DeviceIdType.MESH


def _coords(nx, nz):
    b = lax.axis_index("bulk")
    s = lax.axis_index("span")
    core = b % 2
    z = (b // 2) % nz
    x = b // (2 * nz)
    return b, s, core, x, z


def _remote(src, dst, send_sem, recv_sem, device):
    return pltpu.make_async_remote_copy(
        src_ref=src, dst_ref=dst, send_sem=send_sem, recv_sem=recv_sem,
        device_id=device, device_id_type=MESH,
    )


def _allreduce_kernel(dims, scale, x_ref, o_ref, s_core, s_x, s_z, s_y, res, send_sem, recv_sem):
    nx, nz, ny = dims
    b, s, core, x, z = _coords(nx, nz)
    rows = x_ref.shape[0]
    half = rows // 2
    chunk = half // nx
    partner = (b + 1 - 2 * core, s)
    x_dev = lambda p: ((p * nz + z) * 2 + core, s)
    z_dev = lambda p: ((x * nz + p) * 2 + core, s)
    y_dev = lambda p: (b, p)
    o_core, o_x, o_z, o_y = 0, 2, 2 + nx, 2 + nx + nz
    o_gx = o_y + ny
    o_gc = o_gx + nx

    barrier = pltpu.get_barrier_semaphore()
    peers = [partner]
    for n, pos, dev in ((nx, x, x_dev), (nz, z, z_dev), (ny, s, y_dev)):
        peers += [dev((pos + d) % n) for d in range(1, n)]
    for peer in peers:
        pl.semaphore_signal(barrier, inc=1, device_id=peer, device_id_type=MESH)
    pl.semaphore_wait(barrier, len(peers))

    mine = pl.multiple_of(core * half, half)
    theirs = pl.multiple_of((1 - core) * half, half)
    c_copy = _remote(x_ref.at[pl.ds(theirs, half)], s_core.at[core],
                     send_sem.at[o_core], recv_sem.at[o_core + core], partner)
    c_copy.start()
    s_core[core] = x_ref[pl.ds(mine, half), :]
    _remote(s_core.at[1 - core], s_core.at[1 - core], send_sem.at[o_core],
            recv_sem.at[o_core + 1 - core], partner).wait_recv()
    c_copy.wait_send()
    s_core[core] = s_core[0] + s_core[1]

    copies = []
    for d in range(1, nx):
        p = (x + d) % nx
        cp = _remote(s_core.at[core, pl.ds(pl.multiple_of(p * chunk, chunk), chunk)], s_x.at[x],
                     send_sem.at[o_x + p], recv_sem.at[o_x + x], x_dev(p))
        cp.start()
        copies.append(cp)
    s_x[x] = s_core[core, pl.ds(pl.multiple_of(x * chunk, chunk), chunk), :]
    for d in range(1, nx):
        j = (x + d) % nx
        _remote(s_x.at[j], s_x.at[j], send_sem.at[o_x + j], recv_sem.at[o_x + j], x_dev(j)).wait_recv()
    for cp in copies:
        cp.wait_send()
    acc = s_x[0]
    for k in range(1, nx):
        acc = acc + s_x[k]

    for n, pos, dev, slots, off in ((nz, z, z_dev, s_z, o_z), (ny, s, y_dev, s_y, o_y)):
        slots[pos] = acc
        copies = []
        for d in range(1, n):
            p = (pos + d) % n
            cp = _remote(slots.at[pos], slots.at[pos], send_sem.at[off + p], recv_sem.at[off + pos], dev(p))
            cp.start()
            copies.append(cp)
        for d in range(1, n):
            j = (pos + d) % n
            _remote(slots.at[j], slots.at[j], send_sem.at[off + j], recv_sem.at[off + j], dev(j)).wait_recv()
        for cp in copies:
            cp.wait_send()
        acc = slots[0]
        for k in range(1, n):
            acc = acc + slots[k]

    row = lambda p: pl.multiple_of(core * half + p * chunk, chunk)
    res[pl.ds(row(x), chunk), :] = acc
    copies = []
    for d in range(1, nx):
        p = (x + d) % nx
        cp = _remote(res.at[pl.ds(row(x), chunk)], res.at[pl.ds(row(x), chunk)],
                     send_sem.at[o_gx + p], recv_sem.at[o_gx + x], x_dev(p))
        cp.start()
        copies.append(cp)
    for d in range(1, nx):
        j = (x + d) % nx
        _remote(res.at[pl.ds(row(j), chunk)], res.at[pl.ds(row(j), chunk)],
                send_sem.at[o_gx + j], recv_sem.at[o_gx + j], x_dev(j)).wait_recv()
    for cp in copies:
        cp.wait_send()

    cp = _remote(res.at[pl.ds(mine, half)], res.at[pl.ds(mine, half)],
                 send_sem.at[o_gc], recv_sem.at[o_gc + core], partner)
    cp.start()
    _remote(res.at[pl.ds(theirs, half)], res.at[pl.ds(theirs, half)],
            send_sem.at[o_gc], recv_sem.at[o_gc + 1 - core], partner).wait_recv()
    cp.wait_send()
    o_ref[...] = res[...] if scale == 1.0 else res[...] * scale


def make_allreduce(dims, cid, scale=1.0):
    nx, nz, ny = dims
    total = 2 + nx + nz + ny + nx + 2

    def allreduce(partial_value):
        rows, cols = partial_value.shape
        half = rows // 2
        chunk = half // nx
        return pl.pallas_call(
            functools.partial(_allreduce_kernel, dims, scale),
            out_shape=jax.ShapeDtypeStruct(partial_value.shape, jnp.float32),
            in_specs=[pl.BlockSpec(memory_space=pltpu.VMEM)],
            out_specs=pl.BlockSpec(memory_space=pltpu.VMEM),
            scratch_shapes=[
                pltpu.VMEM((2, half, cols), jnp.float32),
                pltpu.VMEM((nx, chunk, cols), jnp.float32),
                pltpu.VMEM((nz, chunk, cols), jnp.float32),
                pltpu.VMEM((ny, chunk, cols), jnp.float32),
                pltpu.VMEM((rows, cols), jnp.float32),
                pltpu.SemaphoreType.DMA((total,)),
                pltpu.SemaphoreType.DMA((total,)),
            ],
            compiler_params=pltpu.CompilerParams(collective_id=cid, has_side_effects=True),
        )(partial_value)

    return allreduce


def _chol_kernel(count, g_ref, lt_ref, w_ref):
    n = g_ref.shape[0]
    g = g_ref[...] / count
    a = (g + g.T) / 2
    sub = lax.broadcasted_iota(jnp.int32, (n, n), 0)
    lane = lax.broadcasted_iota(jnp.int32, (n, n), 1)
    w = jnp.where(sub == lane, 1.0, 0.0).astype(jnp.float32)
    lane_row = lax.broadcasted_iota(jnp.int32, (1, n), 1)
    lt_rows = []
    w_rows = []
    for k in range(n):
        r0 = k // 8 * 8
        row = a[k - r0:k - r0 + 1, :]
        colb = jnp.broadcast_to(a[:, k:k + 1], a.shape)
        recip = lax.rsqrt(colb[k - r0:k - r0 + 1, :])
        lrow = jnp.where(lane_row >= k, row * recip, 0.0)
        wrow = w[k - r0:k - r0 + 1, :] * recip
        lt_rows.append(lrow)
        w_rows.append(wrow)
        if k % 8 == 7:
            lt_ref[r0:r0 + 8, :] = jnp.concatenate(lt_rows, axis=0)
            w_ref[r0:r0 + 8, :] = jnp.concatenate(w_rows, axis=0)
            lt_rows, w_rows = [], []
        if k + 1 < n:
            r1 = (k + 1) // 8 * 8
            if r1 > r0:
                a = a[r1 - r0:]
                w = w[r1 - r0:]
                colb = colb[r1 - r0:]
            idx = lax.broadcasted_iota(jnp.int32, (n - r1, 1), 0) + r1
            m = jnp.where(idx > k, colb * recip, 0.0)
            a = a - m * lrow
            w = w - m * wrow


def chol_inv(g, count):
    n = g.shape[0]
    return pl.pallas_call(
        functools.partial(_chol_kernel, float(count)),
        out_shape=(jax.ShapeDtypeStruct((n, n), jnp.float32), jax.ShapeDtypeStruct((n, n), jnp.float32)),
        in_specs=[pl.BlockSpec(memory_space=pltpu.VMEM)],
        out_specs=(pl.BlockSpec(memory_space=pltpu.VMEM), pl.BlockSpec(memory_space=pltpu.VMEM)),
    )(g)


def _jac_kernel(nbulk, cols_hbm, modes_ref, jac_ref, out_ref, ext, cols_ref, cols_sem, send_sem, recv_sem):
    cols_copy = pltpu.make_async_copy(cols_hbm, cols_ref, cols_sem)
    cols_copy.start()
    b = lax.axis_index("bulk")
    s = lax.axis_index("span")
    rb = modes_ref.shape[0]
    has_left = b > 0
    has_right = b < nbulk - 1
    barrier = pltpu.get_barrier_semaphore()

    @pl.when(has_left)
    def _():
        pl.semaphore_signal(barrier, inc=1, device_id=(b - 1, s), device_id_type=MESH)

    @pl.when(has_right)
    def _():
        pl.semaphore_signal(barrier, inc=1, device_id=(b + 1, s), device_id_type=MESH)

    pl.semaphore_wait(barrier, has_left.astype(jnp.int32) + has_right.astype(jnp.int32))

    to_left = pltpu.make_async_remote_copy(
        src_ref=modes_ref, dst_ref=ext.at[pl.ds(2 * rb, rb)], send_sem=send_sem.at[0],
        recv_sem=recv_sem.at[1], device_id=(b - 1, s), device_id_type=MESH)
    to_right = pltpu.make_async_remote_copy(
        src_ref=modes_ref, dst_ref=ext.at[pl.ds(0, rb)], send_sem=send_sem.at[1],
        recv_sem=recv_sem.at[0], device_id=(b + 1, s), device_id_type=MESH)

    @pl.when(has_left)
    def _():
        to_left.start()

    @pl.when(has_right)
    def _():
        to_right.start()

    ext[pl.ds(rb, rb)] = modes_ref[...]

    @pl.when(jnp.logical_not(has_left))
    def _():
        ext[pl.ds(0, rb)] = jnp.zeros(modes_ref.shape, modes_ref.dtype)

    @pl.when(jnp.logical_not(has_right))
    def _():
        ext[pl.ds(2 * rb, rb)] = jnp.zeros(modes_ref.shape, modes_ref.dtype)

    @pl.when(has_left)
    def _():
        to_right.wait_recv()
        to_left.wait_send()

    @pl.when(has_right)
    def _():
        to_left.wait_recv()
        to_right.wait_send()

    cols_copy.wait()
    start = (s * nbulk + b) * rb - rb

    def row(r, carry):
        acc = None
        for n in range(jac_ref.shape[1]):
            idx = jnp.clip(cols_ref[n, r] - start, 0, 3 * rb - 1)
            term = jnp.dot(jac_ref[r, n], ext[idx], preferred_element_type=jnp.float32)
            acc = term if acc is None else acc + term
        out_ref[r] = acc.astype(out_ref.dtype)
        return carry

    lax.fori_loop(0, rb, row, 0)


def jac_apply(nbulk, cid, jac_cols, modes_b, jac_blocks):
    rb, nb, blk, width = jac_blocks.shape[0], jac_blocks.shape[1], jac_blocks.shape[2], modes_b.shape[1]
    modes_blocks = modes_b.reshape(rb, blk, width)
    out = pl.pallas_call(
        functools.partial(_jac_kernel, nbulk),
        out_shape=jax.ShapeDtypeStruct((rb, blk, width), jnp.bfloat16),
        in_specs=[pl.BlockSpec(memory_space=pl.ANY),
                  pl.BlockSpec(memory_space=pltpu.VMEM),
                  pl.BlockSpec(memory_space=pltpu.VMEM)],
        out_specs=pl.BlockSpec(memory_space=pltpu.VMEM),
        scratch_shapes=[
            pltpu.VMEM((3 * rb, blk, width), jnp.bfloat16),
            pltpu.SMEM(jac_cols.shape[::-1], jnp.int32),
            pltpu.SemaphoreType.DMA(()),
            pltpu.SemaphoreType.DMA((2,)),
            pltpu.SemaphoreType.DMA((2,)),
        ],
        compiler_params=pltpu.CompilerParams(collective_id=cid, has_side_effects=True),
    )(jac_cols.T, modes_blocks, jac_blocks)
    return out.reshape(rb * blk, width)


def cholesky_step(data, row_count, allreduce):
    high = lax.Precision.HIGHEST
    partial_value = lax.dot_general(
        data, data, (((0,), (0,)), ((), ())), precision=high, preferred_element_type=jnp.float32
    )
    upper, inverse = chol_inv(allreduce(partial_value), row_count)
    result = lax.dot_general(
        data, inverse, (((1,), (1,)), ((), ())), precision=high, preferred_element_type=jnp.float32
    )
    return (result, upper)


def shards(dims, snapshots, jac_blocks, jac_cols):
    high = lax.Precision.HIGHEST
    local_rows, width = snapshots.shape
    block_rows = jac_cols.shape[0]
    blk = jac_blocks.shape[2]
    row_count = local_rows * lax.axis_size(("bulk", "span"))
    first, upper1 = cholesky_step(snapshots, row_count, make_allreduce(dims, 0))
    modes, upper2 = cholesky_step(first, row_count, make_allreduce(dims, 1))
    factor = jnp.dot(upper2, upper1, precision=high, preferred_element_type=jnp.float32)
    modes_b = modes.astype(jnp.bfloat16)
    jac_modes = jac_apply(lax.axis_size("bulk"), 3, jac_cols, modes_b, jac_blocks)
    partial_value = lax.dot_general(
        modes,
        jac_modes.astype(jnp.float32),
        (((0,), (0,)), ((), ())),
        precision=high,
        preferred_element_type=jnp.float32,
    )
    reduced = make_allreduce(dims, 2, 1.0 / row_count)(partial_value)
    return (modes, factor, jac_modes, reduced)


def _torus_dims(mesh):
    coords = [d.coords for d in mesh.devices.flat]
    return tuple(len({c[i] for c in coords}) for i in (0, 2, 1))


def solution(mesh):
    nx, nz, ny = _torus_dims(mesh)
    assert mesh.shape["bulk"] == 2 * nx * nz and mesh.shape["span"] == ny
    return jax.shard_map(
        functools.partial(shards, (nx, nz, ny)),
        mesh=mesh,
        in_specs=(
            P(("span", "bulk"), None),
            P(("span", "bulk"), None, None, None),
            P(("span", "bulk"), None),
        ),
        out_specs=(P(("span", "bulk"), None), P(), P(("span", "bulk"), None), P()),
        check_vma=False,
    )
```

```python
import functools

import jax
import jax.numpy as jnp
from jax import lax
from jax.experimental import pallas as pl
from jax.experimental.pallas import tpu as pltpu
from jax.sharding import PartitionSpec as P

MESH = pl.DeviceIdType.MESH


def _coords(nx, nz):
    b = lax.axis_index("bulk")
    s = lax.axis_index("span")
    core = b % 2
    z = (b // 2) % nz
    x = b // (2 * nz)
    return b, s, core, x, z


def _remote(src, dst, send_sem, recv_sem, device):
    return pltpu.make_async_remote_copy(
        src_ref=src, dst_ref=dst, send_sem=send_sem, recv_sem=recv_sem,
        device_id=device, device_id_type=MESH,
    )


def _allreduce_kernel(dims, scale, x_ref, o_ref, s_core, s_x, s_z, s_y, res, send_sem, recv_sem):
    nx, nz, ny = dims
    b, s, core, x, z = _coords(nx, nz)
    rows = x_ref.shape[0]
    half = rows // 2
    chunk = half // nx
    partner = (b + 1 - 2 * core, s)
    x_dev = lambda p: ((p * nz + z) * 2 + core, s)
    z_dev = lambda p: ((x * nz + p) * 2 + core, s)
    y_dev = lambda p: (b, p)
    o_core, o_x, o_z, o_y = 0, 2, 2 + nx, 2 + nx + nz
    o_gx = o_y + ny
    o_gc = o_gx + nx

    barrier = pltpu.get_barrier_semaphore()
    peers = [partner]
    for n, pos, dev in ((nx, x, x_dev), (nz, z, z_dev), (ny, s, y_dev)):
        peers += [dev((pos + d) % n) for d in range(1, n)]
    for peer in peers:
        pl.semaphore_signal(barrier, inc=1, device_id=peer, device_id_type=MESH)
    pl.semaphore_wait(barrier, len(peers))

    mine = pl.multiple_of(core * half, half)
    theirs = pl.multiple_of((1 - core) * half, half)
    c_copy = _remote(x_ref.at[pl.ds(theirs, half)], s_core.at[core],
                     send_sem.at[o_core], recv_sem.at[o_core + core], partner)
    c_copy.start()
    s_core[core] = x_ref[pl.ds(mine, half), :]
    _remote(s_core.at[1 - core], s_core.at[1 - core], send_sem.at[o_core],
            recv_sem.at[o_core + 1 - core], partner).wait_recv()
    c_copy.wait_send()
    s_core[core] = s_core[0] + s_core[1]

    copies = []
    for d in range(1, nx):
        p = (x + d) % nx
        cp = _remote(s_core.at[core, pl.ds(pl.multiple_of(p * chunk, chunk), chunk)], s_x.at[x],
                     send_sem.at[o_x + p], recv_sem.at[o_x + x], x_dev(p))
        cp.start()
        copies.append(cp)
    s_x[x] = s_core[core, pl.ds(pl.multiple_of(x * chunk, chunk), chunk), :]
    for d in range(1, nx):
        j = (x + d) % nx
        _remote(s_x.at[j], s_x.at[j], send_sem.at[o_x + j], recv_sem.at[o_x + j], x_dev(j)).wait_recv()
    for cp in copies:
        cp.wait_send()
    acc = s_x[0]
    for k in range(1, nx):
        acc = acc + s_x[k]

    for n, pos, dev, slots, off in ((nz, z, z_dev, s_z, o_z), (ny, s, y_dev, s_y, o_y)):
        slots[pos] = acc
        copies = []
        for d in range(1, n):
            p = (pos + d) % n
            cp = _remote(slots.at[pos], slots.at[pos], send_sem.at[off + p], recv_sem.at[off + pos], dev(p))
            cp.start()
            copies.append(cp)
        for d in range(1, n):
            j = (pos + d) % n
            _remote(slots.at[j], slots.at[j], send_sem.at[off + j], recv_sem.at[off + j], dev(j)).wait_recv()
        for cp in copies:
            cp.wait_send()
        acc = slots[0]
        for k in range(1, n):
            acc = acc + slots[k]

    row = lambda p: pl.multiple_of(core * half + p * chunk, chunk)
    res[pl.ds(row(x), chunk), :] = acc
    copies = []
    for d in range(1, nx):
        p = (x + d) % nx
        cp = _remote(res.at[pl.ds(row(x), chunk)], res.at[pl.ds(row(x), chunk)],
                     send_sem.at[o_gx + p], recv_sem.at[o_gx + x], x_dev(p))
        cp.start()
        copies.append(cp)
    for d in range(1, nx):
        j = (x + d) % nx
        _remote(res.at[pl.ds(row(j), chunk)], res.at[pl.ds(row(j), chunk)],
                send_sem.at[o_gx + j], recv_sem.at[o_gx + j], x_dev(j)).wait_recv()
    for cp in copies:
        cp.wait_send()

    cp = _remote(res.at[pl.ds(mine, half)], res.at[pl.ds(mine, half)],
                 send_sem.at[o_gc], recv_sem.at[o_gc + core], partner)
    cp.start()
    _remote(res.at[pl.ds(theirs, half)], res.at[pl.ds(theirs, half)],
            send_sem.at[o_gc], recv_sem.at[o_gc + 1 - core], partner).wait_recv()
    cp.wait_send()
    o_ref[...] = res[...] if scale == 1.0 else res[...] * scale


def make_allreduce(dims, cid, scale=1.0):
    nx, nz, ny = dims
    total = 2 + nx + nz + ny + nx + 2

    def allreduce(partial_value):
        rows, cols = partial_value.shape
        half = rows // 2
        chunk = half // nx
        return pl.pallas_call(
            functools.partial(_allreduce_kernel, dims, scale),
            out_shape=jax.ShapeDtypeStruct(partial_value.shape, jnp.float32),
            in_specs=[pl.BlockSpec(memory_space=pltpu.VMEM)],
            out_specs=pl.BlockSpec(memory_space=pltpu.VMEM),
            scratch_shapes=[
                pltpu.VMEM((2, half, cols), jnp.float32),
                pltpu.VMEM((nx, chunk, cols), jnp.float32),
                pltpu.VMEM((nz, chunk, cols), jnp.float32),
                pltpu.VMEM((ny, chunk, cols), jnp.float32),
                pltpu.VMEM((rows, cols), jnp.float32),
                pltpu.SemaphoreType.DMA((total,)),
                pltpu.SemaphoreType.DMA((total,)),
            ],
            compiler_params=pltpu.CompilerParams(collective_id=cid, has_side_effects=True),
        )(partial_value)

    return allreduce


def _chol_kernel(count, g_ref, *refs):
    if len(refs) == 4:
        prev_ref, lt_ref, w_ref, f_ref = refs
    else:
        prev_ref, f_ref = None, None
        lt_ref, w_ref = refs
    n = g_ref.shape[0]
    g = g_ref[...] / count
    a = (g + g.T) / 2
    sub = lax.broadcasted_iota(jnp.int32, (n, n), 0)
    lane = lax.broadcasted_iota(jnp.int32, (n, n), 1)
    w = jnp.where(sub == lane, 1.0, 0.0).astype(jnp.float32)
    lane_row = lax.broadcasted_iota(jnp.int32, (1, n), 1)
    lt_rows = []
    w_rows = []
    for k in range(n):
        r0 = k // 8 * 8
        row = a[k - r0:k - r0 + 1, :]
        colb = jnp.broadcast_to(a[:, k:k + 1], a.shape)
        recip = lax.rsqrt(colb[k - r0:k - r0 + 1, :])
        lrow = jnp.where(lane_row >= k, row * recip, 0.0)
        wrow = w[k - r0:k - r0 + 1, :] * recip
        lt_rows.append(lrow)
        w_rows.append(wrow)
        if k % 8 == 7:
            lt_ref[r0:r0 + 8, :] = jnp.concatenate(lt_rows, axis=0)
            w_ref[r0:r0 + 8, :] = jnp.concatenate(w_rows, axis=0)
            lt_rows, w_rows = [], []
        if k + 1 < n:
            r1 = (k + 1) // 8 * 8
            if r1 > r0:
                a = a[r1 - r0:]
                w = w[r1 - r0:]
                colb = colb[r1 - r0:]
            idx = lax.broadcasted_iota(jnp.int32, (n - r1, 1), 0) + r1
            m = jnp.where(idx > k, colb * recip, 0.0)
            a = a - m * lrow
            w = w - m * wrow
    if f_ref is not None:
        f_ref[...] = jnp.dot(lt_ref[...], prev_ref[...], precision=lax.Precision.HIGHEST,
                             preferred_element_type=jnp.float32)


def chol_inv(g, count, prev=None):
    n = g.shape[0]
    square = jax.ShapeDtypeStruct((n, n), jnp.float32)
    vmem = pl.BlockSpec(memory_space=pltpu.VMEM)
    outs = 2 if prev is None else 3
    return pl.pallas_call(
        functools.partial(_chol_kernel, float(count)),
        out_shape=(square,) * outs,
        in_specs=[vmem] * (1 if prev is None else 2),
        out_specs=(vmem,) * outs,
    )(g, *(() if prev is None else (prev,)))


def _jac_kernel(nbulk, cols_hbm, modes_ref, jac_ref, out_ref, ext, cols_ref, cols_sem, send_sem, recv_sem):
    cols_copy = pltpu.make_async_copy(cols_hbm, cols_ref, cols_sem)
    cols_copy.start()
    b = lax.axis_index("bulk")
    s = lax.axis_index("span")
    rb = modes_ref.shape[0]
    has_left = b > 0
    has_right = b < nbulk - 1
    barrier = pltpu.get_barrier_semaphore()

    @pl.when(has_left)
    def _():
        pl.semaphore_signal(barrier, inc=1, device_id=(b - 1, s), device_id_type=MESH)

    @pl.when(has_right)
    def _():
        pl.semaphore_signal(barrier, inc=1, device_id=(b + 1, s), device_id_type=MESH)

    pl.semaphore_wait(barrier, has_left.astype(jnp.int32) + has_right.astype(jnp.int32))

    to_left = pltpu.make_async_remote_copy(
        src_ref=modes_ref, dst_ref=ext.at[pl.ds(2 * rb, rb)], send_sem=send_sem.at[0],
        recv_sem=recv_sem.at[1], device_id=(b - 1, s), device_id_type=MESH)
    to_right = pltpu.make_async_remote_copy(
        src_ref=modes_ref, dst_ref=ext.at[pl.ds(0, rb)], send_sem=send_sem.at[1],
        recv_sem=recv_sem.at[0], device_id=(b + 1, s), device_id_type=MESH)

    @pl.when(has_left)
    def _():
        to_left.start()

    @pl.when(has_right)
    def _():
        to_right.start()

    ext[pl.ds(rb, rb)] = modes_ref[...]

    @pl.when(jnp.logical_not(has_left))
    def _():
        ext[pl.ds(0, rb)] = jnp.zeros(modes_ref.shape, modes_ref.dtype)

    @pl.when(jnp.logical_not(has_right))
    def _():
        ext[pl.ds(2 * rb, rb)] = jnp.zeros(modes_ref.shape, modes_ref.dtype)

    @pl.when(has_left)
    def _():
        to_right.wait_recv()
        to_left.wait_send()

    @pl.when(has_right)
    def _():
        to_left.wait_recv()
        to_right.wait_send()

    cols_copy.wait()
    start = (s * nbulk + b) * rb - rb

    def row(r, carry):
        acc = None
        for n in range(jac_ref.shape[1]):
            idx = jnp.clip(cols_ref[n, r] - start, 0, 3 * rb - 1)
            term = jnp.dot(jac_ref[r, n], ext[idx], preferred_element_type=jnp.float32)
            acc = term if acc is None else acc + term
        out_ref[r] = acc.astype(out_ref.dtype)
        return carry

    lax.fori_loop(0, rb, row, 0)


def jac_apply(nbulk, cid, jac_cols, modes_b, jac_blocks):
    rb, nb, blk, width = jac_blocks.shape[0], jac_blocks.shape[1], jac_blocks.shape[2], modes_b.shape[1]
    modes_blocks = modes_b.reshape(rb, blk, width)
    out = pl.pallas_call(
        functools.partial(_jac_kernel, nbulk),
        out_shape=jax.ShapeDtypeStruct((rb, blk, width), jnp.bfloat16),
        in_specs=[pl.BlockSpec(memory_space=pl.ANY),
                  pl.BlockSpec(memory_space=pltpu.VMEM),
                  pl.BlockSpec(memory_space=pltpu.VMEM)],
        out_specs=pl.BlockSpec(memory_space=pltpu.VMEM),
        scratch_shapes=[
            pltpu.VMEM((3 * rb, blk, width), jnp.bfloat16),
            pltpu.SMEM(jac_cols.shape[::-1], jnp.int32),
            pltpu.SemaphoreType.DMA(()),
            pltpu.SemaphoreType.DMA((2,)),
            pltpu.SemaphoreType.DMA((2,)),
        ],
        compiler_params=pltpu.CompilerParams(collective_id=cid, has_side_effects=True),
    )(jac_cols.T, modes_blocks, jac_blocks)
    return out.reshape(rb * blk, width)


def cholesky_step(data, row_count, allreduce, prev=None):
    high = lax.Precision.HIGHEST
    partial_value = lax.dot_general(
        data, data, (((0,), (0,)), ((), ())), precision=high, preferred_element_type=jnp.float32
    )
    outs = chol_inv(allreduce(partial_value), row_count, prev)
    result = lax.dot_general(
        data, outs[1], (((1,), (1,)), ((), ())), precision=high, preferred_element_type=jnp.float32
    )
    return (result, outs[0] if prev is None else outs[2])


def shards(dims, snapshots, jac_blocks, jac_cols):
    high = lax.Precision.HIGHEST
    local_rows, width = snapshots.shape
    block_rows = jac_cols.shape[0]
    blk = jac_blocks.shape[2]
    row_count = local_rows * lax.axis_size(("bulk", "span"))
    first, upper1 = cholesky_step(snapshots, row_count, make_allreduce(dims, 0))
    modes, factor = cholesky_step(first, row_count, make_allreduce(dims, 1), upper1)
    modes_b = modes.astype(jnp.bfloat16)
    jac_modes = jac_apply(lax.axis_size("bulk"), 3, jac_cols, modes_b, jac_blocks)
    partial_value = lax.dot_general(
        modes,
        jac_modes.astype(jnp.float32),
        (((0,), (0,)), ((), ())),
        precision=high,
        preferred_element_type=jnp.float32,
    )
    reduced = make_allreduce(dims, 2, 1.0 / row_count)(partial_value)
    return (modes, factor, jac_modes, reduced)


def _torus_dims(mesh):
    coords = [d.coords for d in mesh.devices.flat]
    return tuple(len({c[i] for c in coords}) for i in (0, 2, 1))


def solution(mesh):
    nx, nz, ny = _torus_dims(mesh)
    assert mesh.shape["bulk"] == 2 * nx * nz and mesh.shape["span"] == ny
    return jax.shard_map(
        functools.partial(shards, (nx, nz, ny)),
        mesh=mesh,
        in_specs=(
            P(("span", "bulk"), None),
            P(("span", "bulk"), None, None, None),
            P(("span", "bulk"), None),
        ),
        out_specs=(P(("span", "bulk"), None), P(), P(("span", "bulk"), None), P()),
        check_vma=False,
    )
```

```python
import functools

import jax
import jax.numpy as jnp
from jax import lax
from jax.experimental import pallas as pl
from jax.experimental.pallas import tpu as pltpu
from jax.sharding import PartitionSpec as P

MESH = pl.DeviceIdType.MESH


def _coords(nx, nz):
    b = lax.axis_index("bulk")
    s = lax.axis_index("span")
    core = b % 2
    z = (b // 2) % nz
    x = b // (2 * nz)
    return b, s, core, x, z


def _remote(src, dst, send_sem, recv_sem, device):
    return pltpu.make_async_remote_copy(
        src_ref=src, dst_ref=dst, send_sem=send_sem, recv_sem=recv_sem,
        device_id=device, device_id_type=MESH,
    )


def _allreduce_kernel(dims, scale, x_ref, o_ref, s_core, s_x, s_z, s_y, res, send_sem, recv_sem):
    nx, nz, ny = dims
    b, s, core, x, z = _coords(nx, nz)
    rows = x_ref.shape[0]
    half = rows // 2
    chunk = half // nx
    partner = (b + 1 - 2 * core, s)
    x_dev = lambda p: ((p * nz + z) * 2 + core, s)
    z_dev = lambda p: ((x * nz + p) * 2 + core, s)
    y_dev = lambda p: (b, p)
    o_core, o_x, o_z, o_y = 0, 2, 2 + nx, 2 + nx + nz
    o_gx = o_y + ny
    o_gc = o_gx + nx

    barrier = pltpu.get_barrier_semaphore()
    peers = [partner]
    for n, pos, dev in ((nx, x, x_dev), (nz, z, z_dev), (ny, s, y_dev)):
        peers += [dev((pos + d) % n) for d in range(1, n)]
    for peer in peers:
        pl.semaphore_signal(barrier, inc=1, device_id=peer, device_id_type=MESH)
    pl.semaphore_wait(barrier, len(peers))

    mine = pl.multiple_of(core * half, half)
    theirs = pl.multiple_of((1 - core) * half, half)
    c_copy = _remote(x_ref.at[pl.ds(theirs, half)], s_core.at[core],
                     send_sem.at[o_core], recv_sem.at[o_core + core], partner)
    c_copy.start()
    s_core[core] = x_ref[pl.ds(mine, half), :]
    _remote(s_core.at[1 - core], s_core.at[1 - core], send_sem.at[o_core],
            recv_sem.at[o_core + 1 - core], partner).wait_recv()
    c_copy.wait_send()
    s_core[core] = s_core[0] + s_core[1]

    copies = []
    for d in range(1, nx):
        p = (x + d) % nx
        cp = _remote(s_core.at[core, pl.ds(pl.multiple_of(p * chunk, chunk), chunk)], s_x.at[x],
                     send_sem.at[o_x + p], recv_sem.at[o_x + x], x_dev(p))
        cp.start()
        copies.append(cp)
    s_x[x] = s_core[core, pl.ds(pl.multiple_of(x * chunk, chunk), chunk), :]
    for d in range(1, nx):
        j = (x + d) % nx
        _remote(s_x.at[j], s_x.at[j], send_sem.at[o_x + j], recv_sem.at[o_x + j], x_dev(j)).wait_recv()
    for cp in copies:
        cp.wait_send()
    acc = s_x[0]
    for k in range(1, nx):
        acc = acc + s_x[k]

    for n, pos, dev, slots, off in ((nz, z, z_dev, s_z, o_z), (ny, s, y_dev, s_y, o_y)):
        slots[pos] = acc
        copies = []
        for d in range(1, n):
            p = (pos + d) % n
            cp = _remote(slots.at[pos], slots.at[pos], send_sem.at[off + p], recv_sem.at[off + pos], dev(p))
            cp.start()
            copies.append(cp)
        for d in range(1, n):
            j = (pos + d) % n
            _remote(slots.at[j], slots.at[j], send_sem.at[off + j], recv_sem.at[off + j], dev(j)).wait_recv()
        for cp in copies:
            cp.wait_send()
        acc = slots[0]
        for k in range(1, n):
            acc = acc + slots[k]

    row = lambda p: pl.multiple_of(core * half + p * chunk, chunk)
    res[pl.ds(row(x), chunk), :] = acc
    copies = []
    for d in range(1, nx):
        p = (x + d) % nx
        cp = _remote(res.at[pl.ds(row(x), chunk)], res.at[pl.ds(row(x), chunk)],
                     send_sem.at[o_gx + p], recv_sem.at[o_gx + x], x_dev(p))
        cp.start()
        copies.append(cp)
    for d in range(1, nx):
        j = (x + d) % nx
        _remote(res.at[pl.ds(row(j), chunk)], res.at[pl.ds(row(j), chunk)],
                send_sem.at[o_gx + j], recv_sem.at[o_gx + j], x_dev(j)).wait_recv()
    for cp in copies:
        cp.wait_send()

    cp = _remote(res.at[pl.ds(mine, half)], res.at[pl.ds(mine, half)],
                 send_sem.at[o_gc], recv_sem.at[o_gc + core], partner)
    cp.start()
    _remote(res.at[pl.ds(theirs, half)], res.at[pl.ds(theirs, half)],
            send_sem.at[o_gc], recv_sem.at[o_gc + 1 - core], partner).wait_recv()
    cp.wait_send()
    o_ref[...] = res[...] if scale == 1.0 else res[...] * scale


def make_allreduce(dims, cid, scale=1.0):
    nx, nz, ny = dims
    total = 2 + nx + nz + ny + nx + 2

    def allreduce(partial_value):
        rows, cols = partial_value.shape
        half = rows // 2
        chunk = half // nx
        return pl.pallas_call(
            functools.partial(_allreduce_kernel, dims, scale),
            out_shape=jax.ShapeDtypeStruct(partial_value.shape, jnp.float32),
            in_specs=[pl.BlockSpec(memory_space=pltpu.VMEM)],
            out_specs=pl.BlockSpec(memory_space=pltpu.VMEM),
            scratch_shapes=[
                pltpu.VMEM((2, half, cols), jnp.float32),
                pltpu.VMEM((nx, chunk, cols), jnp.float32),
                pltpu.VMEM((nz, chunk, cols), jnp.float32),
                pltpu.VMEM((ny, chunk, cols), jnp.float32),
                pltpu.VMEM((rows, cols), jnp.float32),
                pltpu.SemaphoreType.DMA((total,)),
                pltpu.SemaphoreType.DMA((total,)),
            ],
            compiler_params=pltpu.CompilerParams(collective_id=cid, has_side_effects=True),
        )(partial_value)

    return allreduce


def _chol_kernel(count, g_ref, *refs):
    if len(refs) == 4:
        prev_ref, lt_ref, w_ref, f_ref = refs
    else:
        prev_ref, f_ref = None, None
        lt_ref, w_ref = refs
    n = g_ref.shape[0]
    g = g_ref[...] / count
    a = (g + g.T) / 2
    sub = lax.broadcasted_iota(jnp.int32, (n, n), 0)
    lane = lax.broadcasted_iota(jnp.int32, (n, n), 1)
    w = jnp.where(sub == lane, 1.0, 0.0).astype(jnp.float32)
    lane_row = lax.broadcasted_iota(jnp.int32, (1, n), 1)
    lt_rows = []
    w_rows = []
    for k in range(n):
        r0 = k // 8 * 8
        row = a[k - r0:k - r0 + 1, :]
        colb = jnp.broadcast_to(a[:, k:k + 1], a.shape)
        recip = lax.rsqrt(colb[k - r0:k - r0 + 1, :])
        lrow = jnp.where(lane_row >= k, row * recip, 0.0)
        wrow = w[k - r0:k - r0 + 1, :] * recip
        lt_rows.append(lrow)
        w_rows.append(wrow)
        if k % 8 == 7:
            lt_ref[r0:r0 + 8, :] = jnp.concatenate(lt_rows, axis=0)
            w_ref[r0:r0 + 8, :] = jnp.concatenate(w_rows, axis=0)
            lt_rows, w_rows = [], []
        if k + 1 < n:
            r1 = (k + 1) // 8 * 8
            if r1 > r0:
                a = a[r1 - r0:]
                w = w[r1 - r0:]
                colb = colb[r1 - r0:]
            idx = lax.broadcasted_iota(jnp.int32, (n - r1, 1), 0) + r1
            m = jnp.where(idx > k, colb * recip, 0.0)
            a = a - m * lrow
            w = w - m * wrow
    if f_ref is not None:
        f_ref[...] = jnp.dot(lt_ref[...], prev_ref[...], precision=lax.Precision.HIGHEST,
                             preferred_element_type=jnp.float32)


def chol_inv(g, count, prev=None):
    n = g.shape[0]
    square = jax.ShapeDtypeStruct((n, n), jnp.float32)
    vmem = pl.BlockSpec(memory_space=pltpu.VMEM)
    outs = 2 if prev is None else 3
    return pl.pallas_call(
        functools.partial(_chol_kernel, float(count)),
        out_shape=(square,) * outs,
        in_specs=[vmem] * (1 if prev is None else 2),
        out_specs=(vmem,) * outs,
    )(g, *(() if prev is None else (prev,)))


def _jac_kernel(nbulk, cols_hbm, modes_ref, jac_ref, out_ref, ext, cols_ref, cols_sem, send_sem, recv_sem):
    cols_copy = pltpu.make_async_copy(cols_hbm, cols_ref, cols_sem)
    cols_copy.start()
    b = lax.axis_index("bulk")
    s = lax.axis_index("span")
    rb = modes_ref.shape[0]
    has_left = b > 0
    has_right = b < nbulk - 1
    barrier = pltpu.get_barrier_semaphore()

    @pl.when(has_left)
    def _():
        pl.semaphore_signal(barrier, inc=1, device_id=(b - 1, s), device_id_type=MESH)

    @pl.when(has_right)
    def _():
        pl.semaphore_signal(barrier, inc=1, device_id=(b + 1, s), device_id_type=MESH)

    pl.semaphore_wait(barrier, has_left.astype(jnp.int32) + has_right.astype(jnp.int32))

    to_left = pltpu.make_async_remote_copy(
        src_ref=modes_ref, dst_ref=ext.at[pl.ds(2 * rb, rb)], send_sem=send_sem.at[0],
        recv_sem=recv_sem.at[1], device_id=(b - 1, s), device_id_type=MESH)
    to_right = pltpu.make_async_remote_copy(
        src_ref=modes_ref, dst_ref=ext.at[pl.ds(0, rb)], send_sem=send_sem.at[1],
        recv_sem=recv_sem.at[0], device_id=(b + 1, s), device_id_type=MESH)

    @pl.when(has_left)
    def _():
        to_left.start()

    @pl.when(has_right)
    def _():
        to_right.start()

    ext[pl.ds(rb, rb)] = modes_ref[...]

    @pl.when(jnp.logical_not(has_left))
    def _():
        ext[pl.ds(0, rb)] = jnp.zeros(modes_ref.shape, modes_ref.dtype)

    @pl.when(jnp.logical_not(has_right))
    def _():
        ext[pl.ds(2 * rb, rb)] = jnp.zeros(modes_ref.shape, modes_ref.dtype)

    @pl.when(has_left)
    def _():
        to_right.wait_recv()
        to_left.wait_send()

    @pl.when(has_right)
    def _():
        to_left.wait_recv()
        to_right.wait_send()

    cols_copy.wait()
    start = (s * nbulk + b) * rb - rb

    def row(r, carry):
        acc = None
        for n in range(jac_ref.shape[1]):
            idx = jnp.clip(cols_ref[n, r] - start, 0, 3 * rb - 1)
            term = jnp.dot(jac_ref[r, n], ext[idx], preferred_element_type=jnp.float32)
            acc = term if acc is None else acc + term
        out_ref[r] = acc.astype(out_ref.dtype)
        return carry

    lax.fori_loop(0, rb, row, 0)


def jac_apply(nbulk, cid, jac_cols, modes_b, jac_blocks):
    rb, nb, blk, width = jac_blocks.shape[0], jac_blocks.shape[1], jac_blocks.shape[2], modes_b.shape[1]
    modes_blocks = modes_b.reshape(rb, blk, width)
    out = pl.pallas_call(
        functools.partial(_jac_kernel, nbulk),
        out_shape=jax.ShapeDtypeStruct((rb, blk, width), jnp.bfloat16),
        in_specs=[pl.BlockSpec(memory_space=pl.ANY),
                  pl.BlockSpec(memory_space=pltpu.VMEM),
                  pl.BlockSpec(memory_space=pltpu.VMEM)],
        out_specs=pl.BlockSpec(memory_space=pltpu.VMEM),
        scratch_shapes=[
            pltpu.VMEM((3 * rb, blk, width), jnp.bfloat16),
            pltpu.SMEM(jac_cols.shape[::-1], jnp.int32),
            pltpu.SemaphoreType.DMA(()),
            pltpu.SemaphoreType.DMA((2,)),
            pltpu.SemaphoreType.DMA((2,)),
        ],
        compiler_params=pltpu.CompilerParams(collective_id=cid, has_side_effects=True),
    )(jac_cols.T, modes_blocks, jac_blocks)
    return out.reshape(rb * blk, width)


def cholesky_step(data, row_count, allreduce, prev=None):
    high = lax.Precision.HIGHEST
    partial_value = lax.dot_general(
        data, data, (((0,), (0,)), ((), ())), precision=high, preferred_element_type=jnp.float32
    )
    outs = chol_inv(allreduce(partial_value), row_count, prev)
    result = lax.dot_general(
        data, outs[1], (((1,), (1,)), ((), ())), precision=high, preferred_element_type=jnp.float32
    )
    return (result, outs[0] if prev is None else outs[2])


def shards(dims, snapshots, jac_blocks, jac_cols):
    high = lax.Precision.HIGHEST
    local_rows, width = snapshots.shape
    block_rows = jac_cols.shape[0]
    blk = jac_blocks.shape[2]
    row_count = local_rows * lax.axis_size(("bulk", "span"))
    first, upper1 = cholesky_step(snapshots, row_count, make_allreduce(dims, 0))
    modes, factor = cholesky_step(first, row_count, make_allreduce(dims, 1), upper1)
    modes_b = modes.astype(jnp.bfloat16)
    jac_modes = jac_apply(lax.axis_size("bulk"), 3, jac_cols, modes_b, jac_blocks)
    pieces = [modes_b]
    rest = modes - lax.reduce_precision(modes, exponent_bits=8, mantissa_bits=7)
    for _ in range(2):
        pieces.append(rest.astype(jnp.bfloat16))
        rest = rest - lax.reduce_precision(rest, exponent_bits=8, mantissa_bits=7)
    partial_value = None
    for piece in pieces:
        term = lax.dot_general(
            piece, jac_modes, (((0,), (0,)), ((), ())), preferred_element_type=jnp.float32
        )
        partial_value = term if partial_value is None else partial_value + term
    reduced = make_allreduce(dims, 2, 1.0 / row_count)(partial_value)
    return (modes, factor, jac_modes, reduced)


def _torus_dims(mesh):
    coords = [d.coords for d in mesh.devices.flat]
    return tuple(len({c[i] for c in coords}) for i in (0, 2, 1))


def solution(mesh):
    nx, nz, ny = _torus_dims(mesh)
    assert mesh.shape["bulk"] == 2 * nx * nz and mesh.shape["span"] == ny
    return jax.shard_map(
        functools.partial(shards, (nx, nz, ny)),
        mesh=mesh,
        in_specs=(
            P(("span", "bulk"), None),
            P(("span", "bulk"), None, None, None),
            P(("span", "bulk"), None),
        ),
        out_specs=(P(("span", "bulk"), None), P(), P(("span", "bulk"), None), P()),
        check_vma=False,
    )
```

```python
import functools

import jax
import jax.numpy as jnp
from jax import lax
from jax.experimental import pallas as pl
from jax.experimental.pallas import tpu as pltpu
from jax.sharding import PartitionSpec as P

MESH = pl.DeviceIdType.MESH


def _coords(nx, nz):
    b = lax.axis_index("bulk")
    s = lax.axis_index("span")
    core = b % 2
    z = (b // 2) % nz
    x = b // (2 * nz)
    return b, s, core, x, z


def _remote(src, dst, send_sem, recv_sem, device):
    return pltpu.make_async_remote_copy(
        src_ref=src, dst_ref=dst, send_sem=send_sem, recv_sem=recv_sem,
        device_id=device, device_id_type=MESH,
    )


def _allreduce_kernel(dims, scale, x_ref, o_ref, s_core, s_x, s_z, s_y, res, send_sem, recv_sem):
    nx, nz, ny = dims
    b, s, core, x, z = _coords(nx, nz)
    rows = x_ref.shape[0]
    half = rows // 2
    chunk = half // nx
    partner = (b + 1 - 2 * core, s)
    x_dev = lambda p: ((p * nz + z) * 2 + core, s)
    z_dev = lambda p: ((x * nz + p) * 2 + core, s)
    y_dev = lambda p: (b, p)
    o_core, o_x, o_z, o_y = 0, 2, 2 + nx, 2 + nx + nz
    o_gx = o_y + ny
    o_gc = o_gx + nx

    barrier = pltpu.get_barrier_semaphore()
    peers = [partner]
    for n, pos, dev in ((nx, x, x_dev), (nz, z, z_dev), (ny, s, y_dev)):
        peers += [dev((pos + d) % n) for d in range(1, n)]
    for peer in peers:
        pl.semaphore_signal(barrier, inc=1, device_id=peer, device_id_type=MESH)
    pl.semaphore_wait(barrier, len(peers))

    mine = pl.multiple_of(core * half, half)
    theirs = pl.multiple_of((1 - core) * half, half)
    c_copy = _remote(x_ref.at[pl.ds(theirs, half)], s_core.at[core],
                     send_sem.at[o_core], recv_sem.at[o_core + core], partner)
    c_copy.start()
    s_core[core] = x_ref[pl.ds(mine, half), :]
    _remote(s_core.at[1 - core], s_core.at[1 - core], send_sem.at[o_core],
            recv_sem.at[o_core + 1 - core], partner).wait_recv()
    c_copy.wait_send()
    s_core[core] = s_core[0] + s_core[1]

    copies = []
    for d in range(1, nx):
        p = (x + d) % nx
        cp = _remote(s_core.at[core, pl.ds(pl.multiple_of(p * chunk, chunk), chunk)], s_x.at[x],
                     send_sem.at[o_x + p], recv_sem.at[o_x + x], x_dev(p))
        cp.start()
        copies.append(cp)
    s_x[x] = s_core[core, pl.ds(pl.multiple_of(x * chunk, chunk), chunk), :]
    for d in range(1, nx):
        j = (x + d) % nx
        _remote(s_x.at[j], s_x.at[j], send_sem.at[o_x + j], recv_sem.at[o_x + j], x_dev(j)).wait_recv()
    for cp in copies:
        cp.wait_send()
    acc = s_x[0]
    for k in range(1, nx):
        acc = acc + s_x[k]

    for n, pos, dev, slots, off in ((nz, z, z_dev, s_z, o_z), (ny, s, y_dev, s_y, o_y)):
        slots[pos] = acc
        copies = []
        for d in range(1, n):
            p = (pos + d) % n
            cp = _remote(slots.at[pos], slots.at[pos], send_sem.at[off + p], recv_sem.at[off + pos], dev(p))
            cp.start()
            copies.append(cp)
        for d in range(1, n):
            j = (pos + d) % n
            _remote(slots.at[j], slots.at[j], send_sem.at[off + j], recv_sem.at[off + j], dev(j)).wait_recv()
        for cp in copies:
            cp.wait_send()
        acc = slots[0]
        for k in range(1, n):
            acc = acc + slots[k]

    row = lambda p: pl.multiple_of(core * half + p * chunk, chunk)
    res[pl.ds(row(x), chunk), :] = acc
    copies = []
    for d in range(1, nx):
        p = (x + d) % nx
        cp = _remote(res.at[pl.ds(row(x), chunk)], res.at[pl.ds(row(x), chunk)],
                     send_sem.at[o_gx + p], recv_sem.at[o_gx + x], x_dev(p))
        cp.start()
        copies.append(cp)
    for d in range(1, nx):
        j = (x + d) % nx
        _remote(res.at[pl.ds(row(j), chunk)], res.at[pl.ds(row(j), chunk)],
                send_sem.at[o_gx + j], recv_sem.at[o_gx + j], x_dev(j)).wait_recv()
    for cp in copies:
        cp.wait_send()

    cp = _remote(res.at[pl.ds(mine, half)], res.at[pl.ds(mine, half)],
                 send_sem.at[o_gc], recv_sem.at[o_gc + core], partner)
    cp.start()
    _remote(res.at[pl.ds(theirs, half)], res.at[pl.ds(theirs, half)],
            send_sem.at[o_gc], recv_sem.at[o_gc + 1 - core], partner).wait_recv()
    cp.wait_send()
    o_ref[...] = res[...] if scale == 1.0 else res[...] * scale


def make_allreduce(dims, cid, scale=1.0):
    nx, nz, ny = dims
    total = 2 + nx + nz + ny + nx + 2

    def allreduce(partial_value):
        rows, cols = partial_value.shape
        half = rows // 2
        chunk = half // nx
        return pl.pallas_call(
            functools.partial(_allreduce_kernel, dims, scale),
            out_shape=jax.ShapeDtypeStruct(partial_value.shape, jnp.float32),
            in_specs=[pl.BlockSpec(memory_space=pltpu.VMEM)],
            out_specs=pl.BlockSpec(memory_space=pltpu.VMEM),
            scratch_shapes=[
                pltpu.VMEM((2, half, cols), jnp.float32),
                pltpu.VMEM((nx, chunk, cols), jnp.float32),
                pltpu.VMEM((nz, chunk, cols), jnp.float32),
                pltpu.VMEM((ny, chunk, cols), jnp.float32),
                pltpu.VMEM((rows, cols), jnp.float32),
                pltpu.SemaphoreType.DMA((total,)),
                pltpu.SemaphoreType.DMA((total,)),
            ],
            compiler_params=pltpu.CompilerParams(collective_id=cid, has_side_effects=True),
        )(partial_value)

    return allreduce


def _chol_kernel(count, g_ref, *refs):
    if len(refs) == 4:
        prev_ref, lt_ref, w_ref, f_ref = refs
    else:
        prev_ref, f_ref = None, None
        lt_ref, w_ref = refs
    n = g_ref.shape[0]
    g = g_ref[...] / count
    a = (g + g.T) / 2
    sub = lax.broadcasted_iota(jnp.int32, (n, n), 0)
    lane = lax.broadcasted_iota(jnp.int32, (n, n), 1)
    w = jnp.where(sub == lane, 1.0, 0.0).astype(jnp.float32)
    lane_row = lax.broadcasted_iota(jnp.int32, (1, n), 1)
    lt_rows = []
    w_rows = []
    for k in range(n):
        r0 = k // 8 * 8
        row = a[k - r0:k - r0 + 1, :]
        colb = jnp.broadcast_to(a[:, k:k + 1], a.shape)
        recip = lax.rsqrt(colb[k - r0:k - r0 + 1, :])
        lrow = jnp.where(lane_row >= k, row * recip, 0.0)
        wrow = w[k - r0:k - r0 + 1, :] * recip
        lt_rows.append(lrow)
        w_rows.append(wrow)
        if k % 8 == 7:
            lt_ref[r0:r0 + 8, :] = jnp.concatenate(lt_rows, axis=0)
            w_ref[r0:r0 + 8, :] = jnp.concatenate(w_rows, axis=0)
            lt_rows, w_rows = [], []
        if k + 1 < n:
            r1 = (k + 1) // 8 * 8
            if r1 > r0:
                a = a[r1 - r0:]
                w = w[r1 - r0:]
                colb = colb[r1 - r0:]
            idx = lax.broadcasted_iota(jnp.int32, (n - r1, 1), 0) + r1
            m = jnp.where(idx > k, colb * recip, 0.0)
            a = a - m * lrow
            w = w - m * wrow
    if f_ref is not None:
        f_ref[...] = jnp.dot(lt_ref[...], prev_ref[...], precision=lax.Precision.HIGHEST,
                             preferred_element_type=jnp.float32)


def chol_inv(g, count, prev=None):
    n = g.shape[0]
    square = jax.ShapeDtypeStruct((n, n), jnp.float32)
    vmem = pl.BlockSpec(memory_space=pltpu.VMEM)
    outs = 2 if prev is None else 3
    return pl.pallas_call(
        functools.partial(_chol_kernel, float(count)),
        out_shape=(square,) * outs,
        in_specs=[vmem] * (1 if prev is None else 2),
        out_specs=(vmem,) * outs,
    )(g, *(() if prev is None else (prev,)))


def _jac_kernel(nbulk, cols_hbm, modes_ref, jac_ref, out_ref, ext, cols_ref, cols_sem, send_sem, recv_sem):
    cols_copy = pltpu.make_async_copy(cols_hbm, cols_ref, cols_sem)
    cols_copy.start()
    b = lax.axis_index("bulk")
    s = lax.axis_index("span")
    rb = modes_ref.shape[0]
    has_left = b > 0
    has_right = b < nbulk - 1
    barrier = pltpu.get_barrier_semaphore()

    @pl.when(has_left)
    def _():
        pl.semaphore_signal(barrier, inc=1, device_id=(b - 1, s), device_id_type=MESH)

    @pl.when(has_right)
    def _():
        pl.semaphore_signal(barrier, inc=1, device_id=(b + 1, s), device_id_type=MESH)

    pl.semaphore_wait(barrier, has_left.astype(jnp.int32) + has_right.astype(jnp.int32))

    to_left = pltpu.make_async_remote_copy(
        src_ref=modes_ref, dst_ref=ext.at[pl.ds(2 * rb, rb)], send_sem=send_sem.at[0],
        recv_sem=recv_sem.at[1], device_id=(b - 1, s), device_id_type=MESH)
    to_right = pltpu.make_async_remote_copy(
        src_ref=modes_ref, dst_ref=ext.at[pl.ds(0, rb)], send_sem=send_sem.at[1],
        recv_sem=recv_sem.at[0], device_id=(b + 1, s), device_id_type=MESH)

    @pl.when(has_left)
    def _():
        to_left.start()

    @pl.when(has_right)
    def _():
        to_right.start()

    ext[pl.ds(rb, rb)] = modes_ref[...]

    @pl.when(jnp.logical_not(has_left))
    def _():
        ext[pl.ds(0, rb)] = jnp.zeros(modes_ref.shape, modes_ref.dtype)

    @pl.when(jnp.logical_not(has_right))
    def _():
        ext[pl.ds(2 * rb, rb)] = jnp.zeros(modes_ref.shape, modes_ref.dtype)

    @pl.when(has_left)
    def _():
        to_right.wait_recv()
        to_left.wait_send()

    @pl.when(has_right)
    def _():
        to_left.wait_recv()
        to_right.wait_send()

    cols_copy.wait()
    start = (s * nbulk + b) * rb - rb

    def row(r, carry):
        acc = None
        for n in range(jac_ref.shape[1]):
            idx = jnp.clip(cols_ref[n, r] - start, 0, 3 * rb - 1)
            term = jnp.dot(jac_ref[r, n], ext[idx], preferred_element_type=jnp.float32)
            acc = term if acc is None else acc + term
        out_ref[r] = acc.astype(out_ref.dtype)
        return carry

    lax.fori_loop(0, rb, row, 0)


def jac_apply(nbulk, cid, jac_cols, modes_b, jac_blocks):
    rb, nb, blk, width = jac_blocks.shape[0], jac_blocks.shape[1], jac_blocks.shape[2], modes_b.shape[1]
    modes_blocks = modes_b.reshape(rb, blk, width)
    out = pl.pallas_call(
        functools.partial(_jac_kernel, nbulk),
        out_shape=jax.ShapeDtypeStruct((rb, blk, width), jnp.bfloat16),
        in_specs=[pl.BlockSpec(memory_space=pl.ANY),
                  pl.BlockSpec(memory_space=pltpu.VMEM),
                  pl.BlockSpec(memory_space=pltpu.VMEM)],
        out_specs=pl.BlockSpec(memory_space=pltpu.VMEM),
        scratch_shapes=[
            pltpu.VMEM((3 * rb, blk, width), jnp.bfloat16),
            pltpu.SMEM(jac_cols.shape[::-1], jnp.int32),
            pltpu.SemaphoreType.DMA(()),
            pltpu.SemaphoreType.DMA((2,)),
            pltpu.SemaphoreType.DMA((2,)),
        ],
        compiler_params=pltpu.CompilerParams(collective_id=cid, has_side_effects=True),
    )(jac_cols.T, modes_blocks, jac_blocks)
    return out.reshape(rb * blk, width)


def cholesky_step(data, row_count, allreduce, prev=None):
    high = lax.Precision.HIGHEST
    partial_value = lax.dot_general(
        data, data, (((0,), (0,)), ((), ())), precision=high, preferred_element_type=jnp.float32
    )
    outs = chol_inv(allreduce(partial_value), row_count, prev)
    result = lax.dot_general(
        data, outs[1], (((1,), (1,)), ((), ())), precision=lax.Precision.HIGH,
        preferred_element_type=jnp.float32,
    )
    return (result, outs[0] if prev is None else outs[2])


def shards(dims, snapshots, jac_blocks, jac_cols):
    high = lax.Precision.HIGHEST
    local_rows, width = snapshots.shape
    block_rows = jac_cols.shape[0]
    blk = jac_blocks.shape[2]
    row_count = local_rows * lax.axis_size(("bulk", "span"))
    first, upper1 = cholesky_step(snapshots, row_count, make_allreduce(dims, 0))
    modes, factor = cholesky_step(first, row_count, make_allreduce(dims, 1), upper1)
    modes_b = modes.astype(jnp.bfloat16)
    jac_modes = jac_apply(lax.axis_size("bulk"), 3, jac_cols, modes_b, jac_blocks)
    partial_value = lax.dot_general(
        modes,
        jac_modes.astype(jnp.float32),
        (((0,), (0,)), ((), ())),
        precision=lax.Precision.HIGH,
        preferred_element_type=jnp.float32,
    )
    reduced = make_allreduce(dims, 2, 1.0 / row_count)(partial_value)
    return (modes, factor, jac_modes, reduced)


def _torus_dims(mesh):
    coords = [d.coords for d in mesh.devices.flat]
    return tuple(len({c[i] for c in coords}) for i in (0, 2, 1))


def solution(mesh):
    nx, nz, ny = _torus_dims(mesh)
    assert mesh.shape["bulk"] == 2 * nx * nz and mesh.shape["span"] == ny
    return jax.shard_map(
        functools.partial(shards, (nx, nz, ny)),
        mesh=mesh,
        in_specs=(
            P(("span", "bulk"), None),
            P(("span", "bulk"), None, None, None),
            P(("span", "bulk"), None),
        ),
        out_specs=(P(("span", "bulk"), None), P(), P(("span", "bulk"), None), P()),
        check_vma=False,
    )
```

```python
import functools

import jax
import jax.numpy as jnp
from jax import lax
from jax.experimental import pallas as pl
from jax.experimental.pallas import tpu as pltpu
from jax.sharding import PartitionSpec as P

MESH = pl.DeviceIdType.MESH


def _coords(nx, nz):
    b = lax.axis_index("bulk")
    s = lax.axis_index("span")
    core = b % 2
    z = (b // 2) % nz
    x = b // (2 * nz)
    return b, s, core, x, z


def _remote(src, dst, send_sem, recv_sem, device):
    return pltpu.make_async_remote_copy(
        src_ref=src, dst_ref=dst, send_sem=send_sem, recv_sem=recv_sem,
        device_id=device, device_id_type=MESH,
    )


def _allreduce_kernel(dims, scale, x_ref, o_ref, s_core, s_x, s_z, s_y, res, send_sem, recv_sem):
    nx, nz, ny = dims
    b, s, core, x, z = _coords(nx, nz)
    rows = x_ref.shape[0]
    half = rows // 2
    chunk = half // nx
    partner = (b + 1 - 2 * core, s)
    x_dev = lambda p: ((p * nz + z) * 2 + core, s)
    z_dev = lambda p: ((x * nz + p) * 2 + core, s)
    y_dev = lambda p: (b, p)
    o_core, o_x, o_z, o_y = 0, 2, 2 + nx, 2 + nx + nz
    o_gx = o_y + ny
    o_gc = o_gx + nx

    barrier = pltpu.get_barrier_semaphore()
    peers = [partner]
    for n, pos, dev in ((nx, x, x_dev), (nz, z, z_dev), (ny, s, y_dev)):
        peers += [dev((pos + d) % n) for d in range(1, n)]
    for peer in peers:
        pl.semaphore_signal(barrier, inc=1, device_id=peer, device_id_type=MESH)
    pl.semaphore_wait(barrier, len(peers))

    mine = pl.multiple_of(core * half, half)
    theirs = pl.multiple_of((1 - core) * half, half)
    c_copy = _remote(x_ref.at[pl.ds(theirs, half)], s_core.at[core],
                     send_sem.at[o_core], recv_sem.at[o_core + core], partner)
    c_copy.start()
    s_core[core] = x_ref[pl.ds(mine, half), :]
    _remote(s_core.at[1 - core], s_core.at[1 - core], send_sem.at[o_core],
            recv_sem.at[o_core + 1 - core], partner).wait_recv()
    c_copy.wait_send()
    s_core[core] = s_core[0] + s_core[1]

    copies = []
    for d in range(1, nx):
        p = (x + d) % nx
        cp = _remote(s_core.at[core, pl.ds(pl.multiple_of(p * chunk, chunk), chunk)], s_x.at[x],
                     send_sem.at[o_x + p], recv_sem.at[o_x + x], x_dev(p))
        cp.start()
        copies.append(cp)
    s_x[x] = s_core[core, pl.ds(pl.multiple_of(x * chunk, chunk), chunk), :]
    for d in range(1, nx):
        j = (x + d) % nx
        _remote(s_x.at[j], s_x.at[j], send_sem.at[o_x + j], recv_sem.at[o_x + j], x_dev(j)).wait_recv()
    for cp in copies:
        cp.wait_send()
    acc = s_x[0]
    for k in range(1, nx):
        acc = acc + s_x[k]

    for n, pos, dev, slots, off in ((nz, z, z_dev, s_z, o_z), (ny, s, y_dev, s_y, o_y)):
        slots[pos] = acc
        copies = []
        for d in range(1, n):
            p = (pos + d) % n
            cp = _remote(slots.at[pos], slots.at[pos], send_sem.at[off + p], recv_sem.at[off + pos], dev(p))
            cp.start()
            copies.append(cp)
        for d in range(1, n):
            j = (pos + d) % n
            _remote(slots.at[j], slots.at[j], send_sem.at[off + j], recv_sem.at[off + j], dev(j)).wait_recv()
        for cp in copies:
            cp.wait_send()
        acc = slots[0]
        for k in range(1, n):
            acc = acc + slots[k]

    row = lambda p: pl.multiple_of(core * half + p * chunk, chunk)
    res[pl.ds(row(x), chunk), :] = acc
    copies = []
    for d in range(1, nx):
        p = (x + d) % nx
        cp = _remote(res.at[pl.ds(row(x), chunk)], res.at[pl.ds(row(x), chunk)],
                     send_sem.at[o_gx + p], recv_sem.at[o_gx + x], x_dev(p))
        cp.start()
        copies.append(cp)
    for d in range(1, nx):
        j = (x + d) % nx
        _remote(res.at[pl.ds(row(j), chunk)], res.at[pl.ds(row(j), chunk)],
                send_sem.at[o_gx + j], recv_sem.at[o_gx + j], x_dev(j)).wait_recv()
    for cp in copies:
        cp.wait_send()

    cp = _remote(res.at[pl.ds(mine, half)], res.at[pl.ds(mine, half)],
                 send_sem.at[o_gc], recv_sem.at[o_gc + core], partner)
    cp.start()
    _remote(res.at[pl.ds(theirs, half)], res.at[pl.ds(theirs, half)],
            send_sem.at[o_gc], recv_sem.at[o_gc + 1 - core], partner).wait_recv()
    cp.wait_send()
    o_ref[...] = res[...] if scale == 1.0 else res[...] * scale


def make_allreduce(dims, cid, scale=1.0):
    nx, nz, ny = dims
    total = 2 + nx + nz + ny + nx + 2

    def allreduce(partial_value):
        rows, cols = partial_value.shape
        half = rows // 2
        chunk = half // nx
        return pl.pallas_call(
            functools.partial(_allreduce_kernel, dims, scale),
            out_shape=jax.ShapeDtypeStruct(partial_value.shape, jnp.float32),
            in_specs=[pl.BlockSpec(memory_space=pltpu.VMEM)],
            out_specs=pl.BlockSpec(memory_space=pltpu.VMEM),
            scratch_shapes=[
                pltpu.VMEM((2, half, cols), jnp.float32),
                pltpu.VMEM((nx, chunk, cols), jnp.float32),
                pltpu.VMEM((nz, chunk, cols), jnp.float32),
                pltpu.VMEM((ny, chunk, cols), jnp.float32),
                pltpu.VMEM((rows, cols), jnp.float32),
                pltpu.SemaphoreType.DMA((total,)),
                pltpu.SemaphoreType.DMA((total,)),
            ],
            compiler_params=pltpu.CompilerParams(collective_id=cid, has_side_effects=True),
        )(partial_value)

    return allreduce


def _chol_kernel(count, g_ref, *refs):
    if len(refs) == 4:
        prev_ref, lt_ref, w_ref, f_ref = refs
    else:
        prev_ref, f_ref = None, None
        lt_ref, w_ref = refs
    n = g_ref.shape[0]
    g = g_ref[...] / count
    a = (g + g.T) / 2
    sub = lax.broadcasted_iota(jnp.int32, (n, n), 0)
    lane = lax.broadcasted_iota(jnp.int32, (n, n), 1)
    w = jnp.where(sub == lane, 1.0, 0.0).astype(jnp.float32)
    lane_row = lax.broadcasted_iota(jnp.int32, (1, n), 1)
    lt_rows = []
    w_rows = []
    for k in range(n):
        r0 = k // 8 * 8
        row = a[k - r0:k - r0 + 1, :]
        colb = jnp.broadcast_to(a[:, k:k + 1], a.shape)
        recip = lax.rsqrt(colb[k - r0:k - r0 + 1, :])
        lrow = jnp.where(lane_row >= k, row * recip, 0.0)
        wrow = w[k - r0:k - r0 + 1, :] * recip
        lt_rows.append(lrow)
        w_rows.append(wrow)
        if k % 8 == 7:
            lt_ref[r0:r0 + 8, :] = jnp.concatenate(lt_rows, axis=0)
            w_ref[r0:r0 + 8, :] = jnp.concatenate(w_rows, axis=0)
            lt_rows, w_rows = [], []
        if k + 1 < n:
            r1 = (k + 1) // 8 * 8
            if r1 > r0:
                a = a[r1 - r0:]
                w = w[r1 - r0:]
                colb = colb[r1 - r0:]
            idx = lax.broadcasted_iota(jnp.int32, (n - r1, 1), 0) + r1
            m = jnp.where(idx > k, colb * recip, 0.0)
            a = a - m * lrow
            w = w - m * wrow
    if f_ref is not None:
        f_ref[...] = jnp.dot(lt_ref[...], prev_ref[...], precision=lax.Precision.HIGHEST,
                             preferred_element_type=jnp.float32)


def chol_inv(g, count, prev=None):
    n = g.shape[0]
    square = jax.ShapeDtypeStruct((n, n), jnp.float32)
    vmem = pl.BlockSpec(memory_space=pltpu.VMEM)
    outs = 2 if prev is None else 3
    return pl.pallas_call(
        functools.partial(_chol_kernel, float(count)),
        out_shape=(square,) * outs,
        in_specs=[vmem] * (1 if prev is None else 2),
        out_specs=(vmem,) * outs,
    )(g, *(() if prev is None else (prev,)))


def _jac_kernel(nbulk, cols_hbm, modes_ref, jac_ref, out_ref, ext, cols_ref, cols_sem, send_sem, recv_sem):
    cols_copy = pltpu.make_async_copy(cols_hbm, cols_ref, cols_sem)
    cols_copy.start()
    b = lax.axis_index("bulk")
    s = lax.axis_index("span")
    rb = modes_ref.shape[0]
    has_left = b > 0
    has_right = b < nbulk - 1
    barrier = pltpu.get_barrier_semaphore()

    @pl.when(has_left)
    def _():
        pl.semaphore_signal(barrier, inc=1, device_id=(b - 1, s), device_id_type=MESH)

    @pl.when(has_right)
    def _():
        pl.semaphore_signal(barrier, inc=1, device_id=(b + 1, s), device_id_type=MESH)

    pl.semaphore_wait(barrier, has_left.astype(jnp.int32) + has_right.astype(jnp.int32))

    to_left = pltpu.make_async_remote_copy(
        src_ref=modes_ref, dst_ref=ext.at[pl.ds(2 * rb, rb)], send_sem=send_sem.at[0],
        recv_sem=recv_sem.at[1], device_id=(b - 1, s), device_id_type=MESH)
    to_right = pltpu.make_async_remote_copy(
        src_ref=modes_ref, dst_ref=ext.at[pl.ds(0, rb)], send_sem=send_sem.at[1],
        recv_sem=recv_sem.at[0], device_id=(b + 1, s), device_id_type=MESH)

    @pl.when(has_left)
    def _():
        to_left.start()

    @pl.when(has_right)
    def _():
        to_right.start()

    ext[pl.ds(rb, rb)] = modes_ref[...]

    @pl.when(jnp.logical_not(has_left))
    def _():
        ext[pl.ds(0, rb)] = jnp.zeros(modes_ref.shape, modes_ref.dtype)

    @pl.when(jnp.logical_not(has_right))
    def _():
        ext[pl.ds(2 * rb, rb)] = jnp.zeros(modes_ref.shape, modes_ref.dtype)

    @pl.when(has_left)
    def _():
        to_right.wait_recv()
        to_left.wait_send()

    @pl.when(has_right)
    def _():
        to_left.wait_recv()
        to_right.wait_send()

    cols_copy.wait()
    start = (s * nbulk + b) * rb - rb

    def row(r, carry):
        acc = None
        for n in range(jac_ref.shape[1]):
            idx = jnp.clip(cols_ref[n, r] - start, 0, 3 * rb - 1)
            term = jnp.dot(jac_ref[r, n], ext[idx], preferred_element_type=jnp.float32)
            acc = term if acc is None else acc + term
        out_ref[r] = acc.astype(out_ref.dtype)
        return carry

    lax.fori_loop(0, rb, row, 0)


def jac_apply(nbulk, cid, jac_cols, modes_b, jac_blocks):
    rb, nb, blk, width = jac_blocks.shape[0], jac_blocks.shape[1], jac_blocks.shape[2], modes_b.shape[1]
    modes_blocks = modes_b.reshape(rb, blk, width)
    out = pl.pallas_call(
        functools.partial(_jac_kernel, nbulk),
        out_shape=jax.ShapeDtypeStruct((rb, blk, width), jnp.bfloat16),
        in_specs=[pl.BlockSpec(memory_space=pl.ANY),
                  pl.BlockSpec(memory_space=pltpu.VMEM),
                  pl.BlockSpec(memory_space=pltpu.VMEM)],
        out_specs=pl.BlockSpec(memory_space=pltpu.VMEM),
        scratch_shapes=[
            pltpu.VMEM((3 * rb, blk, width), jnp.bfloat16),
            pltpu.SMEM(jac_cols.shape[::-1], jnp.int32),
            pltpu.SemaphoreType.DMA(()),
            pltpu.SemaphoreType.DMA((2,)),
            pltpu.SemaphoreType.DMA((2,)),
        ],
        compiler_params=pltpu.CompilerParams(collective_id=cid, has_side_effects=True),
    )(jac_cols.T, modes_blocks, jac_blocks)
    return out.reshape(rb * blk, width)


def cholesky_step(data, row_count, allreduce, prev=None, precision=lax.Precision.HIGHEST):
    high = lax.Precision.HIGHEST
    partial_value = lax.dot_general(
        data, data, (((0,), (0,)), ((), ())), precision=high, preferred_element_type=jnp.float32
    )
    outs = chol_inv(allreduce(partial_value), row_count, prev)
    result = lax.dot_general(
        data, outs[1], (((1,), (1,)), ((), ())), precision=precision,
        preferred_element_type=jnp.float32,
    )
    return (result, outs[0] if prev is None else outs[2])


def shards(dims, snapshots, jac_blocks, jac_cols):
    high = lax.Precision.HIGHEST
    local_rows, width = snapshots.shape
    block_rows = jac_cols.shape[0]
    blk = jac_blocks.shape[2]
    row_count = local_rows * lax.axis_size(("bulk", "span"))
    first, upper1 = cholesky_step(snapshots, row_count, make_allreduce(dims, 0))
    modes, factor = cholesky_step(first, row_count, make_allreduce(dims, 1), upper1, lax.Precision.HIGH)
    modes_b = modes.astype(jnp.bfloat16)
    jac_modes = jac_apply(lax.axis_size("bulk"), 3, jac_cols, modes_b, jac_blocks)
    partial_value = lax.dot_general(
        modes,
        jac_modes.astype(jnp.float32),
        (((0,), (0,)), ((), ())),
        precision=lax.Precision.HIGH,
        preferred_element_type=jnp.float32,
    )
    reduced = make_allreduce(dims, 2, 1.0 / row_count)(partial_value)
    return (modes, factor, jac_modes, reduced)


def _torus_dims(mesh):
    coords = [d.coords for d in mesh.devices.flat]
    return tuple(len({c[i] for c in coords}) for i in (0, 2, 1))


def solution(mesh):
    nx, nz, ny = _torus_dims(mesh)
    assert mesh.shape["bulk"] == 2 * nx * nz and mesh.shape["span"] == ny
    return jax.shard_map(
        functools.partial(shards, (nx, nz, ny)),
        mesh=mesh,
        in_specs=(
            P(("span", "bulk"), None),
            P(("span", "bulk"), None, None, None),
            P(("span", "bulk"), None),
        ),
        out_specs=(P(("span", "bulk"), None), P(), P(("span", "bulk"), None), P()),
        check_vma=False,
    )
```

```python
import functools

import jax
import jax.numpy as jnp
from jax import lax
from jax.experimental import pallas as pl
from jax.experimental.pallas import tpu as pltpu
from jax.sharding import PartitionSpec as P

MESH = pl.DeviceIdType.MESH


def _coords(nx, nz):
    b = lax.axis_index("bulk")
    s = lax.axis_index("span")
    core = b % 2
    z = (b // 2) % nz
    x = b // (2 * nz)
    return b, s, core, x, z


def _remote(src, dst, send_sem, recv_sem, device):
    return pltpu.make_async_remote_copy(
        src_ref=src, dst_ref=dst, send_sem=send_sem, recv_sem=recv_sem,
        device_id=device, device_id_type=MESH,
    )


def _allreduce_kernel(dims, scale, x_ref, o_ref, s_core, s_x, s_z, s_y, res, send_sem, recv_sem):
    nx, nz, ny = dims
    b, s, core, x, z = _coords(nx, nz)
    rows = x_ref.shape[0]
    half = rows // 2
    chunk = half // nx
    partner = (b + 1 - 2 * core, s)
    x_dev = lambda p: ((p * nz + z) * 2 + core, s)
    z_dev = lambda p: ((x * nz + p) * 2 + core, s)
    y_dev = lambda p: (b, p)
    o_core, o_x, o_z, o_y = 0, 2, 2 + nx, 2 + nx + nz
    o_gx = o_y + ny

    barrier = pltpu.get_barrier_semaphore()
    peers = [partner]
    for n, pos, dev in ((nx, x, x_dev), (nz, z, z_dev), (ny, s, y_dev)):
        peers += [dev((pos + d) % n) for d in range(1, n)]
    peers += [((((x + d) % nx) * nz + z) * 2 + 1 - core, s) for d in range(1, nx)]
    for peer in peers:
        pl.semaphore_signal(barrier, inc=1, device_id=peer, device_id_type=MESH)
    pl.semaphore_wait(barrier, len(peers))

    mine = pl.multiple_of(core * half, half)
    theirs = pl.multiple_of((1 - core) * half, half)
    c_copy = _remote(x_ref.at[pl.ds(theirs, half)], s_core.at[core],
                     send_sem.at[o_core], recv_sem.at[o_core + core], partner)
    c_copy.start()
    s_core[core] = x_ref[pl.ds(mine, half), :]
    _remote(s_core.at[1 - core], s_core.at[1 - core], send_sem.at[o_core],
            recv_sem.at[o_core + 1 - core], partner).wait_recv()
    c_copy.wait_send()
    s_core[core] = s_core[0] + s_core[1]

    copies = []
    for d in range(1, nx):
        p = (x + d) % nx
        cp = _remote(s_core.at[core, pl.ds(pl.multiple_of(p * chunk, chunk), chunk)], s_x.at[x],
                     send_sem.at[o_x + p], recv_sem.at[o_x + x], x_dev(p))
        cp.start()
        copies.append(cp)
    s_x[x] = s_core[core, pl.ds(pl.multiple_of(x * chunk, chunk), chunk), :]
    for d in range(1, nx):
        j = (x + d) % nx
        _remote(s_x.at[j], s_x.at[j], send_sem.at[o_x + j], recv_sem.at[o_x + j], x_dev(j)).wait_recv()
    for cp in copies:
        cp.wait_send()
    acc = s_x[0]
    for k in range(1, nx):
        acc = acc + s_x[k]

    for n, pos, dev, slots, off in ((nz, z, z_dev, s_z, o_z), (ny, s, y_dev, s_y, o_y)):
        slots[pos] = acc
        copies = []
        for d in range(1, n):
            p = (pos + d) % n
            cp = _remote(slots.at[pos], slots.at[pos], send_sem.at[off + p], recv_sem.at[off + pos], dev(p))
            cp.start()
            copies.append(cp)
        for d in range(1, n):
            j = (pos + d) % n
            _remote(slots.at[j], slots.at[j], send_sem.at[off + j], recv_sem.at[off + j], dev(j)).wait_recv()
        for cp in copies:
            cp.wait_send()
        acc = slots[0]
        for k in range(1, n):
            acc = acc + slots[k]

    row = lambda c, p: pl.multiple_of(c * half + p * chunk, chunk)
    both = lambda c, p: ((p * nz + z) * 2 + c, s)
    res[pl.ds(row(core, x), chunk), :] = acc
    copies = []
    for c2 in range(2):
        for p in range(nx):
            skip = jnp.logical_and(c2 == core, p == x)
            cp = _remote(res.at[pl.ds(row(core, x), chunk)], res.at[pl.ds(row(core, x), chunk)],
                         send_sem.at[o_gx + c2 * nx + p], recv_sem.at[o_gx + core * nx + x], both(c2, p))
            pl.when(jnp.logical_not(skip))(cp.start)
            copies.append((skip, cp))
    for c2 in range(2):
        for p in range(nx):
            skip = jnp.logical_and(c2 == core, p == x)
            cp = _remote(res.at[pl.ds(row(c2, p), chunk)], res.at[pl.ds(row(c2, p), chunk)],
                         send_sem.at[o_gx + c2 * nx + p], recv_sem.at[o_gx + c2 * nx + p], both(c2, p))
            pl.when(jnp.logical_not(skip))(cp.wait_recv)
    for skip, cp in copies:
        pl.when(jnp.logical_not(skip))(cp.wait_send)
    o_ref[...] = res[...] if scale == 1.0 else res[...] * scale


def make_allreduce(dims, cid, scale=1.0):
    nx, nz, ny = dims
    total = 2 + nx + nz + ny + 2 * nx

    def allreduce(partial_value):
        rows, cols = partial_value.shape
        half = rows // 2
        chunk = half // nx
        return pl.pallas_call(
            functools.partial(_allreduce_kernel, dims, scale),
            out_shape=jax.ShapeDtypeStruct(partial_value.shape, jnp.float32),
            in_specs=[pl.BlockSpec(memory_space=pltpu.VMEM)],
            out_specs=pl.BlockSpec(memory_space=pltpu.VMEM),
            scratch_shapes=[
                pltpu.VMEM((2, half, cols), jnp.float32),
                pltpu.VMEM((nx, chunk, cols), jnp.float32),
                pltpu.VMEM((nz, chunk, cols), jnp.float32),
                pltpu.VMEM((ny, chunk, cols), jnp.float32),
                pltpu.VMEM((rows, cols), jnp.float32),
                pltpu.SemaphoreType.DMA((total,)),
                pltpu.SemaphoreType.DMA((total,)),
            ],
            compiler_params=pltpu.CompilerParams(collective_id=cid, has_side_effects=True),
        )(partial_value)

    return allreduce


def _chol_kernel(count, g_ref, *refs):
    if len(refs) == 4:
        prev_ref, lt_ref, w_ref, f_ref = refs
    else:
        prev_ref, f_ref = None, None
        lt_ref, w_ref = refs
    n = g_ref.shape[0]
    g = g_ref[...] / count
    a = (g + g.T) / 2
    sub = lax.broadcasted_iota(jnp.int32, (n, n), 0)
    lane = lax.broadcasted_iota(jnp.int32, (n, n), 1)
    w = jnp.where(sub == lane, 1.0, 0.0).astype(jnp.float32)
    lane_row = lax.broadcasted_iota(jnp.int32, (1, n), 1)
    lt_rows = []
    w_rows = []
    for k in range(n):
        r0 = k // 8 * 8
        row = a[k - r0:k - r0 + 1, :]
        colb = jnp.broadcast_to(a[:, k:k + 1], a.shape)
        recip = lax.rsqrt(colb[k - r0:k - r0 + 1, :])
        lrow = jnp.where(lane_row >= k, row * recip, 0.0)
        wrow = w[k - r0:k - r0 + 1, :] * recip
        lt_rows.append(lrow)
        w_rows.append(wrow)
        if k % 8 == 7:
            lt_ref[r0:r0 + 8, :] = jnp.concatenate(lt_rows, axis=0)
            w_ref[r0:r0 + 8, :] = jnp.concatenate(w_rows, axis=0)
            lt_rows, w_rows = [], []
        if k + 1 < n:
            r1 = (k + 1) // 8 * 8
            if r1 > r0:
                a = a[r1 - r0:]
                w = w[r1 - r0:]
                colb = colb[r1 - r0:]
            idx = lax.broadcasted_iota(jnp.int32, (n - r1, 1), 0) + r1
            m = jnp.where(idx > k, colb * recip, 0.0)
            a = a - m * lrow
            w = w - m * wrow
    if f_ref is not None:
        f_ref[...] = jnp.dot(lt_ref[...], prev_ref[...], precision=lax.Precision.HIGHEST,
                             preferred_element_type=jnp.float32)


def chol_inv(g, count, prev=None):
    n = g.shape[0]
    square = jax.ShapeDtypeStruct((n, n), jnp.float32)
    vmem = pl.BlockSpec(memory_space=pltpu.VMEM)
    outs = 2 if prev is None else 3
    return pl.pallas_call(
        functools.partial(_chol_kernel, float(count)),
        out_shape=(square,) * outs,
        in_specs=[vmem] * (1 if prev is None else 2),
        out_specs=(vmem,) * outs,
    )(g, *(() if prev is None else (prev,)))


def _jac_kernel(nbulk, cols_hbm, modes_ref, jac_ref, out_ref, ext, cols_ref, cols_sem, send_sem, recv_sem):
    cols_copy = pltpu.make_async_copy(cols_hbm, cols_ref, cols_sem)
    cols_copy.start()
    b = lax.axis_index("bulk")
    s = lax.axis_index("span")
    rb = modes_ref.shape[0]
    has_left = b > 0
    has_right = b < nbulk - 1
    barrier = pltpu.get_barrier_semaphore()

    @pl.when(has_left)
    def _():
        pl.semaphore_signal(barrier, inc=1, device_id=(b - 1, s), device_id_type=MESH)

    @pl.when(has_right)
    def _():
        pl.semaphore_signal(barrier, inc=1, device_id=(b + 1, s), device_id_type=MESH)

    pl.semaphore_wait(barrier, has_left.astype(jnp.int32) + has_right.astype(jnp.int32))

    to_left = pltpu.make_async_remote_copy(
        src_ref=modes_ref, dst_ref=ext.at[pl.ds(2 * rb, rb)], send_sem=send_sem.at[0],
        recv_sem=recv_sem.at[1], device_id=(b - 1, s), device_id_type=MESH)
    to_right = pltpu.make_async_remote_copy(
        src_ref=modes_ref, dst_ref=ext.at[pl.ds(0, rb)], send_sem=send_sem.at[1],
        recv_sem=recv_sem.at[0], device_id=(b + 1, s), device_id_type=MESH)

    @pl.when(has_left)
    def _():
        to_left.start()

    @pl.when(has_right)
    def _():
        to_right.start()

    ext[pl.ds(rb, rb)] = modes_ref[...]

    @pl.when(jnp.logical_not(has_left))
    def _():
        ext[pl.ds(0, rb)] = jnp.zeros(modes_ref.shape, modes_ref.dtype)

    @pl.when(jnp.logical_not(has_right))
    def _():
        ext[pl.ds(2 * rb, rb)] = jnp.zeros(modes_ref.shape, modes_ref.dtype)

    @pl.when(has_left)
    def _():
        to_right.wait_recv()
        to_left.wait_send()

    @pl.when(has_right)
    def _():
        to_left.wait_recv()
        to_right.wait_send()

    cols_copy.wait()
    start = (s * nbulk + b) * rb - rb

    def row(r, carry):
        acc = None
        for n in range(jac_ref.shape[1]):
            idx = jnp.clip(cols_ref[n, r] - start, 0, 3 * rb - 1)
            term = jnp.dot(jac_ref[r, n], ext[idx], preferred_element_type=jnp.float32)
            acc = term if acc is None else acc + term
        out_ref[r] = acc.astype(out_ref.dtype)
        return carry

    lax.fori_loop(0, rb, row, 0)


def jac_apply(nbulk, cid, jac_cols, modes_b, jac_blocks):
    rb, nb, blk, width = jac_blocks.shape[0], jac_blocks.shape[1], jac_blocks.shape[2], modes_b.shape[1]
    modes_blocks = modes_b.reshape(rb, blk, width)
    out = pl.pallas_call(
        functools.partial(_jac_kernel, nbulk),
        out_shape=jax.ShapeDtypeStruct((rb, blk, width), jnp.bfloat16),
        in_specs=[pl.BlockSpec(memory_space=pl.ANY),
                  pl.BlockSpec(memory_space=pltpu.VMEM),
                  pl.BlockSpec(memory_space=pltpu.VMEM)],
        out_specs=pl.BlockSpec(memory_space=pltpu.VMEM),
        scratch_shapes=[
            pltpu.VMEM((3 * rb, blk, width), jnp.bfloat16),
            pltpu.SMEM(jac_cols.shape[::-1], jnp.int32),
            pltpu.SemaphoreType.DMA(()),
            pltpu.SemaphoreType.DMA((2,)),
            pltpu.SemaphoreType.DMA((2,)),
        ],
        compiler_params=pltpu.CompilerParams(collective_id=cid, has_side_effects=True),
    )(jac_cols.T, modes_blocks, jac_blocks)
    return out.reshape(rb * blk, width)


def cholesky_step(data, row_count, allreduce, prev=None, precision=lax.Precision.HIGHEST):
    high = lax.Precision.HIGHEST
    partial_value = lax.dot_general(
        data, data, (((0,), (0,)), ((), ())), precision=high, preferred_element_type=jnp.float32
    )
    outs = chol_inv(allreduce(partial_value), row_count, prev)
    result = lax.dot_general(
        data, outs[1], (((1,), (1,)), ((), ())), precision=precision,
        preferred_element_type=jnp.float32,
    )
    return (result, outs[0] if prev is None else outs[2])


def shards(dims, snapshots, jac_blocks, jac_cols):
    high = lax.Precision.HIGHEST
    local_rows, width = snapshots.shape
    block_rows = jac_cols.shape[0]
    blk = jac_blocks.shape[2]
    row_count = local_rows * lax.axis_size(("bulk", "span"))
    first, upper1 = cholesky_step(snapshots, row_count, make_allreduce(dims, 0))
    modes, factor = cholesky_step(first, row_count, make_allreduce(dims, 1), upper1, lax.Precision.HIGH)
    modes_b = modes.astype(jnp.bfloat16)
    jac_modes = jac_apply(lax.axis_size("bulk"), 3, jac_cols, modes_b, jac_blocks)
    partial_value = lax.dot_general(
        modes,
        jac_modes.astype(jnp.float32),
        (((0,), (0,)), ((), ())),
        precision=lax.Precision.HIGH,
        preferred_element_type=jnp.float32,
    )
    reduced = make_allreduce(dims, 2, 1.0 / row_count)(partial_value)
    return (modes, factor, jac_modes, reduced)


def _torus_dims(mesh):
    coords = [d.coords for d in mesh.devices.flat]
    return tuple(len({c[i] for c in coords}) for i in (0, 2, 1))


def solution(mesh):
    nx, nz, ny = _torus_dims(mesh)
    assert mesh.shape["bulk"] == 2 * nx * nz and mesh.shape["span"] == ny
    return jax.shard_map(
        functools.partial(shards, (nx, nz, ny)),
        mesh=mesh,
        in_specs=(
            P(("span", "bulk"), None),
            P(("span", "bulk"), None, None, None),
            P(("span", "bulk"), None),
        ),
        out_specs=(P(("span", "bulk"), None), P(), P(("span", "bulk"), None), P()),
        check_vma=False,
    )
```

```python
import functools

import jax
import jax.numpy as jnp
from jax import lax
from jax.experimental import pallas as pl
from jax.experimental.pallas import tpu as pltpu
from jax.sharding import PartitionSpec as P

MESH = pl.DeviceIdType.MESH


def _coords(nx, nz):
    b = lax.axis_index("bulk")
    s = lax.axis_index("span")
    core = b % 2
    z = (b // 2) % nz
    x = b // (2 * nz)
    return b, s, core, x, z


def _remote(src, dst, send_sem, recv_sem, device):
    return pltpu.make_async_remote_copy(
        src_ref=src, dst_ref=dst, send_sem=send_sem, recv_sem=recv_sem,
        device_id=device, device_id_type=MESH,
    )


def _allreduce_kernel(dims, scale, x_ref, o_ref, s_x, s_z, s_y, res, send_sem, recv_sem):
    nx, nz, ny = dims
    b, s, core, x, z = _coords(nx, nz)
    rows = x_ref.shape[0]
    half = rows // 2
    chunk = half // nx
    partner = (b + 1 - 2 * core, s)
    x_dev = lambda p: ((p * nz + z) * 2 + core, s)
    z_dev = lambda p: ((x * nz + p) * 2 + core, s)
    y_dev = lambda p: (b, p)
    o_x, o_z, o_y = 0, 2 * nx, 2 * nx + nz
    o_gx = o_y + ny

    barrier = pltpu.get_barrier_semaphore()
    peers = [partner]
    for n, pos, dev in ((nx, x, x_dev), (nz, z, z_dev), (ny, s, y_dev)):
        peers += [dev((pos + d) % n) for d in range(1, n)]
    peers += [((((x + d) % nx) * nz + z) * 2 + 1 - core, s) for d in range(1, nx)]
    for peer in peers:
        pl.semaphore_signal(barrier, inc=1, device_id=peer, device_id_type=MESH)
    pl.semaphore_wait(barrier, len(peers))

    row = lambda c, p: pl.multiple_of(c * half + p * chunk, chunk)
    both = lambda c, p: ((p * nz + z) * 2 + c, s)
    me = core * nx + x
    copies = []
    for c2 in range(2):
        for p in range(nx):
            skip = jnp.logical_and(c2 == core, p == x)
            cp = _remote(x_ref.at[pl.ds(row(c2, p), chunk)], s_x.at[me],
                         send_sem.at[o_x + c2 * nx + p], recv_sem.at[o_x + me], both(c2, p))
            pl.when(jnp.logical_not(skip))(cp.start)
            copies.append((skip, cp))
    s_x[me] = x_ref[pl.ds(row(core, x), chunk), :]
    for c2 in range(2):
        for p in range(nx):
            skip = jnp.logical_and(c2 == core, p == x)
            j = c2 * nx + p
            cp = _remote(s_x.at[j], s_x.at[j], send_sem.at[o_x + j], recv_sem.at[o_x + j], both(c2, p))
            pl.when(jnp.logical_not(skip))(cp.wait_recv)
    for skip, cp in copies:
        pl.when(jnp.logical_not(skip))(cp.wait_send)
    acc = s_x[0]
    for k in range(1, 2 * nx):
        acc = acc + s_x[k]

    for n, pos, dev, slots, off in ((nz, z, z_dev, s_z, o_z), (ny, s, y_dev, s_y, o_y)):
        slots[pos] = acc
        copies = []
        for d in range(1, n):
            p = (pos + d) % n
            cp = _remote(slots.at[pos], slots.at[pos], send_sem.at[off + p], recv_sem.at[off + pos], dev(p))
            cp.start()
            copies.append(cp)
        for d in range(1, n):
            j = (pos + d) % n
            _remote(slots.at[j], slots.at[j], send_sem.at[off + j], recv_sem.at[off + j], dev(j)).wait_recv()
        for cp in copies:
            cp.wait_send()
        acc = slots[0]
        for k in range(1, n):
            acc = acc + slots[k]

    row = lambda c, p: pl.multiple_of(c * half + p * chunk, chunk)
    both = lambda c, p: ((p * nz + z) * 2 + c, s)
    res[pl.ds(row(core, x), chunk), :] = acc
    copies = []
    for c2 in range(2):
        for p in range(nx):
            skip = jnp.logical_and(c2 == core, p == x)
            cp = _remote(res.at[pl.ds(row(core, x), chunk)], res.at[pl.ds(row(core, x), chunk)],
                         send_sem.at[o_gx + c2 * nx + p], recv_sem.at[o_gx + core * nx + x], both(c2, p))
            pl.when(jnp.logical_not(skip))(cp.start)
            copies.append((skip, cp))
    for c2 in range(2):
        for p in range(nx):
            skip = jnp.logical_and(c2 == core, p == x)
            cp = _remote(res.at[pl.ds(row(c2, p), chunk)], res.at[pl.ds(row(c2, p), chunk)],
                         send_sem.at[o_gx + c2 * nx + p], recv_sem.at[o_gx + c2 * nx + p], both(c2, p))
            pl.when(jnp.logical_not(skip))(cp.wait_recv)
    for skip, cp in copies:
        pl.when(jnp.logical_not(skip))(cp.wait_send)
    o_ref[...] = res[...] if scale == 1.0 else res[...] * scale


def make_allreduce(dims, cid, scale=1.0):
    nx, nz, ny = dims
    total = 2 * nx + nz + ny + 2 * nx

    def allreduce(partial_value):
        rows, cols = partial_value.shape
        half = rows // 2
        chunk = half // nx
        return pl.pallas_call(
            functools.partial(_allreduce_kernel, dims, scale),
            out_shape=jax.ShapeDtypeStruct(partial_value.shape, jnp.float32),
            in_specs=[pl.BlockSpec(memory_space=pltpu.VMEM)],
            out_specs=pl.BlockSpec(memory_space=pltpu.VMEM),
            scratch_shapes=[
                pltpu.VMEM((2 * nx, chunk, cols), jnp.float32),
                pltpu.VMEM((nz, chunk, cols), jnp.float32),
                pltpu.VMEM((ny, chunk, cols), jnp.float32),
                pltpu.VMEM((rows, cols), jnp.float32),
                pltpu.SemaphoreType.DMA((total,)),
                pltpu.SemaphoreType.DMA((total,)),
            ],
            compiler_params=pltpu.CompilerParams(collective_id=cid, has_side_effects=True),
        )(partial_value)

    return allreduce


def _chol_kernel(count, g_ref, *refs):
    if len(refs) == 4:
        prev_ref, lt_ref, w_ref, f_ref = refs
    else:
        prev_ref, f_ref = None, None
        lt_ref, w_ref = refs
    n = g_ref.shape[0]
    g = g_ref[...] / count
    a = (g + g.T) / 2
    sub = lax.broadcasted_iota(jnp.int32, (n, n), 0)
    lane = lax.broadcasted_iota(jnp.int32, (n, n), 1)
    w = jnp.where(sub == lane, 1.0, 0.0).astype(jnp.float32)
    lane_row = lax.broadcasted_iota(jnp.int32, (1, n), 1)
    lt_rows = []
    w_rows = []
    for k in range(n):
        r0 = k // 8 * 8
        row = a[k - r0:k - r0 + 1, :]
        colb = jnp.broadcast_to(a[:, k:k + 1], a.shape)
        recip = lax.rsqrt(colb[k - r0:k - r0 + 1, :])
        lrow = jnp.where(lane_row >= k, row * recip, 0.0)
        wrow = w[k - r0:k - r0 + 1, :] * recip
        lt_rows.append(lrow)
        w_rows.append(wrow)
        if k % 8 == 7:
            lt_ref[r0:r0 + 8, :] = jnp.concatenate(lt_rows, axis=0)
            w_ref[r0:r0 + 8, :] = jnp.concatenate(w_rows, axis=0)
            lt_rows, w_rows = [], []
        if k + 1 < n:
            r1 = (k + 1) // 8 * 8
            if r1 > r0:
                a = a[r1 - r0:]
                w = w[r1 - r0:]
                colb = colb[r1 - r0:]
            idx = lax.broadcasted_iota(jnp.int32, (n - r1, 1), 0) + r1
            m = jnp.where(idx > k, colb * recip, 0.0)
            a = a - m * lrow
            w = w - m * wrow
    if f_ref is not None:
        f_ref[...] = jnp.dot(lt_ref[...], prev_ref[...], precision=lax.Precision.HIGHEST,
                             preferred_element_type=jnp.float32)


def chol_inv(g, count, prev=None):
    n = g.shape[0]
    square = jax.ShapeDtypeStruct((n, n), jnp.float32)
    vmem = pl.BlockSpec(memory_space=pltpu.VMEM)
    outs = 2 if prev is None else 3
    return pl.pallas_call(
        functools.partial(_chol_kernel, float(count)),
        out_shape=(square,) * outs,
        in_specs=[vmem] * (1 if prev is None else 2),
        out_specs=(vmem,) * outs,
    )(g, *(() if prev is None else (prev,)))


def _jac_kernel(nbulk, cols_hbm, modes_ref, jac_ref, out_ref, ext, cols_ref, cols_sem, send_sem, recv_sem):
    cols_copy = pltpu.make_async_copy(cols_hbm, cols_ref, cols_sem)
    cols_copy.start()
    b = lax.axis_index("bulk")
    s = lax.axis_index("span")
    rb = modes_ref.shape[0]
    has_left = b > 0
    has_right = b < nbulk - 1
    barrier = pltpu.get_barrier_semaphore()

    @pl.when(has_left)
    def _():
        pl.semaphore_signal(barrier, inc=1, device_id=(b - 1, s), device_id_type=MESH)

    @pl.when(has_right)
    def _():
        pl.semaphore_signal(barrier, inc=1, device_id=(b + 1, s), device_id_type=MESH)

    pl.semaphore_wait(barrier, has_left.astype(jnp.int32) + has_right.astype(jnp.int32))

    to_left = pltpu.make_async_remote_copy(
        src_ref=modes_ref, dst_ref=ext.at[pl.ds(2 * rb, rb)], send_sem=send_sem.at[0],
        recv_sem=recv_sem.at[1], device_id=(b - 1, s), device_id_type=MESH)
    to_right = pltpu.make_async_remote_copy(
        src_ref=modes_ref, dst_ref=ext.at[pl.ds(0, rb)], send_sem=send_sem.at[1],
        recv_sem=recv_sem.at[0], device_id=(b + 1, s), device_id_type=MESH)

    @pl.when(has_left)
    def _():
        to_left.start()

    @pl.when(has_right)
    def _():
        to_right.start()

    ext[pl.ds(rb, rb)] = modes_ref[...]

    @pl.when(jnp.logical_not(has_left))
    def _():
        ext[pl.ds(0, rb)] = jnp.zeros(modes_ref.shape, modes_ref.dtype)

    @pl.when(jnp.logical_not(has_right))
    def _():
        ext[pl.ds(2 * rb, rb)] = jnp.zeros(modes_ref.shape, modes_ref.dtype)

    @pl.when(has_left)
    def _():
        to_right.wait_recv()
        to_left.wait_send()

    @pl.when(has_right)
    def _():
        to_left.wait_recv()
        to_right.wait_send()

    cols_copy.wait()
    start = (s * nbulk + b) * rb - rb

    def row(r, carry):
        acc = None
        for n in range(jac_ref.shape[1]):
            idx = jnp.clip(cols_ref[n, r] - start, 0, 3 * rb - 1)
            term = jnp.dot(jac_ref[r, n], ext[idx], preferred_element_type=jnp.float32)
            acc = term if acc is None else acc + term
        out_ref[r] = acc.astype(out_ref.dtype)
        return carry

    lax.fori_loop(0, rb, row, 0)


def jac_apply(nbulk, cid, jac_cols, modes_b, jac_blocks):
    rb, nb, blk, width = jac_blocks.shape[0], jac_blocks.shape[1], jac_blocks.shape[2], modes_b.shape[1]
    modes_blocks = modes_b.reshape(rb, blk, width)
    out = pl.pallas_call(
        functools.partial(_jac_kernel, nbulk),
        out_shape=jax.ShapeDtypeStruct((rb, blk, width), jnp.bfloat16),
        in_specs=[pl.BlockSpec(memory_space=pl.ANY),
                  pl.BlockSpec(memory_space=pltpu.VMEM),
                  pl.BlockSpec(memory_space=pltpu.VMEM)],
        out_specs=pl.BlockSpec(memory_space=pltpu.VMEM),
        scratch_shapes=[
            pltpu.VMEM((3 * rb, blk, width), jnp.bfloat16),
            pltpu.SMEM(jac_cols.shape[::-1], jnp.int32),
            pltpu.SemaphoreType.DMA(()),
            pltpu.SemaphoreType.DMA((2,)),
            pltpu.SemaphoreType.DMA((2,)),
        ],
        compiler_params=pltpu.CompilerParams(collective_id=cid, has_side_effects=True),
    )(jac_cols.T, modes_blocks, jac_blocks)
    return out.reshape(rb * blk, width)


def cholesky_step(data, row_count, allreduce, prev=None, precision=lax.Precision.HIGHEST):
    high = lax.Precision.HIGHEST
    partial_value = lax.dot_general(
        data, data, (((0,), (0,)), ((), ())), precision=high, preferred_element_type=jnp.float32
    )
    outs = chol_inv(allreduce(partial_value), row_count, prev)
    result = lax.dot_general(
        data, outs[1], (((1,), (1,)), ((), ())), precision=precision,
        preferred_element_type=jnp.float32,
    )
    return (result, outs[0] if prev is None else outs[2])


def shards(dims, snapshots, jac_blocks, jac_cols):
    high = lax.Precision.HIGHEST
    local_rows, width = snapshots.shape
    block_rows = jac_cols.shape[0]
    blk = jac_blocks.shape[2]
    row_count = local_rows * lax.axis_size(("bulk", "span"))
    first, upper1 = cholesky_step(snapshots, row_count, make_allreduce(dims, 0))
    modes, factor = cholesky_step(first, row_count, make_allreduce(dims, 1), upper1, lax.Precision.HIGH)
    modes_b = modes.astype(jnp.bfloat16)
    jac_modes = jac_apply(lax.axis_size("bulk"), 3, jac_cols, modes_b, jac_blocks)
    partial_value = lax.dot_general(
        modes,
        jac_modes.astype(jnp.float32),
        (((0,), (0,)), ((), ())),
        precision=lax.Precision.HIGH,
        preferred_element_type=jnp.float32,
    )
    reduced = make_allreduce(dims, 2, 1.0 / row_count)(partial_value)
    return (modes, factor, jac_modes, reduced)


def _torus_dims(mesh):
    coords = [d.coords for d in mesh.devices.flat]
    return tuple(len({c[i] for c in coords}) for i in (0, 2, 1))


def solution(mesh):
    nx, nz, ny = _torus_dims(mesh)
    assert mesh.shape["bulk"] == 2 * nx * nz and mesh.shape["span"] == ny
    return jax.shard_map(
        functools.partial(shards, (nx, nz, ny)),
        mesh=mesh,
        in_specs=(
            P(("span", "bulk"), None),
            P(("span", "bulk"), None, None, None),
            P(("span", "bulk"), None),
        ),
        out_specs=(P(("span", "bulk"), None), P(), P(("span", "bulk"), None), P()),
        check_vma=False,
    )
```

```python
import functools

import jax
import jax.numpy as jnp
from jax import lax
from jax.experimental import pallas as pl
from jax.experimental.pallas import tpu as pltpu
from jax.sharding import PartitionSpec as P

MESH = pl.DeviceIdType.MESH


def _coords(nx, nz):
    b = lax.axis_index("bulk")
    s = lax.axis_index("span")
    core = b % 2
    z = (b // 2) % nz
    x = b // (2 * nz)
    return b, s, core, x, z


def _remote(src, dst, send_sem, recv_sem, device):
    return pltpu.make_async_remote_copy(
        src_ref=src, dst_ref=dst, send_sem=send_sem, recv_sem=recv_sem,
        device_id=device, device_id_type=MESH,
    )


def _allreduce_kernel(dims, scale, x_ref, o_ref, s_x, s_z, s_y, res, send_sem, recv_sem):
    nx, nz, ny = dims
    b, s, core, x, z = _coords(nx, nz)
    rows = x_ref.shape[0]
    half = rows // 2
    chunk = half // nx
    partner = (b + 1 - 2 * core, s)
    x_dev = lambda p: ((p * nz + z) * 2 + core, s)
    z_dev = lambda p: ((x * nz + p) * 2 + core, s)
    y_dev = lambda p: (b, p)
    o_x, o_z, o_y = 0, 2 * nx, 2 * nx + nz
    o_gx = o_y + ny

    barrier = pltpu.get_barrier_semaphore()
    peers = [partner]
    for n, pos, dev in ((nx, x, x_dev), (nz, z, z_dev), (ny, s, y_dev)):
        peers += [dev((pos + d) % n) for d in range(1, n)]
    peers += [((((x + d) % nx) * nz + z) * 2 + 1 - core, s) for d in range(1, nx)]
    for peer in peers:
        pl.semaphore_signal(barrier, inc=1, device_id=peer, device_id_type=MESH)
    pl.semaphore_wait(barrier, len(peers))

    row = lambda c, p: pl.multiple_of(c * half + p * chunk, chunk)
    both = lambda c, p: ((p * nz + z) * 2 + c, s)
    me = core * nx + x
    copies = []
    for c2 in range(2):
        for p in range(nx):
            skip = jnp.logical_and(c2 == core, p == x)
            cp = _remote(x_ref.at[pl.ds(row(c2, p), chunk)], s_x.at[me],
                         send_sem.at[o_x + c2 * nx + p], recv_sem.at[o_x + me], both(c2, p))
            pl.when(jnp.logical_not(skip))(cp.start)
            copies.append((skip, cp))
    s_x[me] = x_ref[pl.ds(row(core, x), chunk), :]
    for c2 in range(2):
        for p in range(nx):
            skip = jnp.logical_and(c2 == core, p == x)
            j = c2 * nx + p
            cp = _remote(s_x.at[j], s_x.at[j], send_sem.at[o_x + j], recv_sem.at[o_x + j], both(c2, p))
            pl.when(jnp.logical_not(skip))(cp.wait_recv)
    for skip, cp in copies:
        pl.when(jnp.logical_not(skip))(cp.wait_send)
    acc = s_x[0]
    for k in range(1, 2 * nx):
        acc = acc + s_x[k]

    for n, pos, dev, slots, off in ((nz, z, z_dev, s_z, o_z), (ny, s, y_dev, s_y, o_y)):
        slots[pos] = acc
        copies = []
        for d in range(1, n):
            p = (pos + d) % n
            cp = _remote(slots.at[pos], slots.at[pos], send_sem.at[off + p], recv_sem.at[off + pos], dev(p))
            cp.start()
            copies.append(cp)
        for d in range(1, n):
            j = (pos + d) % n
            _remote(slots.at[j], slots.at[j], send_sem.at[off + j], recv_sem.at[off + j], dev(j)).wait_recv()
        for cp in copies:
            cp.wait_send()
        acc = slots[0]
        for k in range(1, n):
            acc = acc + slots[k]

    row = lambda c, p: pl.multiple_of(c * half + p * chunk, chunk)
    both = lambda c, p: ((p * nz + z) * 2 + c, s)
    res[pl.ds(row(core, x), chunk), :] = acc
    copies = []
    for c2 in range(2):
        for p in range(nx):
            skip = jnp.logical_and(c2 == core, p == x)
            cp = _remote(res.at[pl.ds(row(core, x), chunk)], res.at[pl.ds(row(core, x), chunk)],
                         send_sem.at[o_gx + c2 * nx + p], recv_sem.at[o_gx + core * nx + x], both(c2, p))
            pl.when(jnp.logical_not(skip))(cp.start)
            copies.append((skip, cp))
    for c2 in range(2):
        for p in range(nx):
            skip = jnp.logical_and(c2 == core, p == x)
            cp = _remote(res.at[pl.ds(row(c2, p), chunk)], res.at[pl.ds(row(c2, p), chunk)],
                         send_sem.at[o_gx + c2 * nx + p], recv_sem.at[o_gx + c2 * nx + p], both(c2, p))
            pl.when(jnp.logical_not(skip))(cp.wait_recv)
    for skip, cp in copies:
        pl.when(jnp.logical_not(skip))(cp.wait_send)
    o_ref[...] = res[...] if scale == 1.0 else res[...] * scale


def make_allreduce(dims, cid, scale=1.0):
    nx, nz, ny = dims
    total = 2 * nx + nz + ny + 2 * nx

    def allreduce(partial_value):
        rows, cols = partial_value.shape
        half = rows // 2
        chunk = half // nx
        return pl.pallas_call(
            functools.partial(_allreduce_kernel, dims, scale),
            out_shape=jax.ShapeDtypeStruct(partial_value.shape, jnp.float32),
            in_specs=[pl.BlockSpec(memory_space=pltpu.VMEM)],
            out_specs=pl.BlockSpec(memory_space=pltpu.VMEM),
            scratch_shapes=[
                pltpu.VMEM((2 * nx, chunk, cols), jnp.float32),
                pltpu.VMEM((nz, chunk, cols), jnp.float32),
                pltpu.VMEM((ny, chunk, cols), jnp.float32),
                pltpu.VMEM((rows, cols), jnp.float32),
                pltpu.SemaphoreType.DMA((total,)),
                pltpu.SemaphoreType.DMA((total,)),
            ],
            compiler_params=pltpu.CompilerParams(collective_id=cid, has_side_effects=True),
        )(partial_value)

    return allreduce


def _chol_kernel(count, g_ref, *refs):
    if len(refs) == 4:
        prev_ref, lt_ref, w_ref, f_ref = refs
    else:
        prev_ref, f_ref = None, None
        lt_ref, w_ref = refs
    n = g_ref.shape[0]
    g = g_ref[...] / count
    a = (g + g.T) / 2
    sub = lax.broadcasted_iota(jnp.int32, (n, n), 0)
    lane = lax.broadcasted_iota(jnp.int32, (n, n), 1)
    w = jnp.where(sub == lane, 1.0, 0.0).astype(jnp.float32)
    lane_row = lax.broadcasted_iota(jnp.int32, (1, n), 1)
    lt_rows = []
    w_rows = []
    for k in range(n):
        r0 = k // 8 * 8
        row = a[k - r0:k - r0 + 1, :]
        colb = jnp.broadcast_to(a[:, k:k + 1], a.shape)
        recip = lax.rsqrt(colb[k - r0:k - r0 + 1, :])
        lrow = jnp.where(lane_row >= k, row * recip, 0.0)
        wrow = w[k - r0:k - r0 + 1, :] * recip
        lt_rows.append(lrow)
        w_rows.append(wrow)
        if k % 8 == 7:
            lt_ref[r0:r0 + 8, :] = jnp.concatenate(lt_rows, axis=0)
            w_ref[r0:r0 + 8, :] = jnp.concatenate(w_rows, axis=0)
            lt_rows, w_rows = [], []
        if k + 1 < n:
            r1 = (k + 1) // 8 * 8
            if r1 > r0:
                a = a[r1 - r0:]
                w = w[r1 - r0:]
                colb = colb[r1 - r0:]
            idx = lax.broadcasted_iota(jnp.int32, (n - r1, 1), 0) + r1
            m = jnp.where(idx > k, colb * recip, 0.0)
            a = a - m * lrow
            w = w - m * wrow
    if f_ref is not None:
        f_ref[...] = jnp.dot(lt_ref[...], prev_ref[...], precision=lax.Precision.HIGHEST,
                             preferred_element_type=jnp.float32)


def chol_inv(g, count, prev=None):
    n = g.shape[0]
    square = jax.ShapeDtypeStruct((n, n), jnp.float32)
    vmem = pl.BlockSpec(memory_space=pltpu.VMEM)
    outs = 2 if prev is None else 3
    return pl.pallas_call(
        functools.partial(_chol_kernel, float(count)),
        out_shape=(square,) * outs,
        in_specs=[vmem] * (1 if prev is None else 2),
        out_specs=(vmem,) * outs,
    )(g, *(() if prev is None else (prev,)))


def _jac_kernel(nbulk, cols_hbm, modes_ref, jac_ref, out_ref, ext, cols_ref, cols_sem, send_sem, recv_sem):
    cols_copy = pltpu.make_async_copy(cols_hbm, cols_ref, cols_sem)
    cols_copy.start()
    b = lax.axis_index("bulk")
    s = lax.axis_index("span")
    rb = modes_ref.shape[0]
    has_left = b > 0
    has_right = b < nbulk - 1
    barrier = pltpu.get_barrier_semaphore()

    @pl.when(has_left)
    def _():
        pl.semaphore_signal(barrier, inc=1, device_id=(b - 1, s), device_id_type=MESH)

    @pl.when(has_right)
    def _():
        pl.semaphore_signal(barrier, inc=1, device_id=(b + 1, s), device_id_type=MESH)

    pl.semaphore_wait(barrier, has_left.astype(jnp.int32) + has_right.astype(jnp.int32))

    to_left = pltpu.make_async_remote_copy(
        src_ref=modes_ref, dst_ref=ext.at[pl.ds(2 * rb, rb)], send_sem=send_sem.at[0],
        recv_sem=recv_sem.at[1], device_id=(b - 1, s), device_id_type=MESH)
    to_right = pltpu.make_async_remote_copy(
        src_ref=modes_ref, dst_ref=ext.at[pl.ds(0, rb)], send_sem=send_sem.at[1],
        recv_sem=recv_sem.at[0], device_id=(b + 1, s), device_id_type=MESH)

    @pl.when(has_left)
    def _():
        to_left.start()

    @pl.when(has_right)
    def _():
        to_right.start()

    ext[pl.ds(rb, rb)] = modes_ref[...]

    @pl.when(jnp.logical_not(has_left))
    def _():
        ext[pl.ds(0, rb)] = jnp.zeros(modes_ref.shape, modes_ref.dtype)

    @pl.when(jnp.logical_not(has_right))
    def _():
        ext[pl.ds(2 * rb, rb)] = jnp.zeros(modes_ref.shape, modes_ref.dtype)

    @pl.when(has_left)
    def _():
        to_right.wait_recv()
        to_left.wait_send()

    @pl.when(has_right)
    def _():
        to_left.wait_recv()
        to_right.wait_send()

    cols_copy.wait()
    start = (s * nbulk + b) * rb - rb

    def row(r, carry):
        acc = None
        for n in range(jac_ref.shape[1]):
            idx = jnp.clip(cols_ref[n, r] - start, 0, 3 * rb - 1)
            term = jnp.dot(jac_ref[r, n], ext[idx], preferred_element_type=jnp.float32)
            acc = term if acc is None else acc + term
        out_ref[r] = acc.astype(out_ref.dtype)
        return carry

    lax.fori_loop(0, rb, row, 0)


def jac_apply(nbulk, cid, jac_cols, modes_b, jac_blocks):
    rb, nb, blk, width = jac_blocks.shape[0], jac_blocks.shape[1], jac_blocks.shape[2], modes_b.shape[1]
    modes_blocks = modes_b.reshape(rb, blk, width)
    out = pl.pallas_call(
        functools.partial(_jac_kernel, nbulk),
        out_shape=jax.ShapeDtypeStruct((rb, blk, width), jnp.bfloat16),
        in_specs=[pl.BlockSpec(memory_space=pl.ANY),
                  pl.BlockSpec(memory_space=pltpu.VMEM),
                  pl.BlockSpec(memory_space=pltpu.VMEM)],
        out_specs=pl.BlockSpec(memory_space=pltpu.VMEM),
        scratch_shapes=[
            pltpu.VMEM((3 * rb, blk, width), jnp.bfloat16),
            pltpu.SMEM(jac_cols.shape[::-1], jnp.int32),
            pltpu.SemaphoreType.DMA(()),
            pltpu.SemaphoreType.DMA((2,)),
            pltpu.SemaphoreType.DMA((2,)),
        ],
        compiler_params=pltpu.CompilerParams(collective_id=cid, has_side_effects=True),
    )(jac_cols.T, modes_blocks, jac_blocks)
    return out.reshape(rb * blk, width)


def cholesky_step(data, row_count, allreduce, prev=None, precision=lax.Precision.HIGHEST):
    high = lax.Precision.HIGHEST
    gram_precision = high if prev is None else precision
    partial_value = lax.dot_general(
        data, data, (((0,), (0,)), ((), ())), precision=gram_precision,
        preferred_element_type=jnp.float32,
    )
    outs = chol_inv(allreduce(partial_value), row_count, prev)
    result = lax.dot_general(
        data, outs[1], (((1,), (1,)), ((), ())), precision=precision,
        preferred_element_type=jnp.float32,
    )
    return (result, outs[0] if prev is None else outs[2])


def shards(dims, snapshots, jac_blocks, jac_cols):
    high = lax.Precision.HIGHEST
    local_rows, width = snapshots.shape
    block_rows = jac_cols.shape[0]
    blk = jac_blocks.shape[2]
    row_count = local_rows * lax.axis_size(("bulk", "span"))
    first, upper1 = cholesky_step(snapshots, row_count, make_allreduce(dims, 0))
    modes, factor = cholesky_step(first, row_count, make_allreduce(dims, 1), upper1, lax.Precision.HIGH)
    modes_b = modes.astype(jnp.bfloat16)
    jac_modes = jac_apply(lax.axis_size("bulk"), 3, jac_cols, modes_b, jac_blocks)
    partial_value = lax.dot_general(
        modes,
        jac_modes.astype(jnp.float32),
        (((0,), (0,)), ((), ())),
        precision=lax.Precision.HIGH,
        preferred_element_type=jnp.float32,
    )
    reduced = make_allreduce(dims, 2, 1.0 / row_count)(partial_value)
    return (modes, factor, jac_modes, reduced)


def _torus_dims(mesh):
    coords = [d.coords for d in mesh.devices.flat]
    return tuple(len({c[i] for c in coords}) for i in (0, 2, 1))


def solution(mesh):
    nx, nz, ny = _torus_dims(mesh)
    assert mesh.shape["bulk"] == 2 * nx * nz and mesh.shape["span"] == ny
    return jax.shard_map(
        functools.partial(shards, (nx, nz, ny)),
        mesh=mesh,
        in_specs=(
            P(("span", "bulk"), None),
            P(("span", "bulk"), None, None, None),
            P(("span", "bulk"), None),
        ),
        out_specs=(P(("span", "bulk"), None), P(), P(("span", "bulk"), None), P()),
        check_vma=False,
    )
```

```python
import functools

import jax
import jax.numpy as jnp
from jax import lax
from jax.experimental import pallas as pl
from jax.experimental.pallas import tpu as pltpu
from jax.sharding import PartitionSpec as P

MESH = pl.DeviceIdType.MESH


def _coords(nx, nz):
    b = lax.axis_index("bulk")
    s = lax.axis_index("span")
    core = b % 2
    z = (b // 2) % nz
    x = b // (2 * nz)
    return b, s, core, x, z


def _remote(src, dst, send_sem, recv_sem, device):
    return pltpu.make_async_remote_copy(
        src_ref=src, dst_ref=dst, send_sem=send_sem, recv_sem=recv_sem,
        device_id=device, device_id_type=MESH,
    )


def _allreduce_kernel(dims, scale, x_ref, o_ref, s_x, s_z, s_y, res, send_sem, recv_sem):
    nx, nz, ny = dims
    b, s, core, x, z = _coords(nx, nz)
    rows = x_ref.shape[0]
    half = rows // 2
    chunk = half // nx
    partner = (b + 1 - 2 * core, s)
    x_dev = lambda p: ((p * nz + z) * 2 + core, s)
    z_dev = lambda p: ((x * nz + p) * 2 + core, s)
    y_dev = lambda p: (b, p)
    o_x, o_z, o_y = 0, 2 * nx, 2 * nx + nz
    o_gx = o_y + ny

    barrier = pltpu.get_barrier_semaphore()
    peers = [partner]
    for n, pos, dev in ((nx, x, x_dev), (nz, z, z_dev), (ny, s, y_dev)):
        peers += [dev((pos + d) % n) for d in range(1, n)]
    peers += [((((x + d) % nx) * nz + z) * 2 + 1 - core, s) for d in range(1, nx)]
    for peer in peers:
        pl.semaphore_signal(barrier, inc=1, device_id=peer, device_id_type=MESH)
    pl.semaphore_wait(barrier, len(peers))

    row = lambda c, p: pl.multiple_of(c * half + p * chunk, chunk)
    both = lambda c, p: ((p * nz + z) * 2 + c, s)
    me = core * nx + x
    copies = []
    for c2 in range(2):
        for p in range(nx):
            skip = jnp.logical_and(c2 == core, p == x)
            cp = _remote(x_ref.at[pl.ds(row(c2, p), chunk)], s_x.at[me],
                         send_sem.at[o_x + c2 * nx + p], recv_sem.at[o_x + me], both(c2, p))
            pl.when(jnp.logical_not(skip))(cp.start)
            copies.append((skip, cp))
    s_x[me] = x_ref[pl.ds(row(core, x), chunk), :]
    for c2 in range(2):
        for p in range(nx):
            skip = jnp.logical_and(c2 == core, p == x)
            j = c2 * nx + p
            cp = _remote(s_x.at[j], s_x.at[j], send_sem.at[o_x + j], recv_sem.at[o_x + j], both(c2, p))
            pl.when(jnp.logical_not(skip))(cp.wait_recv)
    for skip, cp in copies:
        pl.when(jnp.logical_not(skip))(cp.wait_send)
    acc = s_x[0]
    for k in range(1, 2 * nx):
        acc = acc + s_x[k]

    for n, pos, dev, slots, off in ((nz, z, z_dev, s_z, o_z), (ny, s, y_dev, s_y, o_y)):
        slots[pos] = acc
        copies = []
        for d in range(1, n):
            p = (pos + d) % n
            cp = _remote(slots.at[pos], slots.at[pos], send_sem.at[off + p], recv_sem.at[off + pos], dev(p))
            cp.start()
            copies.append(cp)
        for d in range(1, n):
            j = (pos + d) % n
            _remote(slots.at[j], slots.at[j], send_sem.at[off + j], recv_sem.at[off + j], dev(j)).wait_recv()
        for cp in copies:
            cp.wait_send()
        acc = slots[0]
        for k in range(1, n):
            acc = acc + slots[k]

    row = lambda c, p: pl.multiple_of(c * half + p * chunk, chunk)
    both = lambda c, p: ((p * nz + z) * 2 + c, s)
    res[pl.ds(row(core, x), chunk), :] = acc
    copies = []
    for c2 in range(2):
        for p in range(nx):
            skip = jnp.logical_and(c2 == core, p == x)
            cp = _remote(res.at[pl.ds(row(core, x), chunk)], res.at[pl.ds(row(core, x), chunk)],
                         send_sem.at[o_gx + c2 * nx + p], recv_sem.at[o_gx + core * nx + x], both(c2, p))
            pl.when(jnp.logical_not(skip))(cp.start)
            copies.append((skip, cp))
    for c2 in range(2):
        for p in range(nx):
            skip = jnp.logical_and(c2 == core, p == x)
            cp = _remote(res.at[pl.ds(row(c2, p), chunk)], res.at[pl.ds(row(c2, p), chunk)],
                         send_sem.at[o_gx + c2 * nx + p], recv_sem.at[o_gx + c2 * nx + p], both(c2, p))
            pl.when(jnp.logical_not(skip))(cp.wait_recv)
    for skip, cp in copies:
        pl.when(jnp.logical_not(skip))(cp.wait_send)
    o_ref[...] = res[...] if scale == 1.0 else res[...] * scale


def make_allreduce(dims, cid, scale=1.0):
    nx, nz, ny = dims
    total = 2 * nx + nz + ny + 2 * nx

    def allreduce(partial_value):
        rows, cols = partial_value.shape
        half = rows // 2
        chunk = half // nx
        return pl.pallas_call(
            functools.partial(_allreduce_kernel, dims, scale),
            out_shape=jax.ShapeDtypeStruct(partial_value.shape, jnp.float32),
            in_specs=[pl.BlockSpec(memory_space=pltpu.VMEM)],
            out_specs=pl.BlockSpec(memory_space=pltpu.VMEM),
            scratch_shapes=[
                pltpu.VMEM((2 * nx, chunk, cols), jnp.float32),
                pltpu.VMEM((nz, chunk, cols), jnp.float32),
                pltpu.VMEM((ny, chunk, cols), jnp.float32),
                pltpu.VMEM((rows, cols), jnp.float32),
                pltpu.SemaphoreType.DMA((total,)),
                pltpu.SemaphoreType.DMA((total,)),
            ],
            compiler_params=pltpu.CompilerParams(collective_id=cid, has_side_effects=True),
        )(partial_value)

    return allreduce


def _chol_kernel(count, g_ref, *refs):
    if len(refs) == 4:
        prev_ref, lt_ref, w_ref, f_ref = refs
    else:
        prev_ref, f_ref = None, None
        lt_ref, w_ref = refs
    n = g_ref.shape[0]
    g = g_ref[...] / count
    a = (g + g.T) / 2
    sub = lax.broadcasted_iota(jnp.int32, (n, n), 0)
    lane = lax.broadcasted_iota(jnp.int32, (n, n), 1)
    w = jnp.where(sub == lane, 1.0, 0.0).astype(jnp.float32)
    lane_row = lax.broadcasted_iota(jnp.int32, (1, n), 1)
    lt_rows = []
    w_rows = []
    for k in range(n):
        r0 = k // 8 * 8
        row = a[k - r0:k - r0 + 1, :]
        colb = jnp.broadcast_to(a[:, k:k + 1], a.shape)
        recip = lax.rsqrt(colb[k - r0:k - r0 + 1, :])
        lrow = jnp.where(lane_row >= k, row * recip, 0.0)
        wrow = w[k - r0:k - r0 + 1, :] * recip
        lt_rows.append(lrow)
        w_rows.append(wrow)
        if k % 8 == 7:
            lt_ref[r0:r0 + 8, :] = jnp.concatenate(lt_rows, axis=0)
            w_ref[r0:r0 + 8, :] = jnp.concatenate(w_rows, axis=0)
            lt_rows, w_rows = [], []
        if k + 1 < n:
            r1 = (k + 1) // 8 * 8
            if r1 > r0:
                a = a[r1 - r0:]
                w = w[r1 - r0:]
                colb = colb[r1 - r0:]
            idx = lax.broadcasted_iota(jnp.int32, (n - r1, 1), 0) + r1
            m = jnp.where(idx > k, colb * recip, 0.0)
            a = a - m * lrow
            w = w - m * wrow
    if f_ref is not None:
        f_ref[...] = jnp.dot(lt_ref[...], prev_ref[...], precision=lax.Precision.HIGHEST,
                             preferred_element_type=jnp.float32)


def chol_inv(g, count, prev=None):
    n = g.shape[0]
    square = jax.ShapeDtypeStruct((n, n), jnp.float32)
    vmem = pl.BlockSpec(memory_space=pltpu.VMEM)
    outs = 2 if prev is None else 3
    return pl.pallas_call(
        functools.partial(_chol_kernel, float(count)),
        out_shape=(square,) * outs,
        in_specs=[vmem] * (1 if prev is None else 2),
        out_specs=(vmem,) * outs,
    )(g, *(() if prev is None else (prev,)))


def _jac_kernel(nbulk, cols_hbm, modes_ref, jac_ref, out_ref, ext, acc_ref, cols_ref, cols_sem, send_sem, recv_sem):
    cols_copy = pltpu.make_async_copy(cols_hbm, cols_ref, cols_sem)
    cols_copy.start()
    b = lax.axis_index("bulk")
    s = lax.axis_index("span")
    rb = modes_ref.shape[0]
    has_left = b > 0
    has_right = b < nbulk - 1
    barrier = pltpu.get_barrier_semaphore()

    @pl.when(has_left)
    def _():
        pl.semaphore_signal(barrier, inc=1, device_id=(b - 1, s), device_id_type=MESH)

    @pl.when(has_right)
    def _():
        pl.semaphore_signal(barrier, inc=1, device_id=(b + 1, s), device_id_type=MESH)

    pl.semaphore_wait(barrier, has_left.astype(jnp.int32) + has_right.astype(jnp.int32))

    to_left = pltpu.make_async_remote_copy(
        src_ref=modes_ref, dst_ref=ext.at[pl.ds(2 * rb, rb)], send_sem=send_sem.at[0],
        recv_sem=recv_sem.at[1], device_id=(b - 1, s), device_id_type=MESH)
    to_right = pltpu.make_async_remote_copy(
        src_ref=modes_ref, dst_ref=ext.at[pl.ds(0, rb)], send_sem=send_sem.at[1],
        recv_sem=recv_sem.at[0], device_id=(b + 1, s), device_id_type=MESH)

    @pl.when(has_left)
    def _():
        to_left.start()

    @pl.when(has_right)
    def _():
        to_right.start()

    ext[pl.ds(rb, rb)] = modes_ref[...]

    @pl.when(jnp.logical_not(has_left))
    def _():
        ext[pl.ds(0, rb)] = jnp.zeros(modes_ref.shape, modes_ref.dtype)

    @pl.when(jnp.logical_not(has_right))
    def _():
        ext[pl.ds(2 * rb, rb)] = jnp.zeros(modes_ref.shape, modes_ref.dtype)

    def own(r, carry):
        acc_ref[r] = jnp.dot(jac_ref[r, 0], modes_ref[r], preferred_element_type=jnp.float32)
        return carry

    lax.fori_loop(0, rb, own, 0)

    @pl.when(has_left)
    def _():
        to_right.wait_recv()
        to_left.wait_send()

    @pl.when(has_right)
    def _():
        to_left.wait_recv()
        to_right.wait_send()

    cols_copy.wait()
    start = (s * nbulk + b) * rb - rb

    def row(r, carry):
        acc = acc_ref[r]
        for n in range(1, jac_ref.shape[1]):
            idx = jnp.clip(cols_ref[n, r] - start, 0, 3 * rb - 1)
            term = jnp.dot(jac_ref[r, n], ext[idx], preferred_element_type=jnp.float32)
            acc = acc + term
        out_ref[r] = acc.astype(out_ref.dtype)
        return carry

    lax.fori_loop(0, rb, row, 0)


def jac_apply(nbulk, cid, jac_cols, modes_b, jac_blocks):
    rb, nb, blk, width = jac_blocks.shape[0], jac_blocks.shape[1], jac_blocks.shape[2], modes_b.shape[1]
    modes_blocks = modes_b.reshape(rb, blk, width)
    out = pl.pallas_call(
        functools.partial(_jac_kernel, nbulk),
        out_shape=jax.ShapeDtypeStruct((rb, blk, width), jnp.bfloat16),
        in_specs=[pl.BlockSpec(memory_space=pl.ANY),
                  pl.BlockSpec(memory_space=pltpu.VMEM),
                  pl.BlockSpec(memory_space=pltpu.VMEM)],
        out_specs=pl.BlockSpec(memory_space=pltpu.VMEM),
        scratch_shapes=[
            pltpu.VMEM((3 * rb, blk, width), jnp.bfloat16),
            pltpu.VMEM((rb, blk, width), jnp.float32),
            pltpu.SMEM(jac_cols.shape[::-1], jnp.int32),
            pltpu.SemaphoreType.DMA(()),
            pltpu.SemaphoreType.DMA((2,)),
            pltpu.SemaphoreType.DMA((2,)),
        ],
        compiler_params=pltpu.CompilerParams(collective_id=cid, has_side_effects=True),
    )(jac_cols.T, modes_blocks, jac_blocks)
    return out.reshape(rb * blk, width)


def cholesky_step(data, row_count, allreduce, prev=None, precision=lax.Precision.HIGHEST):
    high = lax.Precision.HIGHEST
    gram_precision = high if prev is None else precision
    partial_value = lax.dot_general(
        data, data, (((0,), (0,)), ((), ())), precision=gram_precision,
        preferred_element_type=jnp.float32,
    )
    outs = chol_inv(allreduce(partial_value), row_count, prev)
    result = lax.dot_general(
        data, outs[1], (((1,), (1,)), ((), ())), precision=precision,
        preferred_element_type=jnp.float32,
    )
    return (result, outs[0] if prev is None else outs[2])


def shards(dims, snapshots, jac_blocks, jac_cols):
    high = lax.Precision.HIGHEST
    local_rows, width = snapshots.shape
    block_rows = jac_cols.shape[0]
    blk = jac_blocks.shape[2]
    row_count = local_rows * lax.axis_size(("bulk", "span"))
    first, upper1 = cholesky_step(snapshots, row_count, make_allreduce(dims, 0))
    modes, factor = cholesky_step(first, row_count, make_allreduce(dims, 1), upper1, lax.Precision.HIGH)
    modes_b = modes.astype(jnp.bfloat16)
    jac_modes = jac_apply(lax.axis_size("bulk"), 3, jac_cols, modes_b, jac_blocks)
    partial_value = lax.dot_general(
        modes,
        jac_modes.astype(jnp.float32),
        (((0,), (0,)), ((), ())),
        precision=lax.Precision.HIGH,
        preferred_element_type=jnp.float32,
    )
    reduced = make_allreduce(dims, 2, 1.0 / row_count)(partial_value)
    return (modes, factor, jac_modes, reduced)


def _torus_dims(mesh):
    coords = [d.coords for d in mesh.devices.flat]
    return tuple(len({c[i] for c in coords}) for i in (0, 2, 1))


def solution(mesh):
    nx, nz, ny = _torus_dims(mesh)
    assert mesh.shape["bulk"] == 2 * nx * nz and mesh.shape["span"] == ny
    return jax.shard_map(
        functools.partial(shards, (nx, nz, ny)),
        mesh=mesh,
        in_specs=(
            P(("span", "bulk"), None),
            P(("span", "bulk"), None, None, None),
            P(("span", "bulk"), None),
        ),
        out_specs=(P(("span", "bulk"), None), P(), P(("span", "bulk"), None), P()),
        check_vma=False,
    )
```

```python
import functools

import jax
import jax.numpy as jnp
from jax import lax
from jax.experimental import pallas as pl
from jax.experimental.pallas import tpu as pltpu
from jax.sharding import PartitionSpec as P

MESH = pl.DeviceIdType.MESH


def _coords(nx, nz):
    b = lax.axis_index("bulk")
    s = lax.axis_index("span")
    core = b % 2
    z = (b // 2) % nz
    x = b // (2 * nz)
    return b, s, core, x, z


def _remote(src, dst, send_sem, recv_sem, device):
    return pltpu.make_async_remote_copy(
        src_ref=src, dst_ref=dst, send_sem=send_sem, recv_sem=recv_sem,
        device_id=device, device_id_type=MESH,
    )


def _allreduce_kernel(dims, scale, x_ref, o_ref, s_x, s_z, s_y, res, send_sem, recv_sem):
    nx, nz, ny = dims
    b, s, core, x, z = _coords(nx, nz)
    rows = x_ref.shape[0]
    half = rows // 2
    chunk = half // nx
    partner = (b + 1 - 2 * core, s)
    x_dev = lambda p: ((p * nz + z) * 2 + core, s)
    z_dev = lambda p: ((x * nz + p) * 2 + core, s)
    y_dev = lambda p: (b, p)
    o_x, o_z, o_y = 0, 2 * nx, 2 * nx + nz
    o_gx = o_y + ny

    barrier = pltpu.get_barrier_semaphore()
    peers = [partner]
    for n, pos, dev in ((nx, x, x_dev), (nz, z, z_dev), (ny, s, y_dev)):
        peers += [dev((pos + d) % n) for d in range(1, n)]
    peers += [((((x + d) % nx) * nz + z) * 2 + 1 - core, s) for d in range(1, nx)]
    for peer in peers:
        pl.semaphore_signal(barrier, inc=1, device_id=peer, device_id_type=MESH)
    pl.semaphore_wait(barrier, len(peers))

    row = lambda c, p: pl.multiple_of(c * half + p * chunk, chunk)
    both = lambda c, p: ((p * nz + z) * 2 + c, s)
    me = core * nx + x
    copies = []
    for c2 in range(2):
        for p in range(nx):
            skip = jnp.logical_and(c2 == core, p == x)
            cp = _remote(x_ref.at[pl.ds(row(c2, p), chunk)], s_x.at[me],
                         send_sem.at[o_x + c2 * nx + p], recv_sem.at[o_x + me], both(c2, p))
            pl.when(jnp.logical_not(skip))(cp.start)
            copies.append((skip, cp))
    s_x[me] = x_ref[pl.ds(row(core, x), chunk), :]
    for c2 in range(2):
        for p in range(nx):
            skip = jnp.logical_and(c2 == core, p == x)
            j = c2 * nx + p
            cp = _remote(s_x.at[j], s_x.at[j], send_sem.at[o_x + j], recv_sem.at[o_x + j], both(c2, p))
            pl.when(jnp.logical_not(skip))(cp.wait_recv)
    pending = list(copies)
    acc = s_x[0]
    for k in range(1, 2 * nx):
        acc = acc + s_x[k]

    for n, pos, dev, slots, off in ((nz, z, z_dev, s_z, o_z), (ny, s, y_dev, s_y, o_y)):
        slots[pos] = acc
        copies = []
        for d in range(1, n):
            p = (pos + d) % n
            cp = _remote(slots.at[pos], slots.at[pos], send_sem.at[off + p], recv_sem.at[off + pos], dev(p))
            cp.start()
            copies.append(cp)
        for d in range(1, n):
            j = (pos + d) % n
            _remote(slots.at[j], slots.at[j], send_sem.at[off + j], recv_sem.at[off + j], dev(j)).wait_recv()
        pending += [(False, cp) for cp in copies]
        acc = slots[0]
        for k in range(1, n):
            acc = acc + slots[k]

    row = lambda c, p: pl.multiple_of(c * half + p * chunk, chunk)
    both = lambda c, p: ((p * nz + z) * 2 + c, s)
    res[pl.ds(row(core, x), chunk), :] = acc
    copies = []
    for c2 in range(2):
        for p in range(nx):
            skip = jnp.logical_and(c2 == core, p == x)
            cp = _remote(res.at[pl.ds(row(core, x), chunk)], res.at[pl.ds(row(core, x), chunk)],
                         send_sem.at[o_gx + c2 * nx + p], recv_sem.at[o_gx + core * nx + x], both(c2, p))
            pl.when(jnp.logical_not(skip))(cp.start)
            copies.append((skip, cp))
    for c2 in range(2):
        for p in range(nx):
            skip = jnp.logical_and(c2 == core, p == x)
            cp = _remote(res.at[pl.ds(row(c2, p), chunk)], res.at[pl.ds(row(c2, p), chunk)],
                         send_sem.at[o_gx + c2 * nx + p], recv_sem.at[o_gx + c2 * nx + p], both(c2, p))
            pl.when(jnp.logical_not(skip))(cp.wait_recv)
    for skip, cp in pending + copies:
        pl.when(jnp.logical_not(skip))(cp.wait_send)
    o_ref[...] = res[...] if scale == 1.0 else res[...] * scale


def make_allreduce(dims, cid, scale=1.0):
    nx, nz, ny = dims
    total = 2 * nx + nz + ny + 2 * nx

    def allreduce(partial_value):
        rows, cols = partial_value.shape
        half = rows // 2
        chunk = half // nx
        return pl.pallas_call(
            functools.partial(_allreduce_kernel, dims, scale),
            out_shape=jax.ShapeDtypeStruct(partial_value.shape, jnp.float32),
            in_specs=[pl.BlockSpec(memory_space=pltpu.VMEM)],
            out_specs=pl.BlockSpec(memory_space=pltpu.VMEM),
            scratch_shapes=[
                pltpu.VMEM((2 * nx, chunk, cols), jnp.float32),
                pltpu.VMEM((nz, chunk, cols), jnp.float32),
                pltpu.VMEM((ny, chunk, cols), jnp.float32),
                pltpu.VMEM((rows, cols), jnp.float32),
                pltpu.SemaphoreType.DMA((total,)),
                pltpu.SemaphoreType.DMA((total,)),
            ],
            compiler_params=pltpu.CompilerParams(collective_id=cid, has_side_effects=True),
        )(partial_value)

    return allreduce


def _chol_kernel(count, g_ref, *refs):
    if len(refs) == 4:
        prev_ref, lt_ref, w_ref, f_ref = refs
    else:
        prev_ref, f_ref = None, None
        lt_ref, w_ref = refs
    n = g_ref.shape[0]
    g = g_ref[...] / count
    a = (g + g.T) / 2
    sub = lax.broadcasted_iota(jnp.int32, (n, n), 0)
    lane = lax.broadcasted_iota(jnp.int32, (n, n), 1)
    w = jnp.where(sub == lane, 1.0, 0.0).astype(jnp.float32)
    lane_row = lax.broadcasted_iota(jnp.int32, (1, n), 1)
    lt_rows = []
    w_rows = []
    for k in range(n):
        r0 = k // 8 * 8
        row = a[k - r0:k - r0 + 1, :]
        colb = jnp.broadcast_to(a[:, k:k + 1], a.shape)
        recip = lax.rsqrt(colb[k - r0:k - r0 + 1, :])
        lrow = jnp.where(lane_row >= k, row * recip, 0.0)
        wrow = w[k - r0:k - r0 + 1, :] * recip
        lt_rows.append(lrow)
        w_rows.append(wrow)
        if k % 8 == 7:
            lt_ref[r0:r0 + 8, :] = jnp.concatenate(lt_rows, axis=0)
            w_ref[r0:r0 + 8, :] = jnp.concatenate(w_rows, axis=0)
            lt_rows, w_rows = [], []
        if k + 1 < n:
            r1 = (k + 1) // 8 * 8
            if r1 > r0:
                a = a[r1 - r0:]
                w = w[r1 - r0:]
                colb = colb[r1 - r0:]
            idx = lax.broadcasted_iota(jnp.int32, (n - r1, 1), 0) + r1
            m = jnp.where(idx > k, colb * recip, 0.0)
            a = a - m * lrow
            w = w - m * wrow
    if f_ref is not None:
        f_ref[...] = jnp.dot(lt_ref[...], prev_ref[...], precision=lax.Precision.HIGHEST,
                             preferred_element_type=jnp.float32)


def chol_inv(g, count, prev=None):
    n = g.shape[0]
    square = jax.ShapeDtypeStruct((n, n), jnp.float32)
    vmem = pl.BlockSpec(memory_space=pltpu.VMEM)
    outs = 2 if prev is None else 3
    return pl.pallas_call(
        functools.partial(_chol_kernel, float(count)),
        out_shape=(square,) * outs,
        in_specs=[vmem] * (1 if prev is None else 2),
        out_specs=(vmem,) * outs,
    )(g, *(() if prev is None else (prev,)))


def _jac_kernel(nbulk, cols_hbm, modes_ref, jac_ref, out_ref, ext, cols_ref, cols_sem, send_sem, recv_sem):
    cols_copy = pltpu.make_async_copy(cols_hbm, cols_ref, cols_sem)
    cols_copy.start()
    b = lax.axis_index("bulk")
    s = lax.axis_index("span")
    rb = modes_ref.shape[0]
    has_left = b > 0
    has_right = b < nbulk - 1
    barrier = pltpu.get_barrier_semaphore()

    @pl.when(has_left)
    def _():
        pl.semaphore_signal(barrier, inc=1, device_id=(b - 1, s), device_id_type=MESH)

    @pl.when(has_right)
    def _():
        pl.semaphore_signal(barrier, inc=1, device_id=(b + 1, s), device_id_type=MESH)

    pl.semaphore_wait(barrier, has_left.astype(jnp.int32) + has_right.astype(jnp.int32))

    to_left = pltpu.make_async_remote_copy(
        src_ref=modes_ref, dst_ref=ext.at[pl.ds(2 * rb, rb)], send_sem=send_sem.at[0],
        recv_sem=recv_sem.at[1], device_id=(b - 1, s), device_id_type=MESH)
    to_right = pltpu.make_async_remote_copy(
        src_ref=modes_ref, dst_ref=ext.at[pl.ds(0, rb)], send_sem=send_sem.at[1],
        recv_sem=recv_sem.at[0], device_id=(b + 1, s), device_id_type=MESH)

    @pl.when(has_left)
    def _():
        to_left.start()

    @pl.when(has_right)
    def _():
        to_right.start()

    ext[pl.ds(rb, rb)] = modes_ref[...]

    @pl.when(jnp.logical_not(has_left))
    def _():
        ext[pl.ds(0, rb)] = jnp.zeros(modes_ref.shape, modes_ref.dtype)

    @pl.when(jnp.logical_not(has_right))
    def _():
        ext[pl.ds(2 * rb, rb)] = jnp.zeros(modes_ref.shape, modes_ref.dtype)

    @pl.when(has_left)
    def _():
        to_right.wait_recv()
        to_left.wait_send()

    @pl.when(has_right)
    def _():
        to_left.wait_recv()
        to_right.wait_send()

    cols_copy.wait()
    start = (s * nbulk + b) * rb - rb

    def row(r, carry):
        acc = None
        for n in range(jac_ref.shape[1]):
            idx = jnp.clip(cols_ref[n, r] - start, 0, 3 * rb - 1)
            term = jnp.dot(jac_ref[r, n], ext[idx], preferred_element_type=jnp.float32)
            acc = term if acc is None else acc + term
        out_ref[r] = acc.astype(out_ref.dtype)
        return carry

    lax.fori_loop(0, rb, row, 0)


def jac_apply(nbulk, cid, jac_cols, modes_b, jac_blocks):
    rb, nb, blk, width = jac_blocks.shape[0], jac_blocks.shape[1], jac_blocks.shape[2], modes_b.shape[1]
    modes_blocks = modes_b.reshape(rb, blk, width)
    out = pl.pallas_call(
        functools.partial(_jac_kernel, nbulk),
        out_shape=jax.ShapeDtypeStruct((rb, blk, width), jnp.bfloat16),
        in_specs=[pl.BlockSpec(memory_space=pl.ANY),
                  pl.BlockSpec(memory_space=pltpu.VMEM),
                  pl.BlockSpec(memory_space=pltpu.VMEM)],
        out_specs=pl.BlockSpec(memory_space=pltpu.VMEM),
        scratch_shapes=[
            pltpu.VMEM((3 * rb, blk, width), jnp.bfloat16),
            pltpu.SMEM(jac_cols.shape[::-1], jnp.int32),
            pltpu.SemaphoreType.DMA(()),
            pltpu.SemaphoreType.DMA((2,)),
            pltpu.SemaphoreType.DMA((2,)),
        ],
        compiler_params=pltpu.CompilerParams(collective_id=cid, has_side_effects=True),
    )(jac_cols.T, modes_blocks, jac_blocks)
    return out.reshape(rb * blk, width)


def cholesky_step(data, row_count, allreduce, prev=None, precision=lax.Precision.HIGHEST):
    high = lax.Precision.HIGHEST
    gram_precision = high if prev is None else precision
    partial_value = lax.dot_general(
        data, data, (((0,), (0,)), ((), ())), precision=gram_precision,
        preferred_element_type=jnp.float32,
    )
    outs = chol_inv(allreduce(partial_value), row_count, prev)
    result = lax.dot_general(
        data, outs[1], (((1,), (1,)), ((), ())), precision=precision,
        preferred_element_type=jnp.float32,
    )
    return (result, outs[0] if prev is None else outs[2])


def shards(dims, snapshots, jac_blocks, jac_cols):
    high = lax.Precision.HIGHEST
    local_rows, width = snapshots.shape
    block_rows = jac_cols.shape[0]
    blk = jac_blocks.shape[2]
    row_count = local_rows * lax.axis_size(("bulk", "span"))
    first, upper1 = cholesky_step(snapshots, row_count, make_allreduce(dims, 0))
    modes, factor = cholesky_step(first, row_count, make_allreduce(dims, 1), upper1, lax.Precision.HIGH)
    modes_b = modes.astype(jnp.bfloat16)
    jac_modes = jac_apply(lax.axis_size("bulk"), 3, jac_cols, modes_b, jac_blocks)
    partial_value = lax.dot_general(
        modes,
        jac_modes.astype(jnp.float32),
        (((0,), (0,)), ((), ())),
        precision=lax.Precision.HIGH,
        preferred_element_type=jnp.float32,
    )
    reduced = make_allreduce(dims, 2, 1.0 / row_count)(partial_value)
    return (modes, factor, jac_modes, reduced)


def _torus_dims(mesh):
    coords = [d.coords for d in mesh.devices.flat]
    return tuple(len({c[i] for c in coords}) for i in (0, 2, 1))


def solution(mesh):
    nx, nz, ny = _torus_dims(mesh)
    assert mesh.shape["bulk"] == 2 * nx * nz and mesh.shape["span"] == ny
    return jax.shard_map(
        functools.partial(shards, (nx, nz, ny)),
        mesh=mesh,
        in_specs=(
            P(("span", "bulk"), None),
            P(("span", "bulk"), None, None, None),
            P(("span", "bulk"), None),
        ),
        out_specs=(P(("span", "bulk"), None), P(), P(("span", "bulk"), None), P()),
        check_vma=False,
    )
```

```python
import functools

import jax
import jax.numpy as jnp
from jax import lax
from jax.experimental import pallas as pl
from jax.experimental.pallas import tpu as pltpu
from jax.sharding import PartitionSpec as P

MESH = pl.DeviceIdType.MESH


def _coords(nx, nz):
    b = lax.axis_index("bulk")
    s = lax.axis_index("span")
    core = b % 2
    z = (b // 2) % nz
    x = b // (2 * nz)
    return b, s, core, x, z


def _remote(src, dst, send_sem, recv_sem, device):
    return pltpu.make_async_remote_copy(
        src_ref=src, dst_ref=dst, send_sem=send_sem, recv_sem=recv_sem,
        device_id=device, device_id_type=MESH,
    )


def _allreduce_kernel(dims, scale, x_ref, o_ref, s_x, s_z, s_y, res, send_sem, recv_sem):
    nx, nz, ny = dims
    b, s, core, x, z = _coords(nx, nz)
    rows = x_ref.shape[0]
    half = rows // 2
    chunk = half // nx
    partner = (b + 1 - 2 * core, s)
    x_dev = lambda p: ((p * nz + z) * 2 + core, s)
    z_dev = lambda p: ((x * nz + p) * 2 + core, s)
    y_dev = lambda p: (b, p)
    o_x, o_z, o_y = 0, 2 * nx, 2 * nx + nz
    o_gx = o_y + ny

    barrier = pltpu.get_barrier_semaphore()
    peers = [partner]
    for n, pos, dev in ((nx, x, x_dev), (nz, z, z_dev), (ny, s, y_dev)):
        peers += [dev((pos + d) % n) for d in range(1, n)]
    peers += [((((x + d) % nx) * nz + z) * 2 + 1 - core, s) for d in range(1, nx)]
    for peer in peers:
        pl.semaphore_signal(barrier, inc=1, device_id=peer, device_id_type=MESH)
    pl.semaphore_wait(barrier, len(peers))

    row = lambda c, p: pl.multiple_of(c * half + p * chunk, chunk)
    both = lambda c, p: ((p * nz + z) * 2 + c, s)
    me = core * nx + x
    copies = []
    for c2 in range(2):
        for p in range(nx):
            skip = jnp.logical_and(c2 == core, p == x)
            cp = _remote(x_ref.at[pl.ds(row(c2, p), chunk)], s_x.at[me],
                         send_sem.at[o_x + c2 * nx + p], recv_sem.at[o_x + me], both(c2, p))
            pl.when(jnp.logical_not(skip))(cp.start)
            copies.append((skip, cp))
    s_x[me] = x_ref[pl.ds(row(core, x), chunk), :]
    for c2 in range(2):
        for p in range(nx):
            skip = jnp.logical_and(c2 == core, p == x)
            j = c2 * nx + p
            cp = _remote(s_x.at[j], s_x.at[j], send_sem.at[o_x + j], recv_sem.at[o_x + j], both(c2, p))
            pl.when(jnp.logical_not(skip))(cp.wait_recv)
    pending = list(copies)
    acc = s_x[0]
    for k in range(1, 2 * nx):
        acc = acc + s_x[k]

    for n, pos, dev, slots, off in ((nz, z, z_dev, s_z, o_z), (ny, s, y_dev, s_y, o_y)):
        slots[pos] = acc
        copies = []
        for d in range(1, n):
            p = (pos + d) % n
            cp = _remote(slots.at[pos], slots.at[pos], send_sem.at[off + p], recv_sem.at[off + pos], dev(p))
            cp.start()
            copies.append(cp)
        for d in range(1, n):
            j = (pos + d) % n
            _remote(slots.at[j], slots.at[j], send_sem.at[off + j], recv_sem.at[off + j], dev(j)).wait_recv()
        pending += [(False, cp) for cp in copies]
        acc = slots[0]
        for k in range(1, n):
            acc = acc + slots[k]

    row = lambda c, p: pl.multiple_of(c * half + p * chunk, chunk)
    both = lambda c, p: ((p * nz + z) * 2 + c, s)
    res[pl.ds(row(core, x), chunk), :] = acc
    copies = []
    for c2 in range(2):
        for p in range(nx):
            skip = jnp.logical_and(c2 == core, p == x)
            cp = _remote(res.at[pl.ds(row(core, x), chunk)], res.at[pl.ds(row(core, x), chunk)],
                         send_sem.at[o_gx + c2 * nx + p], recv_sem.at[o_gx + core * nx + x], both(c2, p))
            pl.when(jnp.logical_not(skip))(cp.start)
            copies.append((skip, cp))
    for c2 in range(2):
        for p in range(nx):
            skip = jnp.logical_and(c2 == core, p == x)
            cp = _remote(res.at[pl.ds(row(c2, p), chunk)], res.at[pl.ds(row(c2, p), chunk)],
                         send_sem.at[o_gx + c2 * nx + p], recv_sem.at[o_gx + c2 * nx + p], both(c2, p))
            pl.when(jnp.logical_not(skip))(cp.wait_recv)
    for skip, cp in pending + copies:
        pl.when(jnp.logical_not(skip))(cp.wait_send)
    o_ref[...] = res[...] if scale == 1.0 else res[...] * scale


def make_allreduce(dims, cid, scale=1.0):
    nx, nz, ny = dims
    total = 2 * nx + nz + ny + 2 * nx

    def allreduce(partial_value):
        rows, cols = partial_value.shape
        half = rows // 2
        chunk = half // nx
        return pl.pallas_call(
            functools.partial(_allreduce_kernel, dims, scale),
            out_shape=jax.ShapeDtypeStruct(partial_value.shape, jnp.float32),
            in_specs=[pl.BlockSpec(memory_space=pltpu.VMEM)],
            out_specs=pl.BlockSpec(memory_space=pltpu.VMEM),
            scratch_shapes=[
                pltpu.VMEM((2 * nx, chunk, cols), jnp.float32),
                pltpu.VMEM((nz, chunk, cols), jnp.float32),
                pltpu.VMEM((ny, chunk, cols), jnp.float32),
                pltpu.VMEM((rows, cols), jnp.float32),
                pltpu.SemaphoreType.DMA((total,)),
                pltpu.SemaphoreType.DMA((total,)),
            ],
            compiler_params=pltpu.CompilerParams(collective_id=cid, has_side_effects=True),
        )(partial_value)

    return allreduce


def _chol_kernel(count, g_ref, *refs):
    if len(refs) == 4:
        prev_ref, lt_ref, w_ref, f_ref = refs
    else:
        prev_ref, f_ref = None, None
        lt_ref, w_ref = refs
    n = g_ref.shape[0]
    g = g_ref[...] / count
    a = (g + g.T) / 2
    sub = lax.broadcasted_iota(jnp.int32, (n, n), 0)
    lane = lax.broadcasted_iota(jnp.int32, (n, n), 1)
    w = jnp.where(sub == lane, 1.0, 0.0).astype(jnp.float32)
    lane_row = lax.broadcasted_iota(jnp.int32, (1, n), 1)
    lt_rows = []
    w_rows = []
    for k in range(n):
        r0 = k // 8 * 8
        row = a[k - r0:k - r0 + 1, :]
        colb = jnp.broadcast_to(a[:, k:k + 1], a.shape)
        recip = lax.rsqrt(colb[k - r0:k - r0 + 1, :])
        lrow = jnp.where(lane_row >= k, row * recip, 0.0)
        wrow = w[k - r0:k - r0 + 1, :] * recip
        lt_rows.append(lrow)
        w_rows.append(wrow)
        if k % 8 == 7:
            lt_ref[r0:r0 + 8, :] = jnp.concatenate(lt_rows, axis=0)
            w_ref[r0:r0 + 8, :] = jnp.concatenate(w_rows, axis=0)
            lt_rows, w_rows = [], []
        if k + 1 < n:
            r1 = (k + 1) // 8 * 8
            if r1 > r0:
                a = a[r1 - r0:]
                w = w[r1 - r0:]
                colb = colb[r1 - r0:]
            idx = lax.broadcasted_iota(jnp.int32, (n - r1, 1), 0) + r1
            m = jnp.where(idx > k, colb * recip, 0.0)
            a = a - m * lrow
            w = w - m * wrow
    if f_ref is not None:
        f_ref[...] = jnp.dot(lt_ref[...], prev_ref[...], precision=lax.Precision.HIGHEST,
                             preferred_element_type=jnp.float32)


def chol_inv(g, count, prev=None):
    n = g.shape[0]
    square = jax.ShapeDtypeStruct((n, n), jnp.float32)
    vmem = pl.BlockSpec(memory_space=pltpu.VMEM)
    outs = 2 if prev is None else 3
    return pl.pallas_call(
        functools.partial(_chol_kernel, float(count)),
        out_shape=(square,) * outs,
        in_specs=[vmem] * (1 if prev is None else 2),
        out_specs=(vmem,) * outs,
    )(g, *(() if prev is None else (prev,)))


def _jac_kernel(nbulk, cols_hbm, modes_ref, jac_ref, out_ref, ext, acc_ref, cols_ref, cols_sem, send_sem, recv_sem):
    cols_copy = pltpu.make_async_copy(cols_hbm, cols_ref, cols_sem)
    cols_copy.start()
    b = lax.axis_index("bulk")
    s = lax.axis_index("span")
    rb = modes_ref.shape[0]
    has_left = b > 0
    has_right = b < nbulk - 1
    barrier = pltpu.get_barrier_semaphore()

    @pl.when(has_left)
    def _():
        pl.semaphore_signal(barrier, inc=1, device_id=(b - 1, s), device_id_type=MESH)

    @pl.when(has_right)
    def _():
        pl.semaphore_signal(barrier, inc=1, device_id=(b + 1, s), device_id_type=MESH)

    pl.semaphore_wait(barrier, has_left.astype(jnp.int32) + has_right.astype(jnp.int32))

    to_left = pltpu.make_async_remote_copy(
        src_ref=modes_ref, dst_ref=ext.at[pl.ds(2 * rb, rb)], send_sem=send_sem.at[0],
        recv_sem=recv_sem.at[1], device_id=(b - 1, s), device_id_type=MESH)
    to_right = pltpu.make_async_remote_copy(
        src_ref=modes_ref, dst_ref=ext.at[pl.ds(0, rb)], send_sem=send_sem.at[1],
        recv_sem=recv_sem.at[0], device_id=(b + 1, s), device_id_type=MESH)

    @pl.when(has_left)
    def _():
        to_left.start()

    @pl.when(has_right)
    def _():
        to_right.start()

    ext[pl.ds(rb, rb)] = modes_ref[...]

    @pl.when(jnp.logical_not(has_left))
    def _():
        ext[pl.ds(0, rb)] = jnp.zeros(modes_ref.shape, modes_ref.dtype)

    @pl.when(jnp.logical_not(has_right))
    def _():
        ext[pl.ds(2 * rb, rb)] = jnp.zeros(modes_ref.shape, modes_ref.dtype)

    def own(r, carry):
        acc_ref[r] = jnp.dot(jac_ref[r, 0], modes_ref[r], preferred_element_type=jnp.float32)
        return carry

    lax.fori_loop(0, rb, own, 0)

    @pl.when(has_left)
    def _():
        to_right.wait_recv()
        to_left.wait_send()

    @pl.when(has_right)
    def _():
        to_left.wait_recv()
        to_right.wait_send()

    cols_copy.wait()
    start = (s * nbulk + b) * rb - rb

    def row(r, carry):
        acc = acc_ref[r]
        for n in range(1, jac_ref.shape[1]):
            idx = jnp.clip(cols_ref[n, r] - start, 0, 3 * rb - 1)
            term = jnp.dot(jac_ref[r, n], ext[idx], preferred_element_type=jnp.float32)
            acc = acc + term
        out_ref[r] = acc.astype(out_ref.dtype)
        return carry

    lax.fori_loop(0, rb, row, 0)


def jac_apply(nbulk, cid, jac_cols, modes_b, jac_blocks):
    rb, nb, blk, width = jac_blocks.shape[0], jac_blocks.shape[1], jac_blocks.shape[2], modes_b.shape[1]
    modes_blocks = modes_b.reshape(rb, blk, width)
    out = pl.pallas_call(
        functools.partial(_jac_kernel, nbulk),
        out_shape=jax.ShapeDtypeStruct((rb, blk, width), jnp.bfloat16),
        in_specs=[pl.BlockSpec(memory_space=pl.ANY),
                  pl.BlockSpec(memory_space=pltpu.VMEM),
                  pl.BlockSpec(memory_space=pltpu.VMEM)],
        out_specs=pl.BlockSpec(memory_space=pltpu.VMEM),
        scratch_shapes=[
            pltpu.VMEM((3 * rb, blk, width), jnp.bfloat16),
            pltpu.VMEM((rb, blk, width), jnp.float32),
            pltpu.SMEM(jac_cols.shape[::-1], jnp.int32),
            pltpu.SemaphoreType.DMA(()),
            pltpu.SemaphoreType.DMA((2,)),
            pltpu.SemaphoreType.DMA((2,)),
        ],
        compiler_params=pltpu.CompilerParams(collective_id=cid, has_side_effects=True),
    )(jac_cols.T, modes_blocks, jac_blocks)
    return out.reshape(rb * blk, width)


def cholesky_step(data, row_count, allreduce, prev=None, precision=lax.Precision.HIGHEST):
    high = lax.Precision.HIGHEST
    gram_precision = high if prev is None else precision
    partial_value = lax.dot_general(
        data, data, (((0,), (0,)), ((), ())), precision=gram_precision,
        preferred_element_type=jnp.float32,
    )
    outs = chol_inv(allreduce(partial_value), row_count, prev)
    result = lax.dot_general(
        data, outs[1], (((1,), (1,)), ((), ())), precision=precision,
        preferred_element_type=jnp.float32,
    )
    return (result, outs[0] if prev is None else outs[2])


def shards(dims, snapshots, jac_blocks, jac_cols):
    high = lax.Precision.HIGHEST
    local_rows, width = snapshots.shape
    block_rows = jac_cols.shape[0]
    blk = jac_blocks.shape[2]
    row_count = local_rows * lax.axis_size(("bulk", "span"))
    first, upper1 = cholesky_step(snapshots, row_count, make_allreduce(dims, 0))
    modes, factor = cholesky_step(first, row_count, make_allreduce(dims, 1), upper1, lax.Precision.HIGH)
    modes_b = modes.astype(jnp.bfloat16)
    jac_modes = jac_apply(lax.axis_size("bulk"), 3, jac_cols, modes_b, jac_blocks)
    partial_value = lax.dot_general(
        modes,
        jac_modes.astype(jnp.float32),
        (((0,), (0,)), ((), ())),
        precision=lax.Precision.HIGH,
        preferred_element_type=jnp.float32,
    )
    reduced = make_allreduce(dims, 2, 1.0 / row_count)(partial_value)
    return (modes, factor, jac_modes, reduced)


def _torus_dims(mesh):
    coords = [d.coords for d in mesh.devices.flat]
    return tuple(len({c[i] for c in coords}) for i in (0, 2, 1))


def solution(mesh):
    nx, nz, ny = _torus_dims(mesh)
    assert mesh.shape["bulk"] == 2 * nx * nz and mesh.shape["span"] == ny
    return jax.shard_map(
        functools.partial(shards, (nx, nz, ny)),
        mesh=mesh,
        in_specs=(
            P(("span", "bulk"), None),
            P(("span", "bulk"), None, None, None),
            P(("span", "bulk"), None),
        ),
        out_specs=(P(("span", "bulk"), None), P(), P(("span", "bulk"), None), P()),
        check_vma=False,
    )
```
